32 devices in a mesh: stack: 2 (over y), acq: 4 (over x, core), rng: 4 (over z).
Axes of the slice: x: 2, y: 2, z: 4, core: 2. Of those that a mesh axis runs over, the one named last changes fastest.
Arguments:
- images: bfloat16 [2, 16, 128, 1024], P(None, ('stack', 'acq'), None, 'rng'), parts along dimension 1, may hold values from -16 to 16
- pairing: int32 [3, 8], replicated, may hold values from 0 to 7, as said below
- tile_offsets: int32 [3, 2], replicated, may hold values from 0 to 31, as said below
Outputs:
- coherence: float32 [3, 16, 64, 1024], P(None, ('stack', 'acq'), None, 'rng'), parts along dimension 1
- filtered: bfloat16 [2, 3, 16, 64, 1024], P(None, None, ('stack', 'acq'), None, 'rng'), parts along dimension 2
The draws below stay inside these ranges and needn't reach their ends.
There are 2 independent parts, one for each index of `stack`. The reference program is written for one: setup_inputs(seed, part) draws one part's arguments, and reference() takes and returns one part's arrays. A program takes and returns all parts, laid end to end along the dimension named above; an argument that names none is the same for every part. Nothing has to cross between parts.
Inputs may be any that keep to these rules, and one draw needn't show every extreme that they name: In matching m, the partner of acquisition a lies in group (a // 2) XOR (m + 1), and the pairing is an involution. `tile_offsets`: both ends occur in every draw.
All inputs are finite; a program needn't handle non-finite values.
Results may differ from the reference program's by a relative error of at most 0.001.
Values may be sent and summed in bfloat16 or wider, within the bound.
No kernel may reach another device: no remote copies, remote signals or barrier semaphores. Data moves between devices by JAX's collectives and lax.ppermute only.
A program may use at most 64 MiB of HBM per device.

```python
import jax
import jax.numpy as jnp
from jax import lax

LINES = 128
MATCH = 3
REACH = 32
PATCH = 32
HALF = 64
RANGE = 1024
ACQS = 8


def draw_images(key, part):
    folded = jax.random.fold_in(key, 11)
    subkeys = jax.random.split(folded, 7)
    scene_real = jax.random.normal(subkeys[0], (LINES, RANGE), jnp.float32)
    scene_imag = jax.random.normal(subkeys[1], (LINES, RANGE), jnp.float32)
    noise = jax.random.normal(subkeys[2], (2, ACQS, LINES, RANGE), jnp.float32)
    keeping = jax.random.uniform(subkeys[3], (ACQS, 1, 1), jnp.float32, 0.4, 0.9)
    line_rate = jax.random.uniform(subkeys[4], (ACQS, 1, 1), jnp.float32, -0.04, 0.04)
    cell_rate = jax.random.uniform(subkeys[5], (ACQS, 1, 1), jnp.float32, -0.04, 0.04)
    starting = jax.random.uniform(subkeys[6], (ACQS, 1, 1), jnp.float32, -jnp.pi, jnp.pi)
    line_index = jnp.arange(LINES, dtype=jnp.float32)[None, :, None]
    cell_index = jnp.arange(RANGE, dtype=jnp.float32)[None, None, :]
    phases = line_rate * line_index + cell_rate * cell_index + starting
    common = jnp.sqrt(keeping)
    private = jnp.sqrt(1.0 - keeping)
    cosines = jnp.cos(phases)
    sines = jnp.sin(phases)
    real_part = (common * (scene_real * cosines - scene_imag * sines) + private * noise[0]) * 0.7071
    imag_part = (common * (scene_real * sines + scene_imag * cosines) + private * noise[1]) * 0.7071
    return jnp.clip(jnp.stack([real_part, imag_part]), -16.0, 16.0).astype(jnp.bfloat16)


def draw_pairing(key, part):
    crossing = jax.random.randint(jax.random.fold_in(key, 21), (MATCH, ACQS // 2), 0, 2)
    acquired = jnp.arange(ACQS)
    grouped = acquired // 2
    member = acquired % 2
    matched = []
    for matching in range(MATCH):
        partner_group = jnp.bitwise_xor(grouped, matching + 1)
        lowest = jnp.minimum(grouped, partner_group)
        flipped = crossing[matching][lowest]
        matched.append(2 * partner_group + jnp.bitwise_xor(member, flipped))
    return jnp.stack(matched).astype(jnp.int32)


def draw_tile_offsets(key, part):
    folded = jax.random.fold_in(key, 31)
    picks = jax.random.randint(jax.random.fold_in(folded, 1), (2 * MATCH,), 0, PATCH)
    highest = jax.random.randint(jax.random.fold_in(folded, 2), (), 0, 2 * MATCH)
    lowest = (highest + 1 + jax.random.randint(jax.random.fold_in(folded, 3), (), 0, 2 * MATCH - 1)) % (2 * MATCH)
    counter = jnp.arange(2 * MATCH)
    picks = jnp.where(counter == highest, PATCH - 1, jnp.where(counter == lowest, 0, picks))
    return picks.reshape(MATCH, 2).astype(jnp.int32)


def setup_inputs(seed: int = 0, part: int = 0) -> dict:
    splits = jax.random.split(jax.random.key(seed), 4)
    part_keys = jax.random.split(jax.random.fold_in(splits[3], part), 4)
    images = draw_images(jax.random.fold_in(jax.random.fold_in(splits[3], part), 71), part)
    pairing = draw_pairing(jax.random.fold_in(splits[3], 71), part)
    tile_offsets = draw_tile_offsets(jax.random.fold_in(splits[3], 71), part)
    return dict(images=images, pairing=pairing, tile_offsets=tile_offsets)


EPSILON = 1e-06
HIGHEST = lax.Precision.HIGHEST

def gauss_band(height, breadth, offset, float_type):
    spread = jnp.arange(height)[:, None] - jnp.arange(breadth)[None, :] - offset
    width_scale = REACH / 8.0
    weights = jnp.exp(-(spread * spread).astype(float_type) / (2.0 * width_scale * width_scale))
    return jnp.where(jnp.abs(spread) <= REACH, weights, jnp.zeros_like(weights))

def dft_tables(float_type):
    counter = jnp.arange(PATCH)
    angles = 2.0 * jnp.pi / PATCH * (counter[:, None] * counter[None, :] % PATCH).astype(float_type)
    return (jnp.cos(angles), jnp.sin(angles))

def transform(table, field):
    return jnp.einsum('uy,aybx->aubx', table, field, precision=HIGHEST)

def transform_cols(table, field):
    return jnp.einsum('vx,aubx->aubv', table, field, precision=HIGHEST)

def patch_filter(real_part, imag_part, row_offset, col_offset):
    height = real_part.shape[0]
    breadth = real_part.shape[1] - 2 * REACH
    row_count = height // PATCH + 1
    col_count = breadth // PATCH + 1
    cosine_table, sine_table = dft_tables(real_part.dtype)

    def to_tiles(field):
        padded = jnp.pad(field, ((REACH, REACH), (0, 0)))
        window = lax.dynamic_slice(padded, (row_offset, col_offset), (height + PATCH, breadth + PATCH))
        return window.reshape(row_count, PATCH, col_count, PATCH)
    tile_real = to_tiles(real_part)
    tile_imag = to_tiles(imag_part)
    rowwise_real = transform(cosine_table, tile_real) + transform(sine_table, tile_imag)
    rowwise_imag = transform(cosine_table, tile_imag) - transform(sine_table, tile_real)
    freq_real = transform_cols(cosine_table, rowwise_real) + transform_cols(sine_table, rowwise_imag)
    freq_imag = transform_cols(cosine_table, rowwise_imag) - transform_cols(sine_table, rowwise_real)
    magnitude = jnp.sqrt(jnp.sqrt(freq_real * freq_real + freq_imag * freq_imag + EPSILON))
    scaling = magnitude / (lax.optimization_barrier(jnp.mean(magnitude, axis=(1, 3), keepdims=True)) + EPSILON)
    weighted_real = freq_real * scaling
    weighted_imag = freq_imag * scaling
    back_real = transform(cosine_table, weighted_real) - transform(sine_table, weighted_imag)
    back_imag = transform(cosine_table, weighted_imag) + transform(sine_table, weighted_real)
    final_real = (transform_cols(cosine_table, back_real) - transform_cols(sine_table, back_imag)) / (PATCH * PATCH)
    final_imag = (transform_cols(cosine_table, back_imag) + transform_cols(sine_table, back_real)) / (PATCH * PATCH)
    final_real = final_real.reshape(height + PATCH, breadth + PATCH)
    final_imag = final_imag.reshape(height + PATCH, breadth + PATCH)
    starts = (PATCH - row_offset, PATCH - col_offset)
    return (lax.dynamic_slice(final_real, starts, (height, breadth)), lax.dynamic_slice(final_imag, starts, (height, breadth)))

def pair_fields(local_image, remote_image):
    local_real, local_imag = (local_image[0], local_image[1])
    remote_real, remote_imag = (remote_image[0], remote_image[1])
    return jnp.stack([local_real * remote_real + local_imag * remote_imag, local_imag * remote_real - local_real * remote_imag, local_real * local_real + local_imag * local_imag, remote_real * remote_real + remote_imag * remote_imag], axis=-3)

def coherence_of(smoothed):
    inter_real = smoothed[..., 0, :, :]
    inter_imag = smoothed[..., 1, :, :]
    return (inter_real * inter_real + inter_imag * inter_imag) / (smoothed[..., 2, :, :] * smoothed[..., 3, :, :] + EPSILON)

def smooth_range(fields):
    field_count, height, breadth = fields.shape
    blocks = breadth // 128
    padded = jnp.pad(fields, ((0, 0), (0, 0), (REACH, 128 - REACH)))
    tiled_view = padded.reshape(field_count, height, blocks + 1, 128)
    window = jnp.concatenate([tiled_view[:, :, :-1], tiled_view[:, :, 1:, :2 * REACH]], axis=3)
    matrix = gauss_band(128 + 2 * REACH, 128, REACH, fields.dtype)
    smoothed = jnp.einsum('fhbj,jc->fhbc', window, matrix, precision=HIGHEST)
    return smoothed.reshape(field_count, height, breadth)

def reference(images, pairing, tile_offsets):
    coherence_rows = []
    filtered_rows = []
    for matching in range(MATCH):
        for acquired in range(ACQS):
            partner = pairing[matching, acquired]
            grouped = acquired // 2
            upper_half = 1 if grouped > grouped ^ matching + 1 else 0
            first_line = upper_half * HALF
            local_image = images[:, acquired, first_line:first_line + HALF].astype(jnp.float32)
            remote_image = lax.dynamic_index_in_dim(images, partner, 1, keepdims=False)[:, first_line:first_line + HALF].astype(jnp.float32)
            fields = pair_fields(local_image, remote_image)
            range_smoothed = smooth_range(fields)
            azimuth = gauss_band(HALF, HALF, 0, fields.dtype)
            smoothed = jnp.einsum('ih,fhc->fic', azimuth, range_smoothed, precision=HIGHEST)
            coherence_rows.append(coherence_of(smoothed))
            padded = jnp.pad(fields[:2], ((0, 0), (0, 0), (REACH, REACH)))
            filtered_real, filtered_imag = patch_filter(padded[0], padded[1], tile_offsets[matching, 0], tile_offsets[matching, 1])
            filtered_rows.append(jnp.stack([filtered_real, filtered_imag]))
    coherence = jnp.stack(coherence_rows).reshape(MATCH, ACQS, HALF, RANGE)
    filtered = jnp.stack(filtered_rows).reshape(MATCH, ACQS, 2, HALF, RANGE).transpose(2, 0, 1, 3, 4).astype(jnp.bfloat16)
    return (coherence, filtered)
```

```python
import functools

import jax
import jax.numpy as jnp
import numpy as np
from jax import lax
from jax.experimental import pallas as pl
from jax.experimental.pallas import tpu as pltpu
from jax.sharding import PartitionSpec as P

MATCH = 3
REACH = 32
PATCH = 32
EPSILON = 1e-06
BF = jnp.bfloat16
F32 = jnp.float32


def split_table(table):
    high = table.astype(np.float32).astype(BF)
    low = (table - high.astype(np.float64)).astype(np.float32).astype(BF)
    return high, low


def gauss(spread):
    width = REACH / 8.0
    weights = np.exp(-(spread.astype(np.float64) ** 2) / (2.0 * width * width))
    return np.where(np.abs(spread) <= REACH, weights, 0.0)


def range_table(breadth):
    lanes = breadth + 128
    row = np.arange(lanes)
    cell = np.where(row < breadth + REACH, row, row - lanes)
    band = gauss(cell[:, None] - np.arange(breadth)[None, :])
    valid = (row < breadth + REACH) | (row >= lanes - REACH)
    return split_table(band * valid[:, None])


def azimuth_table(height):
    line = np.arange(height)
    high, low = split_table(gauss(line[:, None] - line[None, :]))
    return np.concatenate([high, high, low], axis=1)


def waves(rows, cols):
    angle = 2.0 * np.pi / PATCH * ((rows[:, None] * cols[None, :]) % PATCH)
    return np.cos(angle), np.sin(angle)


def column_tables():
    lane = np.arange(128)
    same = (lane[:, None] // PATCH) == (lane[None, :] // PATCH)
    cosine, sine = waves(lane % PATCH, lane % PATCH)
    cosine, sine = cosine * same, sine * same
    forward = np.block([[cosine, -sine], [sine, cosine]])
    inverse = np.block([[cosine, sine], [-sine, cosine]]) / PATCH
    return split_table(forward), split_table(inverse), same.astype(np.float32).astype(BF)


def row_tables(height):
    patches = height // PATCH + 1
    freq = np.arange(patches * PATCH) % PATCH
    cosine, sine = waves(freq, np.arange(height))
    forward = np.block([[cosine, sine], [-sine, cosine]])
    fwd = split_table(forward)
    inv = split_table(forward.T / PATCH)
    return fwd, np.concatenate([inv[0], inv[0], inv[1]], axis=1)


def halves(value):
    high = value.astype(BF)
    return high, (value - high.astype(F32)).astype(BF)


def mm(left, right):
    return jnp.dot(left, right, preferred_element_type=F32)


def lane_group(shape):
    return lax.broadcasted_iota(jnp.int32, shape, 1) // REACH


def pack_kernel(image_ref, tail_ref, head_ref):
    breadth = image_ref.shape[3]
    for target, first, order in (
        (tail_ref, breadth - 128, ((0, 0, 0), (1, 0, 96), (0, 1, 64), (1, 1, 32))),
        (head_ref, 0, ((0, 0, 0), (1, 1, 32), (0, 1, 64), (1, 0, 96))),
    ):
        blocks = []
        for part, member, shift in order:
            cells = image_ref[part, member, :, first : first + 128].astype(F32)
            blocks.append(pltpu.roll(cells, shift, 1) if shift else cells)
        group = lane_group(blocks[0].shape)
        if first:
            picks = (3, 2, 1, 0)
        else:
            picks = (0, 1, 2, 3)
        value = blocks[picks[0]]
        for position in range(1, 4):
            value = jnp.where(group == position, blocks[picks[position]], value)
        target[...] = value.astype(BF)


def prep_kernel(image_ref, tail_ref, head_ref, far_ref, near_ref, rim_ref):
    lines, height = image_ref.shape[2], image_ref.shape[2] // 2
    tail = tail_ref[...].astype(F32)
    head = head_ref[...].astype(F32)
    odd = lane_group(tail.shape) % 2 == 1
    rim_ref[0] = jnp.where(odd, tail, head).astype(BF)
    rim_ref[1] = pltpu.roll(jnp.where(odd, head, tail), 32, 1).astype(BF)
    grouped = lax.axis_index("acq")
    for target, mask in ((near_ref, 1), (far_ref, 2)):
        upper = (grouped > jnp.bitwise_xor(grouped, mask)).astype(jnp.int32)
        start = pl.multiple_of((1 - upper) * height, height)
        for part in range(2):
            for member in range(2):
                target[2 * part + member] = image_ref[part, member, pl.ds(start, height), :]
            target[4, :, 128 * part : 128 * part + 128] = rim_ref[part, pl.ds(start, height), :]


def match_kernel(
    matching,
    aliased,
    pairing_ref,
    offset_ref,
    image_ref,
    rim_ref,
    remote_ref,
    band_high_ref,
    band_low_ref,
    azimuth_ref,
    forward_high_ref,
    forward_low_ref,
    inverse_high_ref,
    inverse_low_ref,
    same_ref,
    row_high_ref,
    row_low_ref,
    row_inverse_ref,
    *rest,
):
    coherence_ref, filtered_ref = rest[2:] if aliased else rest
    height = image_ref.shape[2] // 2
    breadth = image_ref.shape[3]
    lanes = breadth + 128
    patches = height // PATCH + 1
    freqs = patches * PATCH
    blocks = breadth // 128
    grouped = lax.axis_index("acq")
    upper = (grouped > jnp.bitwise_xor(grouped, matching + 1)).astype(jnp.int32)
    start = pl.multiple_of(upper * height, height)
    row_offset = offset_ref[matching, 0]
    col_offset = offset_ref[matching, 1]

    fields = []
    windows = []
    for member in range(2):
        partner = pairing_ref[matching, 2 * grouped + member] % 2
        ours, theirs = [], []
        for part in range(2):
            rim = rim_ref[part, pl.ds(start, height), :].astype(F32)
            if member:
                rim = pltpu.roll(rim, 64, 1)
            main = image_ref[part, member, pl.ds(start, height), :].astype(F32)
            ours.append(jnp.concatenate([main, rim], axis=1))
            rim = remote_ref[4, :, 128 * part : 128 * part + 128].astype(F32)
            rim = pltpu.roll(rim, 64 * partner, 1)
            main = remote_ref[2 * part + partner].astype(F32)
            theirs.append(jnp.concatenate([main, rim], axis=1))
        inter_real = ours[0] * theirs[0] + ours[1] * theirs[1]
        inter_imag = ours[1] * theirs[0] - ours[0] * theirs[1]
        fields += [
            inter_real,
            inter_imag,
            ours[0] * ours[0] + ours[1] * ours[1],
            theirs[0] * theirs[0] + theirs[1] * theirs[1],
        ]
        windows.append(
            pltpu.roll(jnp.concatenate([inter_real, inter_imag], axis=0), REACH - col_offset, 1)
        )

    field_high, field_low = halves(jnp.concatenate(fields, axis=0))
    band_high = band_high_ref[...]
    ranged = mm(field_high, band_high) + mm(field_low, band_high) + mm(field_high, band_low_ref[...])
    ranged_high, ranged_low = halves(ranged)
    azimuth = azimuth_ref[...]
    for member in range(2):
        smoothed = []
        for field in range(4):
            first = (4 * member + field) * height
            high = ranged_high[first : first + height]
            low = ranged_low[first : first + height]
            smoothed.append(mm(azimuth, jnp.concatenate([high, low, high], axis=0)))
        coherence_ref[0, member] = (smoothed[0] * smoothed[0] + smoothed[1] * smoothed[1]) / (
            smoothed[2] * smoothed[3] + EPSILON
        )

    last = jnp.where(
        lane_group((2 * height, 128)) == 0,
        windows[0][:, breadth:],
        pltpu.roll(windows[1][:, breadth:], 32, 1),
    )
    window = jnp.concatenate([windows[0][:, :breadth], windows[1][:, :breadth], last], axis=1)
    window_high, window_low = halves(window)

    def inside(shape, line_dim, freq_dim):
        line = lax.broadcasted_iota(jnp.int32, shape, line_dim) % height
        freq = lax.broadcasted_iota(jnp.int32, shape, freq_dim) % freqs
        mask = (line + PATCH - row_offset) // PATCH == freq // PATCH
        return jnp.where(mask, 1.0, 0.0).astype(BF)

    keep = inside((2 * freqs, 2 * height), 1, 0)
    row_high = row_high_ref[...] * keep
    row_low = row_low_ref[...] * keep
    rowwise = mm(
        jnp.concatenate([row_high, row_high], axis=1),
        jnp.concatenate([window_high, window_low], axis=0),
    ) + mm(row_low, window_high)
    groups = 2 * blocks + 1
    stacked = jnp.concatenate(
        [
            jnp.concatenate(
                [
                    rowwise[:freqs, 128 * group : 128 * group + 128],
                    rowwise[freqs:, 128 * group : 128 * group + 128],
                ],
                axis=1,
            )
            for group in range(groups)
        ],
        axis=0,
    )
    stacked_high, stacked_low = halves(stacked)
    forward_high = forward_high_ref[...]
    freq = (
        mm(stacked_high, forward_high)
        + mm(stacked_low, forward_high)
        + mm(stacked_high, forward_low_ref[...])
    )
    freq_real, freq_imag = freq[:, :128], freq[:, 128:]
    power = freq_real * freq_real + freq_imag * freq_imag + EPSILON
    magnitude = lax.rsqrt(lax.rsqrt(power))
    count = groups * patches
    sums = jnp.sum(magnitude.reshape(count, PATCH, 128), axis=1)
    sums_high, sums_low = halves(sums)
    same = same_ref[...]
    totals = mm(sums_high, same) + mm(sums_low, same)
    inverse = 1.0 / (totals * (1.0 / (PATCH * PATCH)) + EPSILON)
    scaling = (magnitude.reshape(count, PATCH, 128) * inverse[:, None, :]).reshape(-1, 128)
    weighted = jnp.concatenate([freq_real * scaling, freq_imag * scaling], axis=1)

    weighted_high, weighted_low = halves(weighted)
    inverse_high = inverse_high_ref[...]
    back = (
        mm(weighted_high, inverse_high)
        + mm(weighted_low, inverse_high)
        + mm(weighted_high, inverse_low_ref[...])
    )
    sides = jnp.concatenate(
        [
            jnp.concatenate(
                [
                    back[freqs * group : freqs * group + freqs, :128],
                    back[freqs * group : freqs * group + freqs, 128:],
                ],
                axis=0,
            )
            for group in range(groups)
        ],
        axis=1,
    )
    sides_high, sides_low = halves(sides)
    row_inverse = row_inverse_ref[...] * inside((2 * height, 6 * freqs), 0, 1)
    final = mm(row_inverse, jnp.concatenate([sides_high, sides_low, sides_high], axis=0))
    for member in range(2):
        edge = final[:, 2 * breadth :]
        if member:
            edge = pltpu.roll(edge, 96, 1)
        whole = jnp.concatenate([final[:, member * breadth : (member + 1) * breadth], edge], axis=1)
        cells = pltpu.roll(whole, lanes - REACH + col_offset, 1)[:, :breadth].astype(BF)
        filtered_ref[0, 0, member] = cells[:height]
        filtered_ref[1, 0, member] = cells[height:]


def vmem(count):
    return [pl.BlockSpec(memory_space=pltpu.VMEM)] * count


def match_call(matching, pairing, offsets, image, rims, remote, tables, previous):
    height, breadth = image.shape[2] // 2, image.shape[3]
    aliased = previous is not None
    inputs = [pairing, offsets, image, rims, remote, *tables]
    specs = [pl.BlockSpec(memory_space=pltpu.SMEM)] * 2 + vmem(3 + len(tables))
    aliases = {}
    if aliased:
        aliases = {len(inputs): 0, len(inputs) + 1: 1}
        inputs += list(previous)
        specs += [pl.BlockSpec(memory_space=pl.ANY)] * 2
    return pl.pallas_call(
        functools.partial(match_kernel, matching, aliased),
        grid=(1,),
        out_shape=(
            jax.ShapeDtypeStruct((MATCH, 2, height, breadth), F32),
            jax.ShapeDtypeStruct((2, MATCH, 2, height, breadth), BF),
        ),
        in_specs=specs,
        out_specs=(
            pl.BlockSpec((1, 2, height, breadth), lambda i: (matching, 0, 0, 0)),
            pl.BlockSpec((2, 1, 2, height, breadth), lambda i: (0, matching, 0, 0, 0)),
        ),
        input_output_aliases=aliases,
        cost_estimate=pl.CostEstimate(flops=2 * 10**9, bytes_accessed=3 * 10**6, transcendentals=0),
        name=f"match{matching}",
    )(*inputs)


def xor_swap(value, mask):
    return lax.ppermute(value, "acq", [(i, i ^ mask) for i in range(lax.axis_size("acq"))])


def per_device(images, pairing, tile_offsets):
    lines, breadth = images.shape[2:]
    height = lines // 2
    forward, inverse, same = column_tables()
    row_forward, row_inverse = row_tables(height)
    tables = [
        jnp.asarray(table)
        for table in (
            *range_table(breadth),
            azimuth_table(height),
            *forward,
            *inverse,
            same,
            *row_forward,
            row_inverse,
        )
    ]
    tail, head = pl.pallas_call(
        pack_kernel,
        out_shape=(jax.ShapeDtypeStruct((lines, 128), BF),) * 2,
        in_specs=vmem(1),
        out_specs=tuple(vmem(2)),
        name="pack",
    )(images)
    ends = lax.axis_size("rng") - 1
    tail = lax.ppermute(tail, "rng", [(i, i + 1) for i in range(ends)])
    head = lax.ppermute(head, "rng", [(i + 1, i) for i in range(ends)])
    payload = jax.ShapeDtypeStruct((5, height, breadth), BF)
    far, near, rims = pl.pallas_call(
        prep_kernel,
        out_shape=(payload, payload, jax.ShapeDtypeStruct((2, lines, 128), BF)),
        in_specs=vmem(3),
        out_specs=tuple(vmem(3)),
        name="prep",
    )(images, tail, head)
    far = xor_swap(far, 2)
    near = xor_swap(near, 1)
    both = xor_swap(far, 1)
    outputs = None
    for matching, remote in enumerate((near, far, both)):
        outputs = match_call(
            matching, pairing, tile_offsets, images, rims, remote, tables, outputs
        )
    return outputs


def solution(mesh):
    in_specs = (P(None, ("stack", "acq"), None, "rng"), P(), P())
    out_specs = (
        P(None, ("stack", "acq"), None, "rng"),
        P(None, None, ("stack", "acq"), None, "rng"),
    )
    return jax.shard_map(
        per_device, mesh=mesh, in_specs=in_specs, out_specs=out_specs, check_vma=False
    )
```

```python
import functools

import jax
import jax.numpy as jnp
import numpy as np
from jax import lax
from jax.experimental import pallas as pl
from jax.experimental.pallas import tpu as pltpu
from jax.sharding import PartitionSpec as P

MATCH = 3
REACH = 32
PATCH = 32
EPSILON = 1e-06
BF = jnp.bfloat16
F32 = jnp.float32
GRANT = pltpu.CompilerParams(vmem_limit_bytes=24 << 20)


def split_table(table):
    high = table.astype(np.float32).astype(BF)
    low = (table - high.astype(np.float64)).astype(np.float32).astype(BF)
    return high, low


def gauss(spread):
    width = REACH / 8.0
    weights = np.exp(-(spread.astype(np.float64) ** 2) / (2.0 * width * width))
    return np.where(np.abs(spread) <= REACH, weights, 0.0)


def range_table(breadth):
    lanes = breadth + 128
    row = np.arange(lanes)
    cell = np.where(row < breadth + REACH, row, row - lanes)
    band = gauss(cell[:, None] - np.arange(breadth)[None, :])
    valid = (row < breadth + REACH) | (row >= lanes - REACH)
    return split_table(band * valid[:, None])


def azimuth_table(height):
    line = np.arange(height)
    high, low = split_table(gauss(line[:, None] - line[None, :]))
    return np.concatenate([high, high, low], axis=1)


def waves(rows, cols):
    angle = 2.0 * np.pi / PATCH * ((rows[:, None] * cols[None, :]) % PATCH)
    return np.cos(angle), np.sin(angle)


def column_tables():
    lane = np.arange(128)
    same = (lane[:, None] // PATCH) == (lane[None, :] // PATCH)
    cosine, sine = waves(lane % PATCH, lane % PATCH)
    cosine, sine = cosine * same, sine * same
    forward = np.block([[cosine, -sine], [sine, cosine]])
    inverse = np.block([[cosine, sine], [-sine, cosine]]) / PATCH
    return split_table(forward), split_table(inverse), same.astype(np.float32).astype(BF)


def row_tables(height):
    patches = height // PATCH + 1
    freq = np.arange(patches * PATCH) % PATCH
    cosine, sine = waves(freq, np.arange(height))
    forward = np.block([[cosine, sine], [-sine, cosine]])
    fwd = split_table(forward)
    inv = split_table(forward.T / PATCH)
    return fwd, np.concatenate([inv[0], inv[0], inv[1]], axis=1)


def all_tables(breadth, height):
    forward, inverse, same = column_tables()
    row_forward, row_inverse = row_tables(height)
    parts = {}
    parts["band_high"], parts["band_low"] = range_table(breadth)
    parts["forward_high"], parts["forward_low"] = forward
    parts["inverse_high"], parts["inverse_low"] = inverse
    parts["row_high"], parts["row_low"] = row_forward
    parts["row_inverse"] = row_inverse
    parts["azimuth"] = azimuth_table(height)
    parts["same"] = same
    places, rows, start = {}, [], 0
    for name, part in parts.items():
        tall = -(-part.shape[0] // 16) * 16
        places[name] = []
        for first in range(0, part.shape[1], 256):
            piece = part[:, first : first + 256]
            block = np.zeros((tall, 256), BF)
            block[: piece.shape[0], : piece.shape[1]] = piece
            places[name].append((start, *piece.shape))
            rows.append(block)
            start += tall
    return np.concatenate(rows, axis=0), places


def halves(value):
    high = value.astype(BF)
    return high, (value - high.astype(F32)).astype(BF)


def mm(left, right):
    return jnp.dot(left, right, preferred_element_type=F32)


def lane_group(shape):
    return lax.broadcasted_iota(jnp.int32, shape, 1) >> 5


def even_place():
    return lax.axis_index("rng") % 2 == 0


def pack_kernel(image_ref, first_ref, second_ref):
    breadth = image_ref.shape[3]
    group = lane_group((image_ref.shape[2], 128))
    sides = []
    for first, order in (
        (breadth - 128, ((1, 1, 32), (0, 1, 64), (1, 0, 96), (0, 0, 0))),
        (0, ((0, 0, 0), (1, 1, 32), (0, 1, 64), (1, 0, 96))),
    ):
        value = None
        for position, (part, member, shift) in enumerate(order):
            cells = image_ref[part, member, :, first : first + 128].astype(F32)
            cells = pltpu.roll(cells, shift, 1) if shift else cells
            value = cells if value is None else jnp.where(group == position, cells, value)
        sides.append(value)
    tail, head = sides
    even = even_place()
    first_ref[...] = jnp.where(even, tail, head).astype(BF)
    second_ref[...] = jnp.where(even, head, tail).astype(BF)


def main_kernel(image_ref, far_ref, near_ref):
    height = image_ref.shape[2] // 2
    grouped = lax.axis_index("acq")
    for target, mask in ((near_ref, 1), (far_ref, 2)):
        upper = (grouped > jnp.bitwise_xor(grouped, mask)).astype(jnp.int32)
        start = pl.multiple_of((1 - upper) * height, height)
        for part in range(2):
            for member in range(2):
                target[2 * part + member] = image_ref[part, member, pl.ds(start, height), :]


def rim_kernel(ends, first_ref, second_ref, far_in, near_in, far_ref, near_ref, rim_ref):
    height = far_ref.shape[1]
    even = even_place()
    place = lax.axis_index("rng")
    first = first_ref[...].astype(F32)
    second = second_ref[...].astype(F32)
    head = jnp.where(place < ends, jnp.where(even, first, second), 0.0)
    tail = jnp.where(place > 0, jnp.where(even, second, first), 0.0)
    odd = (lane_group(tail.shape) & 1) == 1
    rim_ref[0] = jnp.where(odd, tail, head).astype(BF)
    rim_ref[1] = pltpu.roll(jnp.where(odd, head, tail), 32, 1).astype(BF)
    grouped = lax.axis_index("acq")
    for target, mask in ((near_ref, 1), (far_ref, 2)):
        upper = (grouped > jnp.bitwise_xor(grouped, mask)).astype(jnp.int32)
        start = pl.multiple_of((1 - upper) * height, height)
        for part in range(2):
            target[4, :, 128 * part : 128 * part + 128] = rim_ref[part, pl.ds(start, height), :]


def match_kernel(matching, aliased, places, pairing_ref, offset_ref, image_ref, rim_ref, remote_ref, table_ref, *rest):
    coherence_ref, filtered_ref = rest[2:] if aliased else rest
    height = image_ref.shape[2] // 2
    breadth = image_ref.shape[3]
    lanes = breadth + 128
    patches = height // PATCH + 1
    freqs = patches * PATCH
    blocks = breadth // 128
    grouped = lax.axis_index("acq")
    upper = (grouped > jnp.bitwise_xor(grouped, matching + 1)).astype(jnp.int32)
    start = pl.multiple_of(upper * height, height)
    row_offset = offset_ref[0, matching]
    col_offset = offset_ref[1, matching]

    def table(name):
        pieces = [table_ref[first : first + rows, :cols] for first, rows, cols in places[name]]
        return jnp.concatenate(pieces, axis=1) if len(pieces) > 1 else pieces[0]

    fields = []
    windows = []
    for member in range(2):
        partner = pairing_ref[matching, 2 * grouped + member] % 2
        ours, theirs = [], []
        for part in range(2):
            rim = rim_ref[part, pl.ds(start, height), :].astype(F32)
            if member:
                rim = pltpu.roll(rim, 64, 1)
            main = image_ref[part, member, pl.ds(start, height), :].astype(F32)
            ours.append(jnp.concatenate([main, rim], axis=1))
            rim = remote_ref[4, :, 128 * part : 128 * part + 128].astype(F32)
            rim = pltpu.roll(rim, 64 * partner, 1)
            main = remote_ref[2 * part + partner].astype(F32)
            theirs.append(jnp.concatenate([main, rim], axis=1))
        inter_real = ours[0] * theirs[0] + ours[1] * theirs[1]
        inter_imag = ours[1] * theirs[0] - ours[0] * theirs[1]
        fields.append(
            [
                inter_real,
                inter_imag,
                ours[0] * ours[0] + ours[1] * ours[1],
                theirs[0] * theirs[0] + theirs[1] * theirs[1],
            ]
        )
        windows.append(
            [pltpu.roll(value, REACH - col_offset, 1) for value in (inter_real, inter_imag)]
        )
    first_lanes = lane_group((height, 128)) == 0
    shared = [
        jnp.where(
            first_lanes,
            windows[0][part][:, breadth:],
            pltpu.roll(windows[1][part][:, breadth:], 32, 1),
        )
        for part in range(2)
    ]

    def groups_of(member):
        found = [
            jnp.concatenate(
                [part[:, 128 * block : 128 * block + 128] for part in windows[member]], axis=1
            )
            for block in range(blocks)
        ]
        return found + ([jnp.concatenate(shared, axis=1)] if member == 0 else [])

    band_high, band_low = table("band_high"), table("band_low")
    forward_high, forward_low = table("forward_high"), table("forward_low")
    inverse_high, inverse_low = table("inverse_high"), table("inverse_low")
    azimuth = table("azimuth")

    ranged = []
    columns = []
    for member in range(2):
        high, low = halves(jnp.concatenate(fields[member], axis=0))
        ranged.append(mm(high, band_high) + mm(low, band_high) + mm(high, band_low))
        high, low = halves(jnp.concatenate(groups_of(member), axis=0))
        columns.append(mm(high, forward_high) + mm(low, forward_high) + mm(high, forward_low))

    line = lax.broadcasted_iota(jnp.int32, (PATCH, 2 * height), 1) & (height - 1)
    patch = (line + PATCH - row_offset) >> 5
    keep = jnp.concatenate(
        [jnp.where(patch == place, 1.0, 0.0).astype(BF) for place in range(patches)] * 2, axis=0
    )
    row_high = table("row_high") * keep
    row_low = table("row_low") * keep
    row_twice = jnp.concatenate([row_high, row_high], axis=1)
    line = lax.broadcasted_iota(jnp.int32, (2 * height, 6 * freqs), 0) & (height - 1)
    lane = lax.broadcasted_iota(jnp.int32, (8, 6 * freqs), 1)
    for step in (4, 2, 1):
        lane = jnp.where(lane >= step * freqs, lane - step * freqs, lane)
    keep = ((line + PATCH - row_offset) >> 5) == (lane >> 5)[:1]
    row_inverse = table("row_inverse") * jnp.where(keep, 1.0, 0.0).astype(BF)

    weighted = []
    same = table("same")
    for member in range(2):
        high, low = halves(ranged[member])
        smoothed = [
            mm(
                azimuth,
                jnp.concatenate(
                    [piece[field * height : field * height + height] for piece in (high, low, high)],
                    axis=0,
                ),
            )
            for field in range(4)
        ]
        coherence_ref[0, member] = (smoothed[0] * smoothed[0] + smoothed[1] * smoothed[1]) / (
            smoothed[2] * smoothed[3] + EPSILON
        )
        column = columns[member]
        count = column.shape[0] // height
        column = jnp.concatenate(
            [
                jnp.concatenate(
                    [column[height * group : height * group + height, 128 * part : 128 * part + 128] for part in range(2)],
                    axis=0,
                )
                for group in range(count)
            ],
            axis=1,
        )
        high, low = halves(column)
        freq = mm(row_twice, jnp.concatenate([high, low], axis=0)) + mm(row_low, high)
        freq_real, freq_imag = freq[:freqs], freq[freqs:]
        power = freq_real * freq_real + freq_imag * freq_imag + EPSILON
        magnitude = lax.rsqrt(lax.rsqrt(power))
        sums = jnp.concatenate(
            [
                jnp.sum(
                    magnitude[PATCH * place : PATCH * place + PATCH, 128 * group : 128 * group + 128],
                    axis=0,
                    keepdims=True,
                )
                for group in range(count)
                for place in range(patches)
            ],
            axis=0,
        )
        high, low = halves(sums)
        totals = mm(high, same) + mm(low, same)
        inverse = 1.0 / (totals * (1.0 / (PATCH * PATCH)) + EPSILON)
        scaling = jnp.concatenate(
            [
                jnp.concatenate(
                    [
                        magnitude[PATCH * place : PATCH * place + PATCH, 128 * group : 128 * group + 128]
                        * inverse[group * patches + place : group * patches + place + 1]
                        for place in range(patches)
                    ],
                    axis=0,
                )
                for group in range(count)
            ],
            axis=1,
        )
        weighted.append(jnp.concatenate([freq_real * scaling, freq_imag * scaling], axis=0))

    final = []
    for member in range(2):
        high, low = halves(weighted[member])
        back = mm(row_inverse, jnp.concatenate([high, low, high], axis=0))
        count = back.shape[1] // 128
        back = jnp.concatenate(
            [
                jnp.concatenate(
                    [back[height * part : height * part + height, 128 * group : 128 * group + 128] for part in range(2)],
                    axis=1,
                )
                for group in range(count)
            ],
            axis=0,
        )
        high, low = halves(back)
        final.append(mm(high, inverse_high) + mm(low, inverse_high) + mm(high, inverse_low))
    edge = final[0][blocks * height :]
    for member in range(2):
        for part in range(2):
            side = edge[:, 128 * part : 128 * part + 128]
            whole = jnp.concatenate(
                [
                    final[member][height * block : height * block + height, 128 * part : 128 * part + 128]
                    for block in range(blocks)
                ]
                + [pltpu.roll(side, 96, 1) if member else side],
                axis=1,
            )
            cells = pltpu.roll(whole, lanes - REACH + col_offset, 1)[:, :breadth]
            filtered_ref[part, 0, member] = cells.astype(BF)


def vmem(count):
    return [pl.BlockSpec(memory_space=pltpu.VMEM)] * count


def match_call(pairing, offsets, image, rims, table, places, matching, remote, previous):
    height, breadth = image.shape[2] // 2, image.shape[3]
    aliased = previous is not None
    inputs = [pairing, offsets, image, rims, remote, table]
    specs = [pl.BlockSpec(memory_space=pltpu.SMEM)] * 2 + vmem(4)
    aliases = {}
    if aliased:
        aliases = {len(inputs): 0, len(inputs) + 1: 1}
        inputs += list(previous)
        specs += [pl.BlockSpec(memory_space=pl.ANY)] * 2
    return pl.pallas_call(
        functools.partial(match_kernel, matching, aliased, places),
        grid=(1,),
        out_shape=(
            jax.ShapeDtypeStruct((MATCH, 2, height, breadth), F32),
            jax.ShapeDtypeStruct((2, MATCH, 2, height, breadth), BF),
        ),
        in_specs=specs,
        out_specs=(
            pl.BlockSpec((1, 2, height, breadth), lambda i: (matching, 0, 0, 0)),
            pl.BlockSpec((2, 1, 2, height, breadth), lambda i: (0, matching, 0, 0, 0)),
        ),
        input_output_aliases=aliases,
        cost_estimate=pl.CostEstimate(flops=2 * 10**9, bytes_accessed=3 * 10**6, transcendentals=0),
        compiler_params=GRANT,
        name=f"match{matching}",
    )(*inputs)


def xor_swap(value, mask):
    return lax.ppermute(value, "acq", [(i, i ^ mask) for i in range(lax.axis_size("acq"))])


def neighbour_swap(value, parity):
    places, groups = lax.axis_size("rng"), lax.axis_size("acq")
    pairs = []
    for group in range(groups):
        for place in range(places):
            other = place + 1 if place % 2 == parity else place - 1
            if 0 <= other < places:
                target = group * places + other
            else:
                target = (group ^ 1) * places + place
            pairs.append((group * places + place, target))
    return lax.ppermute(value, ("acq", "rng"), pairs)


def per_device(images, pairing, tile_offsets):
    lines, breadth = images.shape[2:]
    height = lines // 2
    table, places = all_tables(breadth, height)
    table = jnp.asarray(table)
    side = jax.ShapeDtypeStruct((lines, 128), BF)
    payload = jax.ShapeDtypeStruct((5, height, breadth), BF)
    first, second = pl.pallas_call(
        pack_kernel,
        out_shape=(side, side),
        in_specs=vmem(1),
        out_specs=tuple(vmem(2)),
        compiler_params=GRANT,
        name="pack",
    )(images)
    first = neighbour_swap(first, 0)
    second = neighbour_swap(second, 1)
    far, near = pl.pallas_call(
        main_kernel,
        out_shape=(payload, payload),
        in_specs=vmem(1),
        out_specs=tuple(vmem(2)),
        compiler_params=GRANT,
        name="mains",
    )(images)
    far, near, rims = pl.pallas_call(
        functools.partial(rim_kernel, lax.axis_size("rng") - 1),
        out_shape=(payload, payload, jax.ShapeDtypeStruct((2, lines, 128), BF)),
        in_specs=vmem(4),
        out_specs=tuple(vmem(3)),
        input_output_aliases={2: 0, 3: 1},
        compiler_params=GRANT,
        name="rims",
    )(first, second, far, near)
    far = xor_swap(far, 2)
    near = xor_swap(near, 1)
    call = functools.partial(match_call, pairing, tile_offsets.T, images, rims, table, places)
    outputs = call(0, near, None)
    far, *outputs = lax.optimization_barrier((far, *outputs))
    both = xor_swap(far, 1)
    outputs = call(1, far, outputs)
    return call(2, both, outputs)


def solution(mesh):
    in_specs = (P(None, ("stack", "acq"), None, "rng"), P(), P())
    out_specs = (
        P(None, ("stack", "acq"), None, "rng"),
        P(None, None, ("stack", "acq"), None, "rng"),
    )
    return jax.shard_map(
        per_device, mesh=mesh, in_specs=in_specs, out_specs=out_specs, check_vma=False
    )
```

```python
import functools

import jax
import jax.numpy as jnp
import numpy as np
from jax import lax
from jax.experimental import pallas as pl
from jax.experimental.pallas import tpu as pltpu
from jax.sharding import PartitionSpec as P

MATCH = 3
REACH = 32
PATCH = 32
EPSILON = 1e-06
BF = jnp.bfloat16
F32 = jnp.float32
GRANT = pltpu.CompilerParams(vmem_limit_bytes=24 << 20)


def split_table(table):
    high = table.astype(np.float32).astype(BF)
    low = (table - high.astype(np.float64)).astype(np.float32).astype(BF)
    return high, low


def gauss(spread):
    width = REACH / 8.0
    weights = np.exp(-(spread.astype(np.float64) ** 2) / (2.0 * width * width))
    return np.where(np.abs(spread) <= REACH, weights, 0.0)


def range_table(breadth):
    lanes = breadth + 128
    row = np.arange(lanes)
    cell = np.where(row < breadth + REACH, row, row - lanes)
    band = gauss(cell[:, None] - np.arange(breadth)[None, :])
    valid = (row < breadth + REACH) | (row >= lanes - REACH)
    return split_table(band * valid[:, None])


def azimuth_table(height):
    line = np.arange(height)
    high, low = split_table(gauss(line[:, None] - line[None, :]))
    return np.concatenate([high, high, low], axis=1)


def waves(rows, cols):
    angle = 2.0 * np.pi / PATCH * ((rows[:, None] * cols[None, :]) % PATCH)
    return np.cos(angle), np.sin(angle)


def column_tables():
    lane = np.arange(128)
    same = (lane[:, None] // PATCH) == (lane[None, :] // PATCH)
    cosine, sine = waves(lane % PATCH, lane % PATCH)
    cosine, sine = cosine * same, sine * same
    forward = np.block([[cosine, -sine], [sine, cosine]])
    inverse = np.block([[cosine, sine], [-sine, cosine]]) / PATCH
    return split_table(forward), split_table(inverse), same.astype(np.float32).astype(BF)


def row_tables(height):
    patches = height // PATCH + 1
    freq = np.arange(patches * PATCH) % PATCH
    cosine, sine = waves(freq, np.arange(height))
    forward = np.block([[cosine, sine], [-sine, cosine]])
    fwd = split_table(forward)
    inv = split_table(forward.T / PATCH)
    return fwd, np.concatenate([inv[0], inv[0], inv[1]], axis=1)


def all_tables(breadth, height):
    forward, inverse, same = column_tables()
    row_forward, row_inverse = row_tables(height)
    parts = {}
    parts["band_high"], parts["band_low"] = range_table(breadth)
    parts["forward_high"], parts["forward_low"] = forward
    parts["inverse_high"], parts["inverse_low"] = inverse
    parts["row_high"], parts["row_low"] = row_forward
    parts["row_inverse"] = row_inverse
    parts["azimuth"] = azimuth_table(height)
    parts["same"] = same
    places, rows, start = {}, [], 0
    for name, part in parts.items():
        tall = -(-part.shape[0] // 16) * 16
        places[name] = []
        for first in range(0, part.shape[1], 256):
            piece = part[:, first : first + 256]
            block = np.zeros((tall, 256), BF)
            block[: piece.shape[0], : piece.shape[1]] = piece
            places[name].append((start, *piece.shape))
            rows.append(block)
            start += tall
    return np.concatenate(rows, axis=0), places


def halves(value):
    high = value.astype(BF)
    return high, (value - high.astype(F32)).astype(BF)


def mm(left, right):
    return jnp.dot(left, right, preferred_element_type=F32)


def lane_group(shape):
    return lax.broadcasted_iota(jnp.int32, shape, 1) >> 5


def even_place():
    return lax.axis_index("rng") % 2 == 0


def pack_kernel(source_ref, image_ref, first_ref, second_ref, sem):
    copy = pltpu.make_async_copy(source_ref, image_ref, sem)
    copy.start()
    copy.wait()
    breadth = image_ref.shape[3]
    group = lane_group((image_ref.shape[2], 128))
    sides = []
    for first, order in (
        (breadth - 128, ((1, 1, 32), (0, 1, 64), (1, 0, 96), (0, 0, 0))),
        (0, ((0, 0, 0), (1, 1, 32), (0, 1, 64), (1, 0, 96))),
    ):
        value = None
        for position, (part, member, shift) in enumerate(order):
            cells = image_ref[part, member, :, first : first + 128].astype(F32)
            cells = pltpu.roll(cells, shift, 1) if shift else cells
            value = cells if value is None else jnp.where(group == position, cells, value)
        sides.append(value)
    tail, head = sides
    even = even_place()
    first_ref[...] = jnp.where(even, tail, head).astype(BF)
    second_ref[...] = jnp.where(even, head, tail).astype(BF)


def main_kernel(
    image_ref,
    pairing_source,
    offset_source,
    table_source,
    far_ref,
    near_ref,
    pairing_ref,
    offset_ref,
    table_ref,
    pairing_sem,
    offset_sem,
    table_sem,
):
    copies = [
        pltpu.make_async_copy(table_source, table_ref, table_sem),
        pltpu.make_async_copy(pairing_source, pairing_ref, pairing_sem),
        pltpu.make_async_copy(offset_source, offset_ref, offset_sem),
    ]
    for copy in copies:
        copy.start()
    height = image_ref.shape[2] // 2
    grouped = lax.axis_index("acq")
    for target, mask in ((near_ref, 1), (far_ref, 2)):
        upper = (grouped > jnp.bitwise_xor(grouped, mask)).astype(jnp.int32)
        start = pl.multiple_of((1 - upper) * height, height)
        for part in range(2):
            for member in range(2):
                target[2 * part + member] = image_ref[part, member, pl.ds(start, height), :]
    for copy in copies:
        copy.wait()


def rim_kernel(ends, first_ref, second_ref, far_in, near_in, far_ref, near_ref, rim_ref):
    height = far_ref.shape[1]
    even = even_place()
    place = lax.axis_index("rng")
    first = first_ref[...].astype(F32)
    second = second_ref[...].astype(F32)
    head = jnp.where(place < ends, jnp.where(even, first, second), 0.0)
    tail = jnp.where(place > 0, jnp.where(even, second, first), 0.0)
    odd = (lane_group(tail.shape) & 1) == 1
    rim_ref[0] = jnp.where(odd, tail, head).astype(BF)
    rim_ref[1] = pltpu.roll(jnp.where(odd, head, tail), 32, 1).astype(BF)
    grouped = lax.axis_index("acq")
    for target, mask in ((near_ref, 1), (far_ref, 2)):
        upper = (grouped > jnp.bitwise_xor(grouped, mask)).astype(jnp.int32)
        start = pl.multiple_of((1 - upper) * height, height)
        for part in range(2):
            target[4, :, 128 * part : 128 * part + 128] = rim_ref[part, pl.ds(start, height), :]


def match_kernel(
    matching,
    places,
    finish,
    pairing_ref,
    offset_ref,
    image_ref,
    rim_ref,
    remote_ref,
    table_ref,
    *rest,
):
    copies = []
    if finish:
        earlier, (coherence_out, filtered_out) = rest[: 2 * matching], rest[2 * matching :][:2]
        coherence_ref, filtered_ref, sems = rest[2 * matching + 2 :]

        def send(source, target):
            copy = pltpu.make_async_copy(source, target, sems.at[len(copies)])
            copy.start()
            copies.append(copy)

        for index in range(matching):
            send(earlier[2 * index], coherence_out.at[index])
            for part in range(2):
                send(earlier[2 * index + 1].at[part], filtered_out.at[part, index])
    else:
        coherence_ref, filtered_ref = rest
    height = image_ref.shape[2] // 2
    breadth = image_ref.shape[3]
    lanes = breadth + 128
    patches = height // PATCH + 1
    freqs = patches * PATCH
    blocks = breadth // 128
    grouped = lax.axis_index("acq")
    upper = (grouped > jnp.bitwise_xor(grouped, matching + 1)).astype(jnp.int32)
    start = pl.multiple_of(upper * height, height)
    row_offset = offset_ref[0, matching]
    col_offset = offset_ref[1, matching]

    def table(name):
        pieces = [table_ref[first : first + rows, :cols] for first, rows, cols in places[name]]
        return jnp.concatenate(pieces, axis=1) if len(pieces) > 1 else pieces[0]

    fields = []
    windows = []
    for member in range(2):
        partner = pairing_ref[matching, 2 * grouped + member] % 2
        ours, theirs = [], []
        for part in range(2):
            rim = rim_ref[part, pl.ds(start, height), :].astype(F32)
            if member:
                rim = pltpu.roll(rim, 64, 1)
            main = image_ref[part, member, pl.ds(start, height), :].astype(F32)
            ours.append(jnp.concatenate([main, rim], axis=1))
            rim = remote_ref[4, :, 128 * part : 128 * part + 128].astype(F32)
            rim = pltpu.roll(rim, 64 * partner, 1)
            main = remote_ref[2 * part + partner].astype(F32)
            theirs.append(jnp.concatenate([main, rim], axis=1))
        inter_real = ours[0] * theirs[0] + ours[1] * theirs[1]
        inter_imag = ours[1] * theirs[0] - ours[0] * theirs[1]
        fields.append(
            [
                inter_real,
                inter_imag,
                ours[0] * ours[0] + ours[1] * ours[1],
                theirs[0] * theirs[0] + theirs[1] * theirs[1],
            ]
        )
        windows.append(
            [pltpu.roll(value, REACH - col_offset, 1) for value in (inter_real, inter_imag)]
        )
    first_lanes = lane_group((height, 128)) == 0
    shared = [
        jnp.where(
            first_lanes,
            windows[0][part][:, breadth:],
            pltpu.roll(windows[1][part][:, breadth:], 32, 1),
        )
        for part in range(2)
    ]

    def groups_of(member):
        found = [
            jnp.concatenate(
                [part[:, 128 * block : 128 * block + 128] for part in windows[member]], axis=1
            )
            for block in range(blocks)
        ]
        return found + ([jnp.concatenate(shared, axis=1)] if member == 0 else [])

    band_high, band_low = table("band_high"), table("band_low")
    forward_high, forward_low = table("forward_high"), table("forward_low")
    inverse_high, inverse_low = table("inverse_high"), table("inverse_low")
    azimuth = table("azimuth")

    ranged = []
    columns = []
    for member in range(2):
        high, low = halves(jnp.concatenate(fields[member], axis=0))
        ranged.append(mm(high, band_high) + mm(low, band_high) + mm(high, band_low))
        high, low = halves(jnp.concatenate(groups_of(member), axis=0))
        columns.append(mm(high, forward_high) + mm(low, forward_high) + mm(high, forward_low))

    line = lax.broadcasted_iota(jnp.int32, (PATCH, 2 * height), 1) & (height - 1)
    patch = (line + PATCH - row_offset) >> 5
    keep = jnp.concatenate(
        [jnp.where(patch == place, 1.0, 0.0).astype(BF) for place in range(patches)] * 2, axis=0
    )
    row_high = table("row_high") * keep
    row_low = table("row_low") * keep
    row_twice = jnp.concatenate([row_high, row_high], axis=1)
    line = lax.broadcasted_iota(jnp.int32, (2 * height, 6 * freqs), 0) & (height - 1)
    lane = lax.broadcasted_iota(jnp.int32, (8, 6 * freqs), 1)
    for step in (4, 2, 1):
        lane = jnp.where(lane >= step * freqs, lane - step * freqs, lane)
    keep = ((line + PATCH - row_offset) >> 5) == (lane >> 5)[:1]
    row_inverse = table("row_inverse") * jnp.where(keep, 1.0, 0.0).astype(BF)

    weighted = []
    same = table("same")
    for member in range(2):
        high, low = halves(ranged[member])
        smoothed = [
            mm(
                azimuth,
                jnp.concatenate(
                    [piece[field * height : field * height + height] for piece in (high, low, high)],
                    axis=0,
                ),
            )
            for field in range(4)
        ]
        coherence_ref[member] = (smoothed[0] * smoothed[0] + smoothed[1] * smoothed[1]) / (
            smoothed[2] * smoothed[3] + EPSILON
        )
        if finish:
            send(coherence_ref.at[member], coherence_out.at[matching, member])
        column = columns[member]
        count = column.shape[0] // height
        column = jnp.concatenate(
            [
                jnp.concatenate(
                    [column[height * group : height * group + height, 128 * part : 128 * part + 128] for part in range(2)],
                    axis=0,
                )
                for group in range(count)
            ],
            axis=1,
        )
        high, low = halves(column)
        freq = mm(row_twice, jnp.concatenate([high, low], axis=0)) + mm(row_low, high)
        freq_real, freq_imag = freq[:freqs], freq[freqs:]
        power = freq_real * freq_real + freq_imag * freq_imag + EPSILON
        magnitude = lax.rsqrt(lax.rsqrt(power))
        sums = jnp.concatenate(
            [
                jnp.sum(
                    magnitude[PATCH * place : PATCH * place + PATCH, 128 * group : 128 * group + 128],
                    axis=0,
                    keepdims=True,
                )
                for group in range(count)
                for place in range(patches)
            ],
            axis=0,
        )
        high, low = halves(sums)
        totals = mm(high, same) + mm(low, same)
        inverse = 1.0 / (totals * (1.0 / (PATCH * PATCH)) + EPSILON)
        scaling = jnp.concatenate(
            [
                jnp.concatenate(
                    [
                        magnitude[PATCH * place : PATCH * place + PATCH, 128 * group : 128 * group + 128]
                        * inverse[group * patches + place : group * patches + place + 1]
                        for place in range(patches)
                    ],
                    axis=0,
                )
                for group in range(count)
            ],
            axis=1,
        )
        weighted.append(jnp.concatenate([freq_real * scaling, freq_imag * scaling], axis=0))

    final = []
    for member in range(2):
        high, low = halves(weighted[member])
        back = mm(row_inverse, jnp.concatenate([high, low, high], axis=0))
        count = back.shape[1] // 128
        back = jnp.concatenate(
            [
                jnp.concatenate(
                    [back[height * part : height * part + height, 128 * group : 128 * group + 128] for part in range(2)],
                    axis=1,
                )
                for group in range(count)
            ],
            axis=0,
        )
        high, low = halves(back)
        final.append(mm(high, inverse_high) + mm(low, inverse_high) + mm(high, inverse_low))
    edge = final[0][blocks * height :]
    for member in range(2):
        for part in range(2):
            side = edge[:, 128 * part : 128 * part + 128]
            whole = jnp.concatenate(
                [
                    final[member][height * block : height * block + height, 128 * part : 128 * part + 128]
                    for block in range(blocks)
                ]
                + [pltpu.roll(side, 96, 1) if member else side],
                axis=1,
            )
            cells = pltpu.roll(whole, lanes - REACH + col_offset, 1)[:, :breadth]
            filtered_ref[part, member] = cells.astype(BF)
            if finish:
                send(filtered_ref.at[part, member], filtered_out.at[part, matching, member])
    for copy in copies:
        copy.wait()


def in_hbm(value):
    return pltpu.with_memory_space_constraint(value, pltpu.HBM)


def vmem(count):
    return [pl.BlockSpec(memory_space=pltpu.VMEM)] * count


def match_call(shared, matching, remote, previous):
    pairing, offsets, image, rims, table, places = shared
    height, breadth = image.shape[2] // 2, image.shape[3]
    finish = matching == MATCH - 1
    coherence = pltpu.VMEM((2, height, breadth), F32)
    filtered = pltpu.VMEM((2, 2, height, breadth), BF)
    inputs = [pairing, offsets, image, rims, remote, table]
    specs = [pl.BlockSpec(memory_space=pltpu.SMEM)] * 2 + vmem(4)
    out_shape, out_specs, scratch = (coherence, filtered), vmem(2), []
    if finish:
        inputs += previous
        specs += vmem(len(previous))
        out_shape = (
            jax.ShapeDtypeStruct((MATCH, 2, height, breadth), F32),
            jax.ShapeDtypeStruct((2, MATCH, 2, height, breadth), BF),
        )
        out_specs = [pl.BlockSpec(memory_space=pl.ANY)] * 2
        scratch = [coherence, filtered, pltpu.SemaphoreType.DMA((3 * matching + 6,))]
    return pl.pallas_call(
        functools.partial(match_kernel, matching, places, finish),
        out_shape=out_shape,
        in_specs=specs,
        out_specs=tuple(out_specs),
        scratch_shapes=scratch,
        cost_estimate=pl.CostEstimate(flops=2 * 10**9, bytes_accessed=3 * 10**6, transcendentals=0),
        compiler_params=GRANT,
        name=f"match{matching}",
    )(*inputs)


def xor_swap(value, mask):
    return lax.ppermute(value, "acq", [(i, i ^ mask) for i in range(lax.axis_size("acq"))])


def neighbour_swap(value, parity):
    places, groups = lax.axis_size("rng"), lax.axis_size("acq")
    pairs = []
    for group in range(groups):
        for place in range(places):
            other = place + 1 if place % 2 == parity else place - 1
            if 0 <= other < places:
                target = group * places + other
            else:
                target = (group ^ 1) * places + place
            pairs.append((group * places + place, target))
    return lax.ppermute(value, ("acq", "rng"), pairs)


def per_device(images, pairing, tile_offsets):
    lines, breadth = images.shape[2:]
    height = lines // 2
    table, places = all_tables(breadth, height)
    table = jnp.asarray(table)
    side = pltpu.VMEM((lines, 128), BF)
    payload = pltpu.VMEM((5, height, breadth), BF)
    offsets = tile_offsets.T
    image, first, second = pl.pallas_call(
        pack_kernel,
        out_shape=(pltpu.VMEM(images.shape, BF), side, side),
        in_specs=[pl.BlockSpec(memory_space=pl.ANY)],
        out_specs=tuple(vmem(3)),
        scratch_shapes=[pltpu.SemaphoreType.DMA],
        compiler_params=GRANT,
        name="pack",
    )(in_hbm(images))
    first = neighbour_swap(first, 0)
    second = neighbour_swap(second, 1)
    far, near, pairing, offsets, table = pl.pallas_call(
        main_kernel,
        out_shape=(
            payload,
            payload,
            pltpu.SMEM(pairing.shape, jnp.int32),
            pltpu.SMEM(offsets.shape, jnp.int32),
            pltpu.VMEM(table.shape, BF),
        ),
        in_specs=vmem(1) + [pl.BlockSpec(memory_space=pl.ANY)] * 3,
        out_specs=(*vmem(2), *[pl.BlockSpec(memory_space=pltpu.SMEM)] * 2, *vmem(1)),
        scratch_shapes=[pltpu.SemaphoreType.DMA] * 3,
        compiler_params=GRANT,
        name="mains",
    )(image, in_hbm(pairing), in_hbm(offsets), in_hbm(table))
    far, near, rims = pl.pallas_call(
        functools.partial(rim_kernel, lax.axis_size("rng") - 1),
        out_shape=(payload, payload, pltpu.VMEM((2, lines, 128), BF)),
        in_specs=vmem(4),
        out_specs=tuple(vmem(3)),
        input_output_aliases={2: 0, 3: 1},
        compiler_params=GRANT,
        name="rims",
    )(first, second, far, near)
    far = xor_swap(far, 2)
    near = xor_swap(near, 1)
    call = functools.partial(match_call, (pairing, offsets, image, rims, table, places))
    outputs = call(0, near, ())
    far, *outputs = lax.optimization_barrier((far, *outputs))
    both = xor_swap(far, 1)
    outputs = [*outputs, *call(1, far, ())]
    return tuple(call(2, both, outputs))


def solution(mesh):
    in_specs = (P(None, ("stack", "acq"), None, "rng"), P(), P())
    out_specs = (
        P(None, ("stack", "acq"), None, "rng"),
        P(None, None, ("stack", "acq"), None, "rng"),
    )
    return jax.shard_map(
        per_device, mesh=mesh, in_specs=in_specs, out_specs=out_specs, check_vma=False
    )
```

```python
import functools

import jax
import jax.numpy as jnp
import numpy as np
from jax import lax
from jax.experimental import pallas as pl
from jax.experimental.pallas import tpu as pltpu
from jax.sharding import PartitionSpec as P

MATCH = 3
REACH = 32
PATCH = 32
EPSILON = 1e-06
BF = jnp.bfloat16
F32 = jnp.float32
GRANT = pltpu.CompilerParams(vmem_limit_bytes=24 << 20)


def split_table(table):
    high = table.astype(np.float32).astype(BF)
    low = (table - high.astype(np.float64)).astype(np.float32).astype(BF)
    return high, low


def gauss(spread):
    width = REACH / 8.0
    weights = np.exp(-(spread.astype(np.float64) ** 2) / (2.0 * width * width))
    return np.where(np.abs(spread) <= REACH, weights, 0.0)


def range_table(breadth):
    lanes = breadth + 128
    row = np.arange(lanes)
    cell = np.where(row < breadth + REACH, row, row - lanes)
    band = gauss(cell[:, None] - np.arange(breadth)[None, :])
    valid = (row < breadth + REACH) | (row >= lanes - REACH)
    return split_table(band * valid[:, None])


def azimuth_table(height):
    line = np.arange(height)
    high, low = split_table(gauss(line[:, None] - line[None, :]))
    return np.concatenate([high, high, low], axis=1)


def waves(rows, cols):
    angle = 2.0 * np.pi / PATCH * ((rows[:, None] * cols[None, :]) % PATCH)
    return np.cos(angle), np.sin(angle)


def column_tables():
    lane = np.arange(128)
    same = (lane[:, None] // PATCH) == (lane[None, :] // PATCH)
    cosine, sine = waves(lane % PATCH, lane % PATCH)
    cosine, sine = cosine * same, sine * same
    forward = np.block([[cosine, -sine], [sine, cosine]])
    inverse = np.block([[cosine, sine], [-sine, cosine]]) / PATCH
    return split_table(forward), split_table(inverse), same.astype(np.float32).astype(BF)


def row_tables(height):
    patches = height // PATCH + 1
    freq = np.arange(patches * PATCH) % PATCH
    cosine, sine = waves(freq, np.arange(height))
    forward = np.block([[cosine, sine], [-sine, cosine]])
    fwd = split_table(forward)
    inv = split_table(forward.T / PATCH)
    return fwd, np.concatenate([inv[0], inv[0], inv[1]], axis=1)


def all_tables(breadth, height):
    forward, inverse, same = column_tables()
    row_forward, row_inverse = row_tables(height)
    parts = {}
    parts["band_high"], parts["band_low"] = range_table(breadth)
    parts["forward_high"], parts["forward_low"] = forward
    parts["inverse_high"], parts["inverse_low"] = inverse
    parts["row_high"], parts["row_low"] = row_forward
    parts["row_inverse"] = row_inverse
    parts["azimuth"] = azimuth_table(height)
    parts["same"] = same
    places, rows, start = {}, [], 0
    for name, part in parts.items():
        tall = -(-part.shape[0] // 16) * 16
        places[name] = []
        for first in range(0, part.shape[1], 256):
            piece = part[:, first : first + 256]
            block = np.zeros((tall, 256), BF)
            block[: piece.shape[0], : piece.shape[1]] = piece
            places[name].append((start, *piece.shape))
            rows.append(block)
            start += tall
    return np.concatenate(rows, axis=0), places


def halves(value):
    high = value.astype(BF)
    return high, (value - high.astype(F32)).astype(BF)


def mm(left, right):
    return jnp.dot(left, right, preferred_element_type=F32)


def lane_group(shape):
    return lax.broadcasted_iota(jnp.int32, shape, 1) >> 5


def even_place():
    return lax.axis_index("rng") % 2 == 0


def outgoing(mask, height):
    grouped = lax.axis_index("acq")
    upper = (grouped > jnp.bitwise_xor(grouped, mask)).astype(jnp.int32)
    return pl.multiple_of((1 - upper) * height, height)


def pack_kernel(source_ref, image_ref, first_ref, second_ref, far_ref, sem):
    copy = pltpu.make_async_copy(source_ref, image_ref, sem)
    copy.start()
    copy.wait()
    breadth = image_ref.shape[3]
    group = lane_group((image_ref.shape[2], 128))
    sides = []
    for first, order in (
        (breadth - 128, ((1, 1, 32), (0, 1, 64), (1, 0, 96), (0, 0, 0))),
        (0, ((0, 0, 0), (1, 1, 32), (0, 1, 64), (1, 0, 96))),
    ):
        value = None
        for position, (part, member, shift) in enumerate(order):
            cells = image_ref[part, member, :, first : first + 128].astype(F32)
            cells = pltpu.roll(cells, shift, 1) if shift else cells
            value = cells if value is None else jnp.where(group == position, cells, value)
        sides.append(value)
    tail, head = sides
    even = even_place()
    first_ref[...] = jnp.where(even, tail, head).astype(BF)
    second_ref[...] = jnp.where(even, head, tail).astype(BF)
    height = image_ref.shape[2] // 2
    fill(far_ref, image_ref, outgoing(2, height), height)


def fill(target, image_ref, start, height):
    for part in range(2):
        for member in range(2):
            target[2 * part + member] = image_ref[part, member, pl.ds(start, height), :]


def main_kernel(
    image_ref,
    pairing_source,
    offset_source,
    table_source,
    near_ref,
    pairing_ref,
    offset_ref,
    table_ref,
    pairing_sem,
    offset_sem,
    table_sem,
):
    copies = [
        pltpu.make_async_copy(table_source, table_ref, table_sem),
        pltpu.make_async_copy(pairing_source, pairing_ref, pairing_sem),
        pltpu.make_async_copy(offset_source, offset_ref, offset_sem),
    ]
    for copy in copies:
        copy.start()
    height = image_ref.shape[2] // 2
    fill(near_ref, image_ref, outgoing(1, height), height)
    for copy in copies:
        copy.wait()


def rim_kernel(ends, first_ref, second_ref, near_in, near_ref, far_ref, rim_ref):
    height = far_ref.shape[0]
    even = even_place()
    place = lax.axis_index("rng")
    first = first_ref[...].astype(F32)
    second = second_ref[...].astype(F32)
    head = jnp.where(place < ends, jnp.where(even, first, second), 0.0)
    tail = jnp.where(place > 0, jnp.where(even, second, first), 0.0)
    odd = (lane_group(tail.shape) & 1) == 1
    rim_ref[0] = jnp.where(odd, tail, head).astype(BF)
    rim_ref[1] = pltpu.roll(jnp.where(odd, head, tail), 32, 1).astype(BF)
    for target, mask in ((near_ref.at[4], 1), (far_ref, 2)):
        start = outgoing(mask, height)
        for part in range(2):
            target[:, 128 * part : 128 * part + 128] = rim_ref[part, pl.ds(start, height), :]


def match_kernel(
    matching,
    places,
    finish,
    pairing_ref,
    offset_ref,
    image_ref,
    rim_ref,
    table_ref,
    remote_ref,
    *rest,
):
    if matching:
        remote_rim_ref, *rest = rest
    else:
        remote_rim_ref = remote_ref.at[4]
    copies = []
    if finish:
        earlier, (coherence_out, filtered_out) = rest[: 2 * matching], rest[2 * matching :][:2]
        coherence_ref, filtered_ref, sems = rest[2 * matching + 2 :]

        def send(source, target):
            copy = pltpu.make_async_copy(source, target, sems.at[len(copies)])
            copy.start()
            copies.append(copy)

        for index in range(matching):
            send(earlier[2 * index], coherence_out.at[index])
            for part in range(2):
                send(earlier[2 * index + 1].at[part], filtered_out.at[part, index])
    else:
        coherence_ref, filtered_ref = rest
    height = image_ref.shape[2] // 2
    breadth = image_ref.shape[3]
    lanes = breadth + 128
    patches = height // PATCH + 1
    freqs = patches * PATCH
    blocks = breadth // 128
    grouped = lax.axis_index("acq")
    upper = (grouped > jnp.bitwise_xor(grouped, matching + 1)).astype(jnp.int32)
    start = pl.multiple_of(upper * height, height)
    row_offset = offset_ref[0, matching]
    col_offset = offset_ref[1, matching]

    def table(name):
        pieces = [table_ref[first : first + rows, :cols] for first, rows, cols in places[name]]
        return jnp.concatenate(pieces, axis=1) if len(pieces) > 1 else pieces[0]

    fields = []
    windows = []
    for member in range(2):
        partner = pairing_ref[matching, 2 * grouped + member] % 2
        ours, theirs = [], []
        for part in range(2):
            rim = rim_ref[part, pl.ds(start, height), :].astype(F32)
            if member:
                rim = pltpu.roll(rim, 64, 1)
            main = image_ref[part, member, pl.ds(start, height), :].astype(F32)
            ours.append(jnp.concatenate([main, rim], axis=1))
            rim = remote_rim_ref[:, 128 * part : 128 * part + 128].astype(F32)
            rim = pltpu.roll(rim, 64 * partner, 1)
            main = remote_ref[2 * part + partner].astype(F32)
            theirs.append(jnp.concatenate([main, rim], axis=1))
        inter_real = ours[0] * theirs[0] + ours[1] * theirs[1]
        inter_imag = ours[1] * theirs[0] - ours[0] * theirs[1]
        fields.append(
            [
                inter_real,
                inter_imag,
                ours[0] * ours[0] + ours[1] * ours[1],
                theirs[0] * theirs[0] + theirs[1] * theirs[1],
            ]
        )
        windows.append(
            [pltpu.roll(value, REACH - col_offset, 1) for value in (inter_real, inter_imag)]
        )
    first_lanes = lane_group((height, 128)) == 0
    shared = [
        jnp.where(
            first_lanes,
            windows[0][part][:, breadth:],
            pltpu.roll(windows[1][part][:, breadth:], 32, 1),
        )
        for part in range(2)
    ]

    def groups_of(member):
        found = [
            jnp.concatenate(
                [part[:, 128 * block : 128 * block + 128] for part in windows[member]], axis=1
            )
            for block in range(blocks)
        ]
        return found + ([jnp.concatenate(shared, axis=1)] if member == 0 else [])

    band_high, band_low = table("band_high"), table("band_low")
    forward_high, forward_low = table("forward_high"), table("forward_low")
    inverse_high, inverse_low = table("inverse_high"), table("inverse_low")
    azimuth = table("azimuth")

    ranged = []
    columns = []
    for member in range(2):
        high, low = halves(jnp.concatenate(fields[member], axis=0))
        ranged.append(mm(high, band_high) + mm(low, band_high) + mm(high, band_low))
        high, low = halves(jnp.concatenate(groups_of(member), axis=0))
        columns.append(mm(high, forward_high) + mm(low, forward_high) + mm(high, forward_low))

    line = lax.broadcasted_iota(jnp.int32, (PATCH, 2 * height), 1) & (height - 1)
    patch = (line + PATCH - row_offset) >> 5
    keep = jnp.concatenate(
        [jnp.where(patch == place, 1.0, 0.0).astype(BF) for place in range(patches)] * 2, axis=0
    )
    row_high = table("row_high") * keep
    row_low = table("row_low") * keep
    row_twice = jnp.concatenate([row_high, row_high], axis=1)
    line = lax.broadcasted_iota(jnp.int32, (2 * height, 6 * freqs), 0) & (height - 1)
    lane = lax.broadcasted_iota(jnp.int32, (8, 6 * freqs), 1)
    for step in (4, 2, 1):
        lane = jnp.where(lane >= step * freqs, lane - step * freqs, lane)
    keep = ((line + PATCH - row_offset) >> 5) == (lane >> 5)[:1]
    row_inverse = table("row_inverse") * jnp.where(keep, 1.0, 0.0).astype(BF)

    weighted = []
    same = table("same")
    for member in range(2):
        high, low = halves(ranged[member])
        smoothed = [
            mm(
                azimuth,
                jnp.concatenate(
                    [piece[field * height : field * height + height] for piece in (high, low, high)],
                    axis=0,
                ),
            )
            for field in range(4)
        ]
        coherence_ref[member] = (smoothed[0] * smoothed[0] + smoothed[1] * smoothed[1]) / (
            smoothed[2] * smoothed[3] + EPSILON
        )
        if finish:
            send(coherence_ref.at[member], coherence_out.at[matching, member])
        column = columns[member]
        count = column.shape[0] // height
        column = jnp.concatenate(
            [
                jnp.concatenate(
                    [column[height * group : height * group + height, 128 * part : 128 * part + 128] for part in range(2)],
                    axis=0,
                )
                for group in range(count)
            ],
            axis=1,
        )
        high, low = halves(column)
        freq = mm(row_twice, jnp.concatenate([high, low], axis=0)) + mm(row_low, high)
        freq_real, freq_imag = freq[:freqs], freq[freqs:]
        power = freq_real * freq_real + freq_imag * freq_imag + EPSILON
        magnitude = lax.rsqrt(lax.rsqrt(power))
        sums = jnp.concatenate(
            [
                jnp.sum(
                    magnitude[PATCH * place : PATCH * place + PATCH, 128 * group : 128 * group + 128],
                    axis=0,
                    keepdims=True,
                )
                for group in range(count)
                for place in range(patches)
            ],
            axis=0,
        )
        high, low = halves(sums)
        totals = mm(high, same) + mm(low, same)
        inverse = 1.0 / (totals * (1.0 / (PATCH * PATCH)) + EPSILON)
        scaling = jnp.concatenate(
            [
                jnp.concatenate(
                    [
                        magnitude[PATCH * place : PATCH * place + PATCH, 128 * group : 128 * group + 128]
                        * inverse[group * patches + place : group * patches + place + 1]
                        for place in range(patches)
                    ],
                    axis=0,
                )
                for group in range(count)
            ],
            axis=1,
        )
        weighted.append(jnp.concatenate([freq_real * scaling, freq_imag * scaling], axis=0))

    final = []
    for member in range(2):
        high, low = halves(weighted[member])
        back = mm(row_inverse, jnp.concatenate([high, low, high], axis=0))
        count = back.shape[1] // 128
        back = jnp.concatenate(
            [
                jnp.concatenate(
                    [back[height * part : height * part + height, 128 * group : 128 * group + 128] for part in range(2)],
                    axis=1,
                )
                for group in range(count)
            ],
            axis=0,
        )
        high, low = halves(back)
        final.append(mm(high, inverse_high) + mm(low, inverse_high) + mm(high, inverse_low))
    edge = final[0][blocks * height :]
    for member in range(2):
        for part in range(2):
            side = edge[:, 128 * part : 128 * part + 128]
            whole = jnp.concatenate(
                [
                    final[member][height * block : height * block + height, 128 * part : 128 * part + 128]
                    for block in range(blocks)
                ]
                + [pltpu.roll(side, 96, 1) if member else side],
                axis=1,
            )
            cells = pltpu.roll(whole, lanes - REACH + col_offset, 1)[:, :breadth]
            filtered_ref[part, member] = cells.astype(BF)
            if finish:
                send(filtered_ref.at[part, member], filtered_out.at[part, matching, member])
    for copy in copies:
        copy.wait()


def in_hbm(value):
    return pltpu.with_memory_space_constraint(value, pltpu.HBM)


def vmem(count):
    return [pl.BlockSpec(memory_space=pltpu.VMEM)] * count


def match_call(shared, matching, remote, previous):
    pairing, offsets, image, rims, table, places = shared
    height, breadth = image.shape[2] // 2, image.shape[3]
    finish = matching == MATCH - 1
    coherence = pltpu.VMEM((2, height, breadth), F32)
    filtered = pltpu.VMEM((2, 2, height, breadth), BF)
    inputs = [pairing, offsets, image, rims, table, *remote]
    specs = [pl.BlockSpec(memory_space=pltpu.SMEM)] * 2 + vmem(3 + len(remote))
    out_shape, out_specs, scratch = (coherence, filtered), vmem(2), []
    if finish:
        inputs += previous
        specs += vmem(len(previous))
        out_shape = (
            jax.ShapeDtypeStruct((MATCH, 2, height, breadth), F32),
            jax.ShapeDtypeStruct((2, MATCH, 2, height, breadth), BF),
        )
        out_specs = [pl.BlockSpec(memory_space=pl.ANY)] * 2
        scratch = [coherence, filtered, pltpu.SemaphoreType.DMA((3 * matching + 6,))]
    return pl.pallas_call(
        functools.partial(match_kernel, matching, places, finish),
        out_shape=out_shape,
        in_specs=specs,
        out_specs=tuple(out_specs),
        scratch_shapes=scratch,
        cost_estimate=pl.CostEstimate(flops=2 * 10**9, bytes_accessed=3 * 10**6, transcendentals=0),
        compiler_params=GRANT,
    )(*inputs)


def xor_swap(value, mask):
    return lax.ppermute(value, "acq", [(i, i ^ mask) for i in range(lax.axis_size("acq"))])


def neighbour_swap(value, parity):
    places, groups = lax.axis_size("rng"), lax.axis_size("acq")
    pairs = []
    for group in range(groups):
        for place in range(places):
            other = place + 1 if place % 2 == parity else place - 1
            if 0 <= other < places:
                target = group * places + other
            else:
                target = (group ^ 1) * places + place
            pairs.append((group * places + place, target))
    return lax.ppermute(value, ("acq", "rng"), pairs)


def per_device(images, pairing, tile_offsets):
    lines, breadth = images.shape[2:]
    height = lines // 2
    table, places = all_tables(breadth, height)
    table = jnp.asarray(table)
    side = pltpu.VMEM((lines, 128), BF)
    payload = pltpu.VMEM((5, height, breadth), BF)
    offsets = tile_offsets.T
    mains = pltpu.VMEM((4, height, breadth), BF)
    image, first, second, far = pl.pallas_call(
        pack_kernel,
        out_shape=(pltpu.VMEM(images.shape, BF), side, side, mains),
        in_specs=[pl.BlockSpec(memory_space=pl.ANY)],
        out_specs=tuple(vmem(4)),
        scratch_shapes=[pltpu.SemaphoreType.DMA],
        compiler_params=GRANT,
        name="pack",
    )(in_hbm(images))
    first = neighbour_swap(first, 0)
    second = neighbour_swap(second, 1)
    far = xor_swap(far, 2)
    near, pairing, offsets, table = pl.pallas_call(
        main_kernel,
        out_shape=(
            payload,
            pltpu.SMEM(pairing.shape, jnp.int32),
            pltpu.SMEM(offsets.shape, jnp.int32),
            pltpu.VMEM(table.shape, BF),
        ),
        in_specs=vmem(1) + [pl.BlockSpec(memory_space=pl.ANY)] * 3,
        out_specs=(*vmem(1), *[pl.BlockSpec(memory_space=pltpu.SMEM)] * 2, *vmem(1)),
        scratch_shapes=[pltpu.SemaphoreType.DMA] * 3,
        compiler_params=GRANT,
        name="mains",
    )(image, in_hbm(pairing), in_hbm(offsets), in_hbm(table))
    near, far_rims, rims = pl.pallas_call(
        functools.partial(rim_kernel, lax.axis_size("rng") - 1),
        out_shape=(
            payload,
            pltpu.VMEM((height, breadth), BF),
            pltpu.VMEM((2, lines, 128), BF),
        ),
        in_specs=vmem(3),
        out_specs=tuple(vmem(3)),
        input_output_aliases={2: 0},
        compiler_params=GRANT,
        name="rims",
    )(first, second, near)
    near = xor_swap(near, 1)
    far_rims = xor_swap(far_rims, 2)
    call = functools.partial(match_call, (pairing, offsets, image, rims, table, places))
    outputs = call(0, (near,), ())
    far, far_rims, *outputs = lax.optimization_barrier((far, far_rims, *outputs))
    both = xor_swap(far, 1)
    both_rims = xor_swap(far_rims, 1)
    outputs = [*outputs, *call(1, (far, far_rims), ())]
    return tuple(call(2, (both, both_rims), outputs))


def solution(mesh):
    in_specs = (P(None, ("stack", "acq"), None, "rng"), P(), P())
    out_specs = (
        P(None, ("stack", "acq"), None, "rng"),
        P(None, None, ("stack", "acq"), None, "rng"),
    )

    return jax.shard_map(
        per_device, mesh=mesh, in_specs=in_specs, out_specs=out_specs, check_vma=False
    )
```

```python
import functools

import jax
import jax.numpy as jnp
import numpy as np
from jax import lax
from jax.experimental import pallas as pl
from jax.experimental.pallas import tpu as pltpu
from jax.sharding import PartitionSpec as P

MATCH = 3
REACH = 32
PATCH = 32
EPSILON = 1e-06
BF = jnp.bfloat16
F32 = jnp.float32
GRANT = pltpu.CompilerParams(vmem_limit_bytes=24 << 20)


def split_table(table):
    high = table.astype(np.float32).astype(BF)
    low = (table - high.astype(np.float64)).astype(np.float32).astype(BF)
    return high, low


def gauss(spread):
    width = REACH / 8.0
    weights = np.exp(-(spread.astype(np.float64) ** 2) / (2.0 * width * width))
    return np.where(np.abs(spread) <= REACH, weights, 0.0)


def stacked(table, copies=1):
    high, low = split_table(table)
    return np.concatenate([high] * copies + [low], axis=0)


def range_table(breadth):
    lanes = breadth + 128
    row = np.arange(lanes)
    cell = np.where(row < breadth + REACH, row, row - lanes)
    band = gauss(cell[:, None] - np.arange(breadth)[None, :])
    valid = (row < breadth + REACH) | (row >= lanes - REACH)
    return stacked(band * valid[:, None])


def azimuth_table(height):
    line = np.arange(height)
    return stacked(gauss(line[:, None] - line[None, :]), 2).T


def waves(rows, cols):
    angle = 2.0 * np.pi / PATCH * ((rows[:, None] * cols[None, :]) % PATCH)
    return np.cos(angle), np.sin(angle)


def column_tables():
    lane = np.arange(128)
    same = (lane[:, None] // PATCH) == (lane[None, :] // PATCH)
    cosine, sine = waves(lane % PATCH, lane % PATCH)
    cosine, sine = cosine * same, sine * same
    forward = np.block([[cosine, -sine], [sine, cosine]])
    return stacked(forward), same.astype(np.float32).astype(BF)


def row_tables(height):
    patches = height // PATCH + 1
    freq = np.arange(patches * PATCH) % PATCH
    cosine, sine = waves(freq, np.arange(height))
    forward = np.block([[cosine, sine], [-sine, cosine]])
    return stacked(forward.T).T, stacked(forward / (PATCH * PATCH), 2).T


def all_tables(breadth, height):
    parts = {}
    parts["row_forward"], parts["row_inverse"] = row_tables(height)
    early = list(parts)
    parts["azimuth"], parts["band"] = azimuth_table(height), range_table(breadth)
    parts["forward"], parts["same"] = column_tables()
    places, rows, start = {}, [], 0
    for name, part in parts.items():
        tall = -(-part.shape[0] // 16) * 16
        places[name] = []
        for first in range(0, part.shape[1], 256):
            piece = part[:, first : first + 256]
            block = np.zeros((tall, 256), BF)
            block[: piece.shape[0], : piece.shape[1]] = piece
            places[name].append((start, *piece.shape))
            rows.append(block)
            start += tall
        if name == early[-1]:
            places["early"] = start
    return np.concatenate(rows, axis=0), places


def halves(value):
    high = value.astype(BF)
    return high, (value - high.astype(F32)).astype(BF)


def thirds(value, axis):
    high, low = halves(value)
    return jnp.concatenate([high, low, high], axis=axis)


def fold(table, axis):
    high, low = jnp.split(table, 2, axis=axis)
    return jnp.concatenate([high, high, low], axis=axis)


def mm(left, right):
    return jnp.dot(left, right, preferred_element_type=F32)


def lane_group(shape):
    return lax.broadcasted_iota(jnp.int32, shape, 1) >> 5


def even_place():
    return lax.axis_index("rng") % 2 == 0


def outgoing(mask, height):
    grouped = lax.axis_index("acq")
    upper = (grouped > jnp.bitwise_xor(grouped, mask)).astype(jnp.int32)
    return pl.multiple_of((1 - upper) * height, height)


def pack_kernel(source_ref, image_ref, first_ref, second_ref, far_ref, sem):
    copy = pltpu.make_async_copy(source_ref, image_ref, sem)
    copy.start()
    copy.wait()
    breadth = image_ref.shape[3]
    group = lane_group((image_ref.shape[2], 128))
    sides = []
    for first, order in (
        (breadth - 128, ((1, 1, 32), (0, 1, 64), (1, 0, 96), (0, 0, 0))),
        (0, ((0, 0, 0), (1, 1, 32), (0, 1, 64), (1, 0, 96))),
    ):
        value = None
        for position, (part, member, shift) in enumerate(order):
            cells = image_ref[part, member, :, first : first + 128].astype(F32)
            cells = pltpu.roll(cells, shift, 1) if shift else cells
            value = cells if value is None else jnp.where(group == position, cells, value)
        sides.append(value)
    tail, head = sides
    even = even_place()
    first_ref[...] = jnp.where(even, tail, head).astype(BF)
    second_ref[...] = jnp.where(even, head, tail).astype(BF)
    height = image_ref.shape[2] // 2
    fill(far_ref, image_ref, outgoing(2, height), height)


def fill(target, image_ref, start, height):
    for part in range(2):
        for member in range(2):
            target[2 * part + member] = image_ref[part, member, pl.ds(start, height), :]


def row_mask(height, row_offset, freq_dim, thrice):
    freqs = height + PATCH
    rows, cols = 2 * height, 2 * freqs
    if freq_dim == 0:
        line = lax.broadcasted_iota(jnp.int32, (PATCH, rows), 1) & (height - 1)
        patch = (line + PATCH - row_offset) >> 5
        keep = jnp.concatenate(
            [jnp.where(patch == place, 1.0, 0.0).astype(BF) for place in range(freqs // PATCH)] * 2,
            axis=0,
        )
        return jnp.concatenate([keep] * thrice, axis=1)
    line = lax.broadcasted_iota(jnp.int32, (rows, thrice * cols), 0) & (height - 1)
    lane = lax.broadcasted_iota(jnp.int32, (8, thrice * cols), 1)
    for step in (4, 2, 1):
        lane = jnp.where(lane >= step * freqs, lane - step * freqs, lane)
    keep = ((line + PATCH - row_offset) >> 5) == (lane >> 5)[:1]
    return jnp.where(keep, 1.0, 0.0).astype(BF)


def table_part(table_ref, pieces):
    pieces = [table_ref[first : first + rows, :cols] for first, rows, cols in pieces]
    return jnp.concatenate(pieces, axis=1) if len(pieces) > 1 else pieces[0]


def main_kernel(
    places,
    image_ref,
    pairing_source,
    offset_source,
    table_source,
    near_ref,
    pairing_ref,
    offset_ref,
    table_ref,
    forward_ref,
    inverse_ref,
    pairing_sem,
    offset_sem,
    early_sem,
    late_sem,
):
    early = places["early"]
    late = pl.ds(early, table_ref.shape[0] - early)
    copies = [
        pltpu.make_async_copy(offset_source, offset_ref, offset_sem),
        pltpu.make_async_copy(table_source.at[:early], table_ref.at[:early], early_sem),
        pltpu.make_async_copy(table_source.at[late], table_ref.at[late], late_sem),
        pltpu.make_async_copy(pairing_source, pairing_ref, pairing_sem),
    ]
    for copy in copies:
        copy.start()
    height = image_ref.shape[2] // 2
    fill(near_ref, image_ref, outgoing(1, height), height)
    for copy in copies[:2]:
        copy.wait()
    row_forward = table_part(table_ref, places["row_forward"])
    row_inverse = table_part(table_ref, places["row_inverse"])
    for matching in range(MATCH):
        row_offset = offset_ref[0, matching]
        forward_ref[matching] = row_forward * row_mask(height, row_offset, 0, 2)
        inverse_ref[matching] = row_inverse * row_mask(height, row_offset, 1, 3)
    for copy in copies[2:]:
        copy.wait()


def rim_kernel(ends, first_ref, second_ref, near_in, near_ref, far_ref, rim_ref):
    height = far_ref.shape[0]
    even = even_place()
    place = lax.axis_index("rng")
    first = first_ref[...].astype(F32)
    second = second_ref[...].astype(F32)
    head = jnp.where(place < ends, jnp.where(even, first, second), 0.0)
    tail = jnp.where(place > 0, jnp.where(even, second, first), 0.0)
    odd = (lane_group(tail.shape) & 1) == 1
    rim_ref[0] = jnp.where(odd, tail, head).astype(BF)
    rim_ref[1] = pltpu.roll(jnp.where(odd, head, tail), 32, 1).astype(BF)
    for target, mask in ((near_ref.at[4], 1), (far_ref, 2)):
        start = outgoing(mask, height)
        for part in range(2):
            target[:, 128 * part : 128 * part + 128] = rim_ref[part, pl.ds(start, height), :]


def half_of(matching, height):
    grouped = lax.axis_index("acq")
    upper = (grouped > jnp.bitwise_xor(grouped, matching + 1)).astype(jnp.int32)
    return pl.multiple_of(upper * height, height)


def own_cells(image_ref, rim_ref, part, member, start, height):
    rim = rim_ref[part, pl.ds(start, height), :].astype(F32)
    if member:
        rim = pltpu.roll(rim, 64, 1)
    main = image_ref[part, member, pl.ds(start, height), :].astype(F32)
    return jnp.concatenate([main, rim], axis=1)


def along_lines(azimuth, ranged, index, height):
    return mm(azimuth, thirds(ranged[index * height : index * height + height], 0))


def power_kernel(places, image_ref, rim_ref, table_ref, power_ref):
    height = image_ref.shape[2] // 2
    fields = []
    for matching in range(2):
        for member in range(2):
            real, imag = [
                own_cells(image_ref, rim_ref, part, member, half_of(matching, height), height)
                for part in range(2)
            ]
            fields.append(real * real + imag * imag)
    azimuth = table_part(table_ref, places["azimuth"])
    for matching in range(2):
        pair = jnp.concatenate(fields[2 * matching : 2 * matching + 2], axis=0)
        ranged = mm(thirds(pair, 1), fold(table_part(table_ref, places["band"]), 0))
        for member in range(2):
            power_ref[matching, member] = along_lines(azimuth, ranged, member, height)


JC, JR, JI = True, True, False
ORDER = (
    "F0", "F1", "R1", "C0", "C1", "R0", "Z0", "A1", "S0", "Z1",
    "S1", "B0", "B1", "M0", "M1", "A0", "I0", "I1", "O1", "O0",
)


def match_kernel(
    matching,
    places,
    finish,
    pairing_ref,
    offset_ref,
    image_ref,
    rim_ref,
    table_ref,
    forward_ref,
    inverse_ref,
    power_ref,
    remote_ref,
    *rest,
):
    if matching:
        remote_rim_ref, *rest = rest
    else:
        remote_rim_ref = remote_ref.at[4]
    copies = []

    def send(source, target):
        copy = pltpu.make_async_copy(source, target, sems.at[len(copies)])
        copy.start()
        copies.append(copy)

    if finish:
        earlier, (coherence_out, filtered_out) = rest[: 2 * matching], rest[2 * matching :][:2]
        coherence_ref, filtered_ref, sems = rest[2 * matching + 2 :]
        for index in range(matching):
            send(earlier[2 * index], coherence_out.at[index])
            for part in range(2):
                send(earlier[2 * index + 1].at[part], filtered_out.at[part, index])
    else:
        coherence_ref, filtered_ref = rest
    height = image_ref.shape[2] // 2
    breadth = image_ref.shape[3]
    patches = height // PATCH + 1
    freqs = patches * PATCH
    blocks = breadth // 128
    grouped = lax.axis_index("acq")
    start = half_of(matching, height)
    shift = REACH - offset_ref[1, matching]
    lane = lax.broadcasted_iota(jnp.int32, (height, 128), 1)
    state = {}

    def block(value, index):
        return value[:, 128 * index : 128 * index + 128]

    def fields(member):
        partner = pairing_ref[matching, 2 * grouped + member] % 2
        ours, theirs = [], []
        for part in range(2):
            ours.append(own_cells(image_ref, rim_ref, part, member, start, height))
            rim = block(remote_rim_ref[...], part).astype(F32)
            rim = pltpu.roll(rim, 64 * partner, 1)
            main = remote_ref[2 * part + partner].astype(F32)
            theirs.append(jnp.concatenate([main, rim], axis=1))
        inter_real = ours[0] * theirs[0] + ours[1] * theirs[1]
        inter_imag = ours[1] * theirs[0] - ours[0] * theirs[1]
        power = theirs[0] * theirs[0] + theirs[1] * theirs[1]
        state["fields", member] = [inter_real, inter_imag, power]
        windows = []
        for value in (inter_real, inter_imag):
            turned = [pltpu.roll(block(value, index), shift, 1) for index in range(blocks + 1)]
            windows.append(
                [jnp.where(lane < shift, turned[index - 1], turned[index]) for index in range(blocks + 1)]
            )
        state["window", member] = windows

    def joint(stage, together, member):
        if not together:
            return [(member,)]
        return [(0, 1)] if ("ready " + stage, 1 - member) in state else []

    def columns(member):
        windows = state["window", member]
        groups = [
            jnp.concatenate([part[index] for part in windows], axis=1) for index in range(blocks)
        ]
        if member == 0:
            other = state["window", 1]
            groups.append(
                jnp.concatenate(
                    [
                        jnp.where(
                            lane < PATCH, windows[part][blocks], pltpu.roll(other[part][blocks], PATCH, 1)
                        )
                        for part in range(2)
                    ],
                    axis=1,
                )
            )
        state["ready column", member] = groups
        for members in joint("column", JC, member):
            values = sum((state["ready column", one] for one in members), [])
            found = mm(
                thirds(jnp.concatenate(values, axis=0), 1),
                fold(table_part(table_ref, places["forward"]), 0),
            )
            for one in members:
                count = len(state["ready column", one])
                state["column", one] = jnp.concatenate(
                    [
                        jnp.concatenate(
                            [
                                block(found[height * group : height * group + height], part)
                                for part in range(2)
                            ],
                            axis=0,
                        )
                        for group in range(count)
                    ],
                    axis=1,
                )
                found = found[count * height :]

    def ranges(member):
        state["ready range", member] = state["fields", member]
        for members in joint("range", JR, member):
            values = sum((state["fields", one] for one in members), [])
            found = mm(
                thirds(jnp.concatenate(values, axis=0), 1),
                fold(table_part(table_ref, places["band"]), 0),
            )
            for one in members:
                state["range", one], found = found[: 3 * height], found[3 * height :]

    def coherence(member):
        azimuth = table_part(table_ref, places["azimuth"])
        real, imag, power = [
            along_lines(azimuth, state["range", member], index, height) for index in range(3)
        ]
        own = power_ref[min(matching, 1), member]
        coherence_ref[member] = (real * real + imag * imag) / (own * power + EPSILON)
        if finish:
            send(coherence_ref.at[member], coherence_out.at[matching, member])

    def rows(member):
        state["freq", member] = mm(fold(forward_ref[matching], 1), thirds(state["column", member], 0))

    def scaled(member):
        freq = state["freq", member]
        freq_real, freq_imag = freq[:freqs], freq[freqs:]
        power = freq_real * freq_real + freq_imag * freq_imag + EPSILON
        magnitude = lax.rsqrt(lax.rsqrt(power))

        state["magnitude", member] = magnitude
        state["weighted", member] = jnp.concatenate(
            [freq_real * magnitude, freq_imag * magnitude], axis=0
        )

    def means(member):
        magnitude = state["magnitude", member]
        count = magnitude.shape[1] // 128
        sums = [
            jnp.sum(block(magnitude[PATCH * place : PATCH * place + PATCH], group), axis=0, keepdims=True)
            for group in range(count)
            for place in range(patches)
        ]
        high, low = halves(jnp.concatenate(sums, axis=0))
        same = table_part(table_ref, places["same"])
        totals = mm(high, same) + mm(low, same)
        inverse = 1.0 / (totals * (1.0 / (PATCH * PATCH)) + EPSILON)
        line = lax.broadcasted_iota(jnp.int32, (height, 128), 0)
        patch = (line + PATCH - offset_ref[0, matching]) >> 5
        scales = []
        for group in range(count):
            scale = inverse[group * patches][None]
            for place in range(1, patches):
                scale = jnp.where(patch == place, inverse[group * patches + place][None], scale)
            scales.append(scale)
        state["scale", member] = scales

    def backs(member):
        back = mm(inverse_ref[matching], thirds(state["weighted", member], 0))
        state["back", member] = [
            jnp.concatenate(
                [block(back[height * part : height * part + height], group) for part in (1, 0)], axis=1
            )
            for group in range(back.shape[1] // 128)
        ]

    def inverses(member):
        state["ready final", member] = state["back", member]
        for members in joint("final", JI, member):
            values = sum((state["back", one] for one in members), [])
            found = mm(
                thirds(jnp.concatenate(values, axis=0), 1),
                fold(table_part(table_ref, places["forward"]), 0),
            )
            for one in members:
                count = len(state["back", one])
                state["final", one] = [
                    found[height * group : height * group + height] for group in range(count)
                ]
                found = found[count * height :]

    def outputs(member):
        edge = state["final", 0][blocks]
        edge_scale = state["scale", 0][blocks]
        for part in range(2):
            whole = [
                block(group, 1 - part) * scale
                for group, scale in zip(state["final", member][:blocks], state["scale", member])
            ]
            side = block(edge, 1 - part) * edge_scale
            turned = [pltpu.roll(value, 128 - shift, 1) for value in whole]
            turned.append(pltpu.roll(side, (128 - PATCH if member else 128) - shift, 1))
            cells = [
                jnp.where(lane < 128 - shift, turned[index], turned[index + 1])
                for index in range(blocks)
            ]
            filtered_ref[part, member] = jnp.concatenate(cells, axis=1).astype(BF)
            if finish:
                send(filtered_ref.at[part, member], filtered_out.at[part, matching, member])

    stages = dict(
        F=fields, C=columns, R=ranges, A=coherence, Z=rows, S=scaled, M=means, B=backs, I=inverses, O=outputs
    )
    for step in ORDER:
        stages[step[0]](int(step[1]))
    for copy in copies:
        copy.wait()


def in_hbm(value):
    return pltpu.with_memory_space_constraint(value, pltpu.HBM)


def vmem(count):
    return [pl.BlockSpec(memory_space=pltpu.VMEM)] * count


def match_call(shared, matching, remote, previous):
    pairing, offsets, image, rims, table, forward, inverse, power, places = shared
    height, breadth = image.shape[2] // 2, image.shape[3]
    finish = matching == MATCH - 1
    coherence = pltpu.VMEM((2, height, breadth), F32)
    filtered = pltpu.VMEM((2, 2, height, breadth), BF)
    inputs = [pairing, offsets, image, rims, table, forward, inverse, power, *remote]
    specs = [pl.BlockSpec(memory_space=pltpu.SMEM)] * 2 + vmem(6 + len(remote))
    out_shape, out_specs, scratch = (coherence, filtered), vmem(2), []
    if finish:
        inputs += previous
        specs += vmem(len(previous))
        out_shape = (
            jax.ShapeDtypeStruct((MATCH, 2, height, breadth), F32),
            jax.ShapeDtypeStruct((2, MATCH, 2, height, breadth), BF),
        )
        out_specs = [pl.BlockSpec(memory_space=pl.ANY)] * 2
        scratch = [coherence, filtered, pltpu.SemaphoreType.DMA((3 * matching + 6,))]
    return pl.pallas_call(
        functools.partial(match_kernel, matching, places, finish),
        out_shape=out_shape,
        in_specs=specs,
        out_specs=tuple(out_specs),
        scratch_shapes=scratch,
        cost_estimate=pl.CostEstimate(flops=2 * 10**9, bytes_accessed=3 * 10**6, transcendentals=0),
        compiler_params=GRANT,
    )(*inputs)


def xor_swap(value, mask):
    return lax.ppermute(value, "acq", [(i, i ^ mask) for i in range(lax.axis_size("acq"))])


def neighbour_swap(value, parity):
    places, groups = lax.axis_size("rng"), lax.axis_size("acq")
    pairs = []
    for group in range(groups):
        for place in range(places):
            other = place + 1 if place % 2 == parity else place - 1
            if 0 <= other < places:
                target = group * places + other
            else:
                target = (group ^ 1) * places + place
            pairs.append((group * places + place, target))
    return lax.ppermute(value, ("acq", "rng"), pairs)


def per_device(images, pairing, tile_offsets):
    lines, breadth = images.shape[2:]
    height = lines // 2
    table, places = all_tables(breadth, height)
    table = jnp.asarray(table)
    side = pltpu.VMEM((lines, 128), BF)
    payload = pltpu.VMEM((5, height, breadth), BF)
    offsets = tile_offsets.T
    mains = pltpu.VMEM((4, height, breadth), BF)
    image, first, second, far = pl.pallas_call(
        pack_kernel,
        out_shape=(pltpu.VMEM(images.shape, BF), side, side, mains),
        in_specs=[pl.BlockSpec(memory_space=pl.ANY)],
        out_specs=tuple(vmem(4)),
        scratch_shapes=[pltpu.SemaphoreType.DMA],
        compiler_params=GRANT,
        name="pack",
    )(in_hbm(images))
    first = neighbour_swap(first, 0)
    second = neighbour_swap(second, 1)
    far = xor_swap(far, 2)
    freqs = height + PATCH
    near, pairing, offsets, table, forward, inverse = pl.pallas_call(
        functools.partial(main_kernel, places),
        out_shape=(
            payload,
            pltpu.SMEM(pairing.shape, jnp.int32),
            pltpu.SMEM(offsets.shape, jnp.int32),
            pltpu.VMEM(table.shape, BF),
            pltpu.VMEM((MATCH, 2 * freqs, 4 * height), BF),
            pltpu.VMEM((MATCH, 2 * height, 6 * freqs), BF),
        ),
        in_specs=vmem(1) + [pl.BlockSpec(memory_space=pl.ANY)] * 3,
        out_specs=(*vmem(1), *[pl.BlockSpec(memory_space=pltpu.SMEM)] * 2, *vmem(3)),
        scratch_shapes=[pltpu.SemaphoreType.DMA] * 4,
        compiler_params=GRANT,
        name="mains",
    )(image, in_hbm(pairing), in_hbm(offsets), in_hbm(table))
    near, far_rims, rims = pl.pallas_call(
        functools.partial(rim_kernel, lax.axis_size("rng") - 1),
        out_shape=(
            payload,
            pltpu.VMEM((height, breadth), BF),
            pltpu.VMEM((2, lines, 128), BF),
        ),
        in_specs=vmem(3),
        out_specs=tuple(vmem(3)),
        input_output_aliases={2: 0},
        compiler_params=GRANT,
        name="rims",
    )(first, second, near)
    near = xor_swap(near, 1)
    far_rims = xor_swap(far_rims, 2)
    power = pl.pallas_call(
        functools.partial(power_kernel, places),
        out_shape=pltpu.VMEM((2, 2, height, breadth), F32),
        in_specs=vmem(3),
        out_specs=vmem(1)[0],
        cost_estimate=pl.CostEstimate(flops=10**9, bytes_accessed=10**6, transcendentals=0),
        compiler_params=GRANT,
        name="power",
    )(image, rims, table)
    call = functools.partial(
        match_call, (pairing, offsets, image, rims, table, forward, inverse, power, places)
    )
    outputs = call(0, (near,), ())
    far, far_rims, *outputs = lax.optimization_barrier((far, far_rims, *outputs))
    both = xor_swap(far, 1)
    both_rims = xor_swap(far_rims, 1)
    outputs = [*outputs, *call(1, (far, far_rims), ())]
    return tuple(call(2, (both, both_rims), outputs))


def solution(mesh):
    in_specs = (P(None, ("stack", "acq"), None, "rng"), P(), P())
    out_specs = (
        P(None, ("stack", "acq"), None, "rng"),
        P(None, None, ("stack", "acq"), None, "rng"),
    )

    return jax.shard_map(
        per_device, mesh=mesh, in_specs=in_specs, out_specs=out_specs, check_vma=False
    )
```

```python
import functools

import jax
import jax.numpy as jnp
import numpy as np
from jax import lax
from jax.experimental import pallas as pl
from jax.experimental.pallas import tpu as pltpu
from jax.sharding import PartitionSpec as P

MATCH = 3
REACH = 32
PATCH = 32
EPSILON = 1e-06
BF = jnp.bfloat16
F32 = jnp.float32
GRANT = pltpu.CompilerParams(vmem_limit_bytes=24 << 20)


def split_table(table):
    high = table.astype(np.float32).astype(BF)
    low = (table - high.astype(np.float64)).astype(np.float32).astype(BF)
    return high, low


def gauss(spread):
    width = REACH / 8.0
    weights = np.exp(-(spread.astype(np.float64) ** 2) / (2.0 * width * width))
    return np.where(np.abs(spread) <= REACH, weights, 0.0)


def stacked(table, copies=1):
    high, low = split_table(table)
    return np.concatenate([high] * copies + [low], axis=0)


def range_table(breadth):
    lanes = breadth + 128
    row = np.arange(lanes)
    cell = np.where(row < breadth + REACH, row, row - lanes)
    band = gauss(cell[:, None] - np.arange(breadth)[None, :])
    valid = (row < breadth + REACH) | (row >= lanes - REACH)
    return stacked(band * valid[:, None])


def azimuth_table(height):
    line = np.arange(height)
    return stacked(gauss(line[:, None] - line[None, :]), 2).T


def waves(rows, cols):
    angle = 2.0 * np.pi / PATCH * ((rows[:, None] * cols[None, :]) % PATCH)
    return np.cos(angle), np.sin(angle)


def column_tables():
    lane = np.arange(128)
    same = (lane[:, None] // PATCH) == (lane[None, :] // PATCH)
    cosine, sine = waves(lane % PATCH, lane % PATCH)
    cosine, sine = cosine * same, sine * same
    forward = np.block([[cosine, -sine], [sine, cosine]])
    return stacked(forward), same.astype(np.float32).astype(BF)


def row_tables(height):
    patches = height // PATCH + 1
    freq = np.arange(patches * PATCH) % PATCH
    cosine, sine = waves(freq, np.arange(height))
    forward = np.block([[cosine, sine], [-sine, cosine]])
    return stacked(forward.T).T, stacked(forward / (PATCH * PATCH), 2).T


def laid_out(parts):
    places, rows, start = {}, [], 0
    for name, part in parts.items():
        tall = -(-part.shape[0] // 16) * 16
        places[name] = []
        for first in range(0, part.shape[1], 256):
            piece = part[:, first : first + 256]
            block = np.zeros((tall, 256), BF)
            block[: piece.shape[0], : piece.shape[1]] = piece
            places[name].append((start, *piece.shape))
            rows.append(block)
            start += tall
    return np.concatenate(rows, axis=0), places


def all_tables(breadth, height):
    parts = {"band": range_table(breadth), "azimuth": azimuth_table(height)}
    parts["forward"], parts["same"] = column_tables()
    return laid_out(parts)


def line_tables(height):
    forward, inverse = row_tables(height)
    return laid_out({"row_forward": forward, "row_inverse": inverse})


def halves(value):
    high = value.astype(BF)
    return high, (value - high.astype(F32)).astype(BF)


def thirds(value, axis):
    high, low = halves(value)
    return jnp.concatenate([high, low, high], axis=axis)


def fold(table, axis):
    high, low = jnp.split(table, 2, axis=axis)
    return jnp.concatenate([high, high, low], axis=axis)


def mm(left, right):
    return jnp.dot(left, right, preferred_element_type=F32)


def lane_group(shape):
    return lax.broadcasted_iota(jnp.int32, shape, 1) >> 5


def even_place():
    return lax.axis_index("rng") % 2 == 0


def outgoing(mask, height):
    grouped = lax.axis_index("acq")
    upper = (grouped > jnp.bitwise_xor(grouped, mask)).astype(jnp.int32)
    return pl.multiple_of((1 - upper) * height, height)


def pack_kernel(source_ref, image_ref, first_ref, second_ref, far_ref, sem):
    copy = pltpu.make_async_copy(source_ref, image_ref, sem)
    copy.start()
    copy.wait()
    breadth = image_ref.shape[3]
    group = lane_group((image_ref.shape[2], 128))
    sides = []
    for first, order in (
        (breadth - 128, ((1, 1, 32), (0, 1, 64), (1, 0, 96), (0, 0, 0))),
        (0, ((0, 0, 0), (1, 1, 32), (0, 1, 64), (1, 0, 96))),
    ):
        value = None
        for position, (part, member, shift) in enumerate(order):
            cells = image_ref[part, member, :, first : first + 128].astype(F32)
            cells = pltpu.roll(cells, shift, 1) if shift else cells
            value = cells if value is None else jnp.where(group == position, cells, value)
        sides.append(value)
    tail, head = sides
    even = even_place()
    first_ref[...] = jnp.where(even, tail, head).astype(BF)
    second_ref[...] = jnp.where(even, head, tail).astype(BF)
    height = image_ref.shape[2] // 2
    fill(far_ref, image_ref, outgoing(2, height), height)


def fill(target, image_ref, start, height):
    for part in range(2):
        for member in range(2):
            target[2 * part + member] = image_ref[part, member, pl.ds(start, height), :]


def row_mask(height, row_offset, freq_dim, thrice):
    freqs = height + PATCH
    rows, cols = 2 * height, 2 * freqs
    if freq_dim == 0:
        line = lax.broadcasted_iota(jnp.int32, (PATCH, rows), 1) & (height - 1)
        patch = (line + PATCH - row_offset) >> 5
        keep = jnp.concatenate(
            [jnp.where(patch == place, 1.0, 0.0).astype(BF) for place in range(freqs // PATCH)] * 2,
            axis=0,
        )
        return jnp.concatenate([keep] * thrice, axis=1)
    line = lax.broadcasted_iota(jnp.int32, (rows, thrice * cols), 0) & (height - 1)
    lane = lax.broadcasted_iota(jnp.int32, (8, thrice * cols), 1)
    for step in (4, 2, 1):
        lane = jnp.where(lane >= step * freqs, lane - step * freqs, lane)
    keep = ((line + PATCH - row_offset) >> 5) == (lane >> 5)[:1]
    return jnp.where(keep, 1.0, 0.0).astype(BF)


def table_part(table_ref, pieces):
    pieces = [table_ref[first : first + rows, :cols] for first, rows, cols in pieces]
    return jnp.concatenate(pieces, axis=1) if len(pieces) > 1 else pieces[0]


def main_kernel(
    places,
    image_ref,
    pairing_source,
    offset_source,
    row_ref,
    near_ref,
    forward_ref,
    inverse_ref,
    pairing_ref,
    offset_ref,
    sem,
):
    copies = [
        pltpu.make_async_copy(pairing_source, pairing_ref, sem.at[0]),
        pltpu.make_async_copy(offset_source, offset_ref, sem.at[1]),
    ]
    for copy in copies:
        copy.start()
    height = image_ref.shape[2] // 2
    fill(near_ref, image_ref, outgoing(1, height), height)
    for copy in copies:
        copy.wait()
    row_forward = table_part(row_ref, places["row_forward"])
    row_inverse = table_part(row_ref, places["row_inverse"])
    for matching in range(MATCH):
        row_offset = offset_ref[0, matching]
        forward_ref[matching] = row_forward * row_mask(height, row_offset, 0, 2)
        inverse_ref[matching] = row_inverse * row_mask(height, row_offset, 1, 3)


def rim_kernel(ends, first_ref, second_ref, near_in, near_ref, far_ref, rim_ref):
    height = far_ref.shape[0]
    even = even_place()
    place = lax.axis_index("rng")
    first = first_ref[...].astype(F32)
    second = second_ref[...].astype(F32)
    head = jnp.where(place < ends, jnp.where(even, first, second), 0.0)
    tail = jnp.where(place > 0, jnp.where(even, second, first), 0.0)
    odd = (lane_group(tail.shape) & 1) == 1
    rim_ref[0] = jnp.where(odd, tail, head).astype(BF)
    rim_ref[1] = pltpu.roll(jnp.where(odd, head, tail), 32, 1).astype(BF)
    for target, mask in ((near_ref.at[4], 1), (far_ref, 2)):
        start = outgoing(mask, height)
        for part in range(2):
            target[:, 128 * part : 128 * part + 128] = rim_ref[part, pl.ds(start, height), :]


def half_of(matching, height):
    grouped = lax.axis_index("acq")
    upper = (grouped > jnp.bitwise_xor(grouped, matching + 1)).astype(jnp.int32)
    return pl.multiple_of(upper * height, height)


def own_cells(image_ref, rim_ref, part, member, start, height):
    rim = rim_ref[part, pl.ds(start, height), :].astype(F32)
    if member:
        rim = pltpu.roll(rim, 64, 1)
    main = image_ref[part, member, pl.ds(start, height), :].astype(F32)
    return jnp.concatenate([main, rim], axis=1)


def along_lines(azimuth, ranged, index, height):
    return mm(azimuth, thirds(ranged[index * height : index * height + height], 0))


def power_kernel(places, image_ref, rim_ref, table_ref, power_ref):
    height = image_ref.shape[2] // 2
    fields = []
    for matching in range(2):
        for member in range(2):
            real, imag = [
                own_cells(image_ref, rim_ref, part, member, half_of(matching, height), height)
                for part in range(2)
            ]
            fields.append(real * real + imag * imag)
    azimuth = table_part(table_ref, places["azimuth"])
    ranged = [
        mm(
            thirds(jnp.concatenate(fields[first : first + 2], axis=0), 1),
            fold(table_part(table_ref, places["band"]), 0),
        )
        for first in (0, 2)
    ]
    for index in range(2):
        for matching in range(2):
            power_ref[matching, index] = along_lines(azimuth, ranged[matching], index, height)


COST = 4 * 10**9
JC, JR, JI = True, True, False
ORDER = (
    "F0", "F1", "R1", "C0", "C1", "R0", "Z0", "A1", "S0", "Z1",
    "S1", "B0", "B1", "M1", "M0", "A0", "I0", "I1", "O1", "O0",
)


def match_kernel(
    matching,
    places,
    finish,
    pairing_ref,
    offset_ref,
    image_ref,
    rim_ref,
    table_ref,
    forward_ref,
    inverse_ref,
    power_ref,
    remote_ref,
    *rest,
):
    if matching:
        remote_rim_ref, *rest = rest
    else:
        remote_rim_ref = remote_ref.at[4]
    copies = []

    def send(source, target):
        copy = pltpu.make_async_copy(source, target, sems.at[len(copies)])
        copy.start()
        copies.append(copy)

    if finish:
        earlier, (coherence_out, filtered_out) = rest[: 2 * matching], rest[2 * matching :][:2]
        coherence_ref, filtered_ref, sems = rest[2 * matching + 2 :]
        for index in range(matching):
            send(earlier[2 * index], coherence_out.at[index])
            for part in range(2):
                send(earlier[2 * index + 1].at[part], filtered_out.at[part, index])
    else:
        coherence_ref, filtered_ref = rest
    height = image_ref.shape[2] // 2
    breadth = image_ref.shape[3]
    patches = height // PATCH + 1
    freqs = patches * PATCH
    blocks = breadth // 128
    grouped = lax.axis_index("acq")
    start = half_of(matching, height)
    shift = REACH - offset_ref[1, matching]
    lane = lax.broadcasted_iota(jnp.int32, (height, 128), 1)
    state = {}

    def block(value, index):
        return value[:, 128 * index : 128 * index + 128]

    def fields(member):
        partner = pairing_ref[matching, 2 * grouped + member] % 2
        ours, theirs = [], []
        for part in range(2):
            ours.append(own_cells(image_ref, rim_ref, part, member, start, height))
            if ("rims", part) not in state:
                rim = block(remote_rim_ref[...], part).astype(F32)
                state["rims", part] = rim, pltpu.roll(rim, 64, 1)
            rim = jnp.where(partner == 1, *state["rims", part][::-1])
            main = remote_ref[2 * part + partner].astype(F32)
            theirs.append(jnp.concatenate([main, rim], axis=1))
        inter_real = ours[0] * theirs[0] + ours[1] * theirs[1]
        inter_imag = ours[1] * theirs[0] - ours[0] * theirs[1]
        power = theirs[0] * theirs[0] + theirs[1] * theirs[1]
        state["fields", member] = [inter_real, inter_imag, power]
        windows = []
        for value in (inter_real, inter_imag):
            turned = [pltpu.roll(block(value, index), shift, 1) for index in range(blocks + 1)]
            windows.append(
                [jnp.where(lane < shift, turned[index - 1], turned[index]) for index in range(blocks + 1)]
            )
        state["window", member] = windows

    def joint(stage, together, member):
        if not together:
            return [(member,)]
        return [(0, 1)] if ("ready " + stage, 1 - member) in state else []

    def columns(member):
        windows = state["window", member]
        groups = [
            jnp.concatenate([part[index] for part in windows], axis=1) for index in range(blocks)
        ]
        if member == 0:
            other = state["window", 1]
            groups.append(
                jnp.concatenate(
                    [
                        jnp.where(
                            lane < PATCH, windows[part][blocks], pltpu.roll(other[part][blocks], PATCH, 1)
                        )
                        for part in range(2)
                    ],
                    axis=1,
                )
            )
        state["ready column", member] = groups
        for members in joint("column", JC, member):
            values = sum((state["ready column", one] for one in members), [])
            found = mm(
                thirds(jnp.concatenate(values, axis=0), 1),
                fold(table_part(table_ref, places["forward"]), 0),
            )
            for one in members:
                count = len(state["ready column", one])
                state["column", one] = jnp.concatenate(
                    [
                        jnp.concatenate(
                            [
                                block(found[height * group : height * group + height], part)
                                for part in range(2)
                            ],
                            axis=0,
                        )
                        for group in range(count)
                    ],
                    axis=1,
                )
                found = found[count * height :]

    def ranges(member):
        state["ready range", member] = state["fields", member]
        for members in joint("range", JR, member):
            values = sum((state["fields", one] for one in members), [])
            found = mm(
                thirds(jnp.concatenate(values, axis=0), 1),
                fold(table_part(table_ref, places["band"]), 0),
            )
            for one in members:
                state["range", one], found = found[: 3 * height], found[3 * height :]

    def coherence(member):
        azimuth = table_part(table_ref, places["azimuth"])
        real, imag, power = [
            along_lines(azimuth, state["range", member], index, height) for index in range(3)
        ]
        own = power_ref[min(matching, 1), member]
        coherence_ref[member] = (real * real + imag * imag) / (own * power + EPSILON)
        if finish:
            send(coherence_ref.at[member], coherence_out.at[matching, member])

    def rows(member):
        state["freq", member] = mm(fold(forward_ref[matching], 1), thirds(state["column", member], 0))

    def scaled(member):
        freq = state["freq", member]
        freq_real, freq_imag = freq[:freqs], freq[freqs:]
        power = freq_real * freq_real + freq_imag * freq_imag + EPSILON
        magnitude = lax.rsqrt(lax.rsqrt(power))

        state["magnitude", member] = magnitude
        state["weighted", member] = jnp.concatenate(
            [freq_real * magnitude, freq_imag * magnitude], axis=0
        )

    def means(member):
        magnitude = state["magnitude", member]
        count = magnitude.shape[1] // 128
        sums = [
            jnp.sum(block(magnitude[PATCH * place : PATCH * place + PATCH], group), axis=0, keepdims=True)
            for group in range(count)
            for place in range(patches)
        ]
        high, low = halves(jnp.concatenate(sums, axis=0))
        same = table_part(table_ref, places["same"])
        totals = mm(high, same) + mm(low, same)
        inverse = 1.0 / (totals * (1.0 / (PATCH * PATCH)) + EPSILON)
        line = lax.broadcasted_iota(jnp.int32, (height, 128), 0)
        patch = (line + PATCH - offset_ref[0, matching]) >> 5
        scales = []
        for group in range(count):
            scale = inverse[group * patches][None]
            for place in range(1, patches):
                scale = jnp.where(patch == place, inverse[group * patches + place][None], scale)
            scales.append(scale)
        state["scale", member] = scales

    def backs(member):
        back = mm(inverse_ref[matching], thirds(state["weighted", member], 0))
        state["back", member] = [
            jnp.concatenate(
                [block(back[height * part : height * part + height], group) for part in (1, 0)], axis=1
            )
            for group in range(back.shape[1] // 128)
        ]

    def inverses(member):
        state["ready final", member] = state["back", member]
        for members in joint("final", JI, member):
            values = sum((state["back", one] for one in members), [])
            found = mm(
                thirds(jnp.concatenate(values, axis=0), 1),
                fold(table_part(table_ref, places["forward"]), 0),
            )
            for one in members:
                count = len(state["back", one])
                state["final", one] = [
                    found[height * group : height * group + height] for group in range(count)
                ]
                found = found[count * height :]

    def outputs(member):
        edge = state["final", 0][blocks]
        edge_scale = state["scale", 0][blocks]
        for part in range(2):
            whole = [
                block(group, 1 - part) * scale
                for group, scale in zip(state["final", member][:blocks], state["scale", member])
            ]
            side = block(edge, 1 - part) * edge_scale
            turned = [pltpu.roll(value, 128 - shift, 1) for value in whole]
            turned.append(pltpu.roll(side, (128 - PATCH if member else 128) - shift, 1))
            cells = [
                jnp.where(lane < 128 - shift, turned[index], turned[index + 1])
                for index in range(blocks)
            ]
            filtered_ref[part, member] = jnp.concatenate(cells, axis=1).astype(BF)
            if finish:
                send(filtered_ref.at[part, member], filtered_out.at[part, matching, member])

    stages = dict(
        F=fields, C=columns, R=ranges, A=coherence, Z=rows, S=scaled, M=means, B=backs, I=inverses, O=outputs
    )
    for step in ORDER:
        stages[step[0]](int(step[1]))
    for copy in copies:
        copy.wait()


def in_hbm(value):
    return pltpu.with_memory_space_constraint(value, pltpu.HBM)


def vmem(count):
    return [pl.BlockSpec(memory_space=pltpu.VMEM)] * count


def match_call(shared, matching, remote, previous):
    pairing, offsets, image, rims, table, forward, inverse, power, places = shared
    height, breadth = image.shape[2] // 2, image.shape[3]
    finish = matching == MATCH - 1
    coherence = pltpu.VMEM((2, height, breadth), F32)
    filtered = pltpu.VMEM((2, 2, height, breadth), BF)
    inputs = [pairing, offsets, image, rims, table, forward, inverse, power, *remote]
    specs = [pl.BlockSpec(memory_space=pltpu.SMEM)] * 2 + vmem(6 + len(remote))
    out_shape, out_specs, scratch = (coherence, filtered), vmem(2), []
    if finish:
        inputs += previous
        specs += vmem(len(previous))
        out_shape = (
            jax.ShapeDtypeStruct((MATCH, 2, height, breadth), F32),
            jax.ShapeDtypeStruct((2, MATCH, 2, height, breadth), BF),
        )
        out_specs = [pl.BlockSpec(memory_space=pl.ANY)] * 2
        scratch = [coherence, filtered, pltpu.SemaphoreType.DMA((3 * matching + 6,))]
    return pl.pallas_call(
        functools.partial(match_kernel, matching, places, finish),
        out_shape=out_shape,
        in_specs=specs,
        out_specs=tuple(out_specs),
        scratch_shapes=scratch,
        cost_estimate=pl.CostEstimate(flops=2 * 10**9, bytes_accessed=3 * 10**6, transcendentals=0),
        compiler_params=GRANT,
    )(*inputs)


def xor_swap(value, mask):
    return lax.ppermute(value, "acq", [(i, i ^ mask) for i in range(lax.axis_size("acq"))])


def neighbour_swap(value, parity):
    places, groups = lax.axis_size("rng"), lax.axis_size("acq")
    pairs = []
    for group in range(groups):
        for place in range(places):
            other = place + 1 if place % 2 == parity else place - 1
            if 0 <= other < places:
                target = group * places + other
            else:
                target = (group ^ 1) * places + place
            pairs.append((group * places + place, target))
    return lax.ppermute(value, ("acq", "rng"), pairs)


def per_device(images, pairing, tile_offsets):
    lines, breadth = images.shape[2:]
    height = lines // 2
    table, places = all_tables(breadth, height)
    row_table, row_places = line_tables(height)
    table, row_table = jnp.asarray(table), jnp.asarray(row_table)
    side = pltpu.VMEM((lines, 128), BF)
    payload = pltpu.VMEM((5, height, breadth), BF)
    offsets = tile_offsets.T
    mains = pltpu.VMEM((4, height, breadth), BF)
    scalars = [pl.BlockSpec(memory_space=pltpu.SMEM)] * 2
    image, first, second, far = pl.pallas_call(
        pack_kernel,
        out_shape=(pltpu.VMEM(images.shape, BF), side, side, mains),
        in_specs=[pl.BlockSpec(memory_space=pl.ANY)],
        out_specs=tuple(vmem(4)),
        scratch_shapes=[pltpu.SemaphoreType.DMA],
        cost_estimate=pl.CostEstimate(flops=COST, bytes_accessed=10**6, transcendentals=0),
        compiler_params=GRANT,
        name="pack",
    )(in_hbm(images))
    first = neighbour_swap(first, 0)
    second = neighbour_swap(second, 1)
    far = xor_swap(far, 2)
    freqs = height + PATCH
    near, forward, inverse, pairing, offsets = pl.pallas_call(
        functools.partial(main_kernel, row_places),
        out_shape=(
            payload,
            pltpu.VMEM((MATCH, 2 * freqs, 4 * height), BF),
            pltpu.VMEM((MATCH, 2 * height, 6 * freqs), BF),
            pltpu.SMEM(pairing.shape, jnp.int32),
            pltpu.SMEM(offsets.shape, jnp.int32),
        ),
        in_specs=[*vmem(1), *[pl.BlockSpec(memory_space=pl.ANY)] * 2, *vmem(1)],
        out_specs=(*vmem(3), *scalars),
        scratch_shapes=[pltpu.SemaphoreType.DMA((2,))],
        cost_estimate=pl.CostEstimate(flops=COST, bytes_accessed=10**6, transcendentals=0),
        compiler_params=GRANT,
        name="mains",
    )(image, in_hbm(pairing), in_hbm(offsets), row_table)
    near, far_rims, rims = pl.pallas_call(
        functools.partial(rim_kernel, lax.axis_size("rng") - 1),
        out_shape=(
            payload,
            pltpu.VMEM((height, breadth), BF),
            pltpu.VMEM((2, lines, 128), BF),
        ),
        in_specs=vmem(3),
        out_specs=tuple(vmem(3)),
        input_output_aliases={2: 0},
        compiler_params=GRANT,
        name="rims",
    )(first, second, near)
    near = xor_swap(near, 1)
    far_rims = xor_swap(far_rims, 2)
    power = pl.pallas_call(
        functools.partial(power_kernel, places),
        out_shape=pltpu.VMEM((2, 2, height, breadth), F32),
        in_specs=vmem(3),
        out_specs=vmem(1)[0],
        cost_estimate=pl.CostEstimate(flops=10**9, bytes_accessed=10**6, transcendentals=0),
        compiler_params=GRANT,
        name="power",
    )(image, rims, table)
    call = functools.partial(
        match_call, (pairing, offsets, image, rims, table, forward, inverse, power, places)
    )
    outputs = call(0, (near,), ())
    far, far_rims, *outputs = lax.optimization_barrier((far, far_rims, *outputs))
    both = xor_swap(far, 1)
    both_rims = xor_swap(far_rims, 1)
    outputs = [*outputs, *call(1, (far, far_rims), ())]
    return tuple(call(2, (both, both_rims), outputs))


def solution(mesh):
    in_specs = (P(None, ("stack", "acq"), None, "rng"), P(), P())
    out_specs = (
        P(None, ("stack", "acq"), None, "rng"),
        P(None, None, ("stack", "acq"), None, "rng"),
    )

    return jax.shard_map(
        per_device, mesh=mesh, in_specs=in_specs, out_specs=out_specs, check_vma=False
    )
```

```python
import functools

import jax
import jax.numpy as jnp
import numpy as np
from jax import lax
from jax.experimental import pallas as pl
from jax.experimental.pallas import tpu as pltpu
from jax.sharding import PartitionSpec as P

MATCH = 3
REACH = 32
PATCH = 32
EPSILON = 1e-06
BF = jnp.bfloat16
F32 = jnp.float32
GRANT = pltpu.CompilerParams(vmem_limit_bytes=24 << 20)


def split_table(table):
    high = table.astype(np.float32).astype(BF)
    low = (table - high.astype(np.float64)).astype(np.float32).astype(BF)
    return high, low


def gauss(spread):
    width = REACH / 8.0
    weights = np.exp(-(spread.astype(np.float64) ** 2) / (2.0 * width * width))
    return np.where(np.abs(spread) <= REACH, weights, 0.0)


def stacked(table, copies=1):
    high, low = split_table(table)
    return np.concatenate([high] * copies + [low], axis=0)


def range_table(breadth):
    lanes = breadth + 128
    row = np.arange(lanes)
    cell = np.where(row < breadth + REACH, row, row - lanes)
    band = gauss(cell[:, None] - np.arange(breadth)[None, :])
    valid = (row < breadth + REACH) | (row >= lanes - REACH)
    return stacked(band * valid[:, None])


def azimuth_table(height):
    line = np.arange(height)
    return stacked(gauss(line[:, None] - line[None, :]), 2).T


def waves(rows, cols):
    angle = 2.0 * np.pi / PATCH * ((rows[:, None] * cols[None, :]) % PATCH)
    return np.cos(angle), np.sin(angle)


def column_tables():
    lane = np.arange(128)
    same = (lane[:, None] // PATCH) == (lane[None, :] // PATCH)
    cosine, sine = waves(lane % PATCH, lane % PATCH)
    cosine, sine = cosine * same, sine * same
    forward = np.block([[cosine, -sine], [sine, cosine]])
    return stacked(forward), same.astype(np.float32).astype(BF)


def row_tables(height):
    patches = height // PATCH + 1
    freq = np.arange(patches * PATCH) % PATCH
    cosine, sine = waves(freq, np.arange(height))
    forward = np.block([[cosine, sine], [-sine, cosine]])
    return stacked(forward.T).T, stacked(forward / (PATCH * PATCH), 2).T


def laid_out(parts):
    places, rows, start = {}, [], 0
    for name, part in parts.items():
        tall = -(-part.shape[0] // 16) * 16
        places[name] = []
        for first in range(0, part.shape[1], 256):
            piece = part[:, first : first + 256]
            block = np.zeros((tall, 256), BF)
            block[: piece.shape[0], : piece.shape[1]] = piece
            places[name].append((start, *piece.shape))
            rows.append(block)
            start += tall
    return np.concatenate(rows, axis=0), places


def all_tables(breadth, height):
    parts = {"band": range_table(breadth), "azimuth": azimuth_table(height)}
    parts["forward"], parts["same"] = column_tables()
    return laid_out(parts)


def line_tables(height):
    forward, inverse = row_tables(height)
    return laid_out({"row_forward": forward, "row_inverse": inverse})


def halves(value):
    high = value.astype(BF)
    return high, (value - high.astype(F32)).astype(BF)


def thirds(value, axis):
    high, low = halves(value)
    return jnp.concatenate([high, low, high], axis=axis)


def fold(table, axis):
    high, low = jnp.split(table, 2, axis=axis)
    return jnp.concatenate([high, high, low], axis=axis)


def mm(left, right):
    return jnp.dot(left, right, preferred_element_type=F32)


def lane_group(shape):
    return lax.broadcasted_iota(jnp.int32, shape, 1) >> 5


def even_place():
    return lax.axis_index("rng") % 2 == 0


def outgoing(mask, height):
    grouped = lax.axis_index("acq")
    upper = (grouped > jnp.bitwise_xor(grouped, mask)).astype(jnp.int32)
    return pl.multiple_of((1 - upper) * height, height)


def pack_kernel(
    source_ref,
    pairing_source,
    offset_source,
    image_ref,
    first_ref,
    second_ref,
    far_ref,
    pairing_ref,
    offset_ref,
    sem,
):
    copies = [
        pltpu.make_async_copy(source_ref, image_ref, sem.at[0]),
        pltpu.make_async_copy(pairing_source, pairing_ref, sem.at[1]),
        pltpu.make_async_copy(offset_source, offset_ref, sem.at[2]),
    ]
    for copy in copies:
        copy.start()
    copies[0].wait()
    breadth = image_ref.shape[3]
    group = lane_group((image_ref.shape[2], 128))
    sides = []
    for first, order in (
        (breadth - 128, ((1, 1, 32), (0, 1, 64), (1, 0, 96), (0, 0, 0))),
        (0, ((0, 0, 0), (1, 1, 32), (0, 1, 64), (1, 0, 96))),
    ):
        value = None
        for position, (part, member, shift) in enumerate(order):
            cells = image_ref[part, member, :, first : first + 128].astype(F32)
            cells = pltpu.roll(cells, shift, 1) if shift else cells
            value = cells if value is None else jnp.where(group == position, cells, value)
        sides.append(value)
    tail, head = sides
    even = even_place()
    first_ref[...] = jnp.where(even, tail, head).astype(BF)
    second_ref[...] = jnp.where(even, head, tail).astype(BF)
    height = image_ref.shape[2] // 2
    fill(far_ref, image_ref, outgoing(2, height), height)
    for copy in copies[1:]:
        copy.wait()


def fill(target, image_ref, start, height):
    for part in range(2):
        for member in range(2):
            target[2 * part + member] = image_ref[part, member, pl.ds(start, height), :]


def row_mask(height, row_offset, freq_dim, thrice):
    freqs = height + PATCH
    rows, cols = 2 * height, 2 * freqs
    if freq_dim == 0:
        line = lax.broadcasted_iota(jnp.int32, (PATCH, rows), 1) & (height - 1)
        patch = (line + PATCH - row_offset) >> 5
        keep = jnp.concatenate(
            [jnp.where(patch == place, 1.0, 0.0).astype(BF) for place in range(freqs // PATCH)] * 2,
            axis=0,
        )
        return jnp.concatenate([keep] * thrice, axis=1)
    line = lax.broadcasted_iota(jnp.int32, (rows, thrice * cols), 0) & (height - 1)
    lane = lax.broadcasted_iota(jnp.int32, (8, thrice * cols), 1)
    for step in (4, 2, 1):
        lane = jnp.where(lane >= step * freqs, lane - step * freqs, lane)
    keep = ((line + PATCH - row_offset) >> 5) == (lane >> 5)[:1]
    return jnp.where(keep, 1.0, 0.0).astype(BF)


def table_part(table_ref, pieces):
    pieces = [table_ref[first : first + rows, :cols] for first, rows, cols in pieces]
    return jnp.concatenate(pieces, axis=1) if len(pieces) > 1 else pieces[0]


def main_kernel(places, image_ref, offset_ref, row_ref, near_ref, forward_ref, inverse_ref):
    height = image_ref.shape[2] // 2
    fill(near_ref, image_ref, outgoing(1, height), height)
    row_forward = table_part(row_ref, places["row_forward"])
    row_inverse = table_part(row_ref, places["row_inverse"])
    for matching in range(MATCH):
        row_offset = offset_ref[0, matching]
        forward_ref[matching] = row_forward * row_mask(height, row_offset, 0, 2)
        inverse_ref[matching] = row_inverse * row_mask(height, row_offset, 1, 3)


def rim_kernel(ends, first_ref, second_ref, near_in, near_ref, far_ref, rim_ref):
    height = far_ref.shape[0]
    even = even_place()
    place = lax.axis_index("rng")
    first = first_ref[...].astype(F32)
    second = second_ref[...].astype(F32)
    head = jnp.where(place < ends, jnp.where(even, first, second), 0.0)
    tail = jnp.where(place > 0, jnp.where(even, second, first), 0.0)
    odd = (lane_group(tail.shape) & 1) == 1
    rim_ref[0] = jnp.where(odd, tail, head).astype(BF)
    rim_ref[1] = pltpu.roll(jnp.where(odd, head, tail), 32, 1).astype(BF)
    for target, mask in ((near_ref.at[4], 1), (far_ref, 2)):
        start = outgoing(mask, height)
        for part in range(2):
            target[:, 128 * part : 128 * part + 128] = rim_ref[part, pl.ds(start, height), :]


def half_of(matching, height):
    grouped = lax.axis_index("acq")
    upper = (grouped > jnp.bitwise_xor(grouped, matching + 1)).astype(jnp.int32)
    return pl.multiple_of(upper * height, height)


def own_cells(image_ref, rim_ref, part, member, start, height):
    rim = rim_ref[part, pl.ds(start, height), :].astype(F32)
    if member:
        rim = pltpu.roll(rim, 64, 1)
    main = image_ref[part, member, pl.ds(start, height), :].astype(F32)
    return jnp.concatenate([main, rim], axis=1)


def along_lines(azimuth, ranged, index, height):
    return mm(azimuth, thirds(ranged[index * height : index * height + height], 0))


def power_kernel(places, image_ref, rim_ref, table_ref, power_ref):
    height = image_ref.shape[2] // 2
    fields = []
    for matching in range(2):
        for member in range(2):
            real, imag = [
                own_cells(image_ref, rim_ref, part, member, half_of(matching, height), height)
                for part in range(2)
            ]
            fields.append(real * real + imag * imag)
    azimuth = table_part(table_ref, places["azimuth"])
    ranged = [
        mm(
            thirds(jnp.concatenate(fields[first : first + 2], axis=0), 1),
            fold(table_part(table_ref, places["band"]), 0),
        )
        for first in (0, 2)
    ]
    for index in range(2):
        for matching in range(2):
            power_ref[matching, index] = along_lines(azimuth, ranged[matching], index, height)


COST = 4 * 10**9
JC, JR, JI = True, True, False
ORDER = (
    "F0", "F1", "R1", "C0", "C1", "R0", "Z0", "A1", "S0", "Z1",
    "S1", "B0", "B1", "M1", "M0", "A0", "I0", "I1", "O1", "O0",
)


def match_kernel(
    matching,
    places,
    finish,
    pairing_ref,
    offset_ref,
    image_ref,
    rim_ref,
    table_ref,
    forward_ref,
    inverse_ref,
    power_ref,
    remote_ref,
    *rest,
):
    if matching:
        remote_rim_ref, *rest = rest
    else:
        remote_rim_ref = remote_ref.at[4]
    copies = []

    def send(source, target):
        copy = pltpu.make_async_copy(source, target, sems.at[len(copies)])
        copy.start()
        copies.append(copy)

    if finish:
        earlier, (coherence_out, filtered_out) = rest[: 2 * matching], rest[2 * matching :][:2]
        coherence_ref, filtered_ref, sems = rest[2 * matching + 2 :]
        for index in range(matching):
            send(earlier[2 * index], coherence_out.at[index])
            for part in range(2):
                send(earlier[2 * index + 1].at[part], filtered_out.at[part, index])
    else:
        coherence_ref, filtered_ref = rest
    height = image_ref.shape[2] // 2
    breadth = image_ref.shape[3]
    patches = height // PATCH + 1
    freqs = patches * PATCH
    blocks = breadth // 128
    grouped = lax.axis_index("acq")
    start = half_of(matching, height)
    shift = REACH - offset_ref[1, matching]
    lane = lax.broadcasted_iota(jnp.int32, (height, 128), 1)
    state = {}

    def block(value, index):
        return value[:, 128 * index : 128 * index + 128]

    def fields(member):
        partner = pairing_ref[matching, 2 * grouped + member] % 2
        ours, theirs = [], []
        for part in range(2):
            ours.append(own_cells(image_ref, rim_ref, part, member, start, height))
            if ("rims", part) not in state:
                rim = block(remote_rim_ref[...], part).astype(F32)
                state["rims", part] = rim, pltpu.roll(rim, 64, 1)
            rim = jnp.where(partner == 1, *state["rims", part][::-1])
            main = remote_ref[2 * part + partner].astype(F32)
            theirs.append(jnp.concatenate([main, rim], axis=1))
        inter_real = ours[0] * theirs[0] + ours[1] * theirs[1]
        inter_imag = ours[1] * theirs[0] - ours[0] * theirs[1]
        power = theirs[0] * theirs[0] + theirs[1] * theirs[1]
        state["fields", member] = [inter_real, inter_imag, power]
        windows = []
        for value in (inter_real, inter_imag):
            turned = [pltpu.roll(block(value, index), shift, 1) for index in range(blocks + 1)]
            windows.append(
                [jnp.where(lane < shift, turned[index - 1], turned[index]) for index in range(blocks + 1)]
            )
        state["window", member] = windows

    def joint(stage, together, member):
        if not together:
            return [(member,)]
        return [(0, 1)] if ("ready " + stage, 1 - member) in state else []

    def columns(member):
        windows = state["window", member]
        groups = [
            jnp.concatenate([part[index] for part in windows], axis=1) for index in range(blocks)
        ]
        if member == 0:
            other = state["window", 1]
            groups.append(
                jnp.concatenate(
                    [
                        jnp.where(
                            lane < PATCH, windows[part][blocks], pltpu.roll(other[part][blocks], PATCH, 1)
                        )
                        for part in range(2)
                    ],
                    axis=1,
                )
            )
        state["ready column", member] = groups
        for members in joint("column", JC, member):
            values = sum((state["ready column", one] for one in members), [])
            found = mm(
                thirds(jnp.concatenate(values, axis=0), 1),
                fold(table_part(table_ref, places["forward"]), 0),
            )
            for one in members:
                count = len(state["ready column", one])
                state["column", one] = jnp.concatenate(
                    [
                        jnp.concatenate(
                            [
                                block(found[height * group : height * group + height], part)
                                for part in range(2)
                            ],
                            axis=0,
                        )
                        for group in range(count)
                    ],
                    axis=1,
                )
                found = found[count * height :]

    def ranges(member):
        state["ready range", member] = state["fields", member]
        for members in joint("range", JR, member):
            values = sum((state["fields", one] for one in members), [])
            found = mm(
                thirds(jnp.concatenate(values, axis=0), 1),
                fold(table_part(table_ref, places["band"]), 0),
            )
            for one in members:
                state["range", one], found = found[: 3 * height], found[3 * height :]

    def coherence(member):
        azimuth = table_part(table_ref, places["azimuth"])
        real, imag, power = [
            along_lines(azimuth, state["range", member], index, height) for index in range(3)
        ]
        own = power_ref[min(matching, 1), member]
        coherence_ref[member] = (real * real + imag * imag) / (own * power + EPSILON)
        if finish:
            send(coherence_ref.at[member], coherence_out.at[matching, member])

    def rows(member):
        state["freq", member] = mm(fold(forward_ref[matching], 1), thirds(state["column", member], 0))

    def scaled(member):
        freq = state["freq", member]
        freq_real, freq_imag = freq[:freqs], freq[freqs:]
        power = freq_real * freq_real + freq_imag * freq_imag + EPSILON
        magnitude = lax.rsqrt(lax.rsqrt(power))

        state["magnitude", member] = magnitude
        state["weighted", member] = jnp.concatenate(
            [freq_real * magnitude, freq_imag * magnitude], axis=0
        )

    def means(member):
        magnitude = state["magnitude", member]
        count = magnitude.shape[1] // 128
        sums = [
            jnp.sum(block(magnitude[PATCH * place : PATCH * place + PATCH], group), axis=0, keepdims=True)
            for group in range(count)
            for place in range(patches)
        ]
        high, low = halves(jnp.concatenate(sums, axis=0))
        same = table_part(table_ref, places["same"])
        totals = mm(high, same) + mm(low, same)
        inverse = 1.0 / (totals * (1.0 / (PATCH * PATCH)) + EPSILON)
        line = lax.broadcasted_iota(jnp.int32, (height, 128), 0)
        patch = (line + PATCH - offset_ref[0, matching]) >> 5
        scales = []
        for group in range(count):
            scale = inverse[group * patches][None]
            for place in range(1, patches):
                scale = jnp.where(patch == place, inverse[group * patches + place][None], scale)
            scales.append(scale)
        state["scale", member] = scales

    def backs(member):
        back = mm(inverse_ref[matching], thirds(state["weighted", member], 0))
        state["back", member] = [
            jnp.concatenate(
                [block(back[height * part : height * part + height], group) for part in (1, 0)], axis=1
            )
            for group in range(back.shape[1] // 128)
        ]

    def inverses(member):
        state["ready final", member] = state["back", member]
        for members in joint("final", JI, member):
            values = sum((state["back", one] for one in members), [])
            found = mm(
                thirds(jnp.concatenate(values, axis=0), 1),
                fold(table_part(table_ref, places["forward"]), 0),
            )
            for one in members:
                count = len(state["back", one])
                state["final", one] = [
                    found[height * group : height * group + height] for group in range(count)
                ]
                found = found[count * height :]

    def outputs(member):
        edge = state["final", 0][blocks]
        edge_scale = state["scale", 0][blocks]
        for part in range(2):
            whole = [
                block(group, 1 - part) * scale
                for group, scale in zip(state["final", member][:blocks], state["scale", member])
            ]
            side = block(edge, 1 - part) * edge_scale
            turned = [pltpu.roll(value, 128 - shift, 1) for value in whole]
            turned.append(pltpu.roll(side, (128 - PATCH if member else 128) - shift, 1))
            cells = [
                jnp.where(lane < 128 - shift, turned[index], turned[index + 1])
                for index in range(blocks)
            ]
            filtered_ref[part, member] = jnp.concatenate(cells, axis=1).astype(BF)
            if finish:
                send(filtered_ref.at[part, member], filtered_out.at[part, matching, member])

    stages = dict(
        F=fields, C=columns, R=ranges, A=coherence, Z=rows, S=scaled, M=means, B=backs, I=inverses, O=outputs
    )
    for step in ORDER:
        stages[step[0]](int(step[1]))
    for copy in copies:
        copy.wait()


def in_hbm(value):
    return pltpu.with_memory_space_constraint(value, pltpu.HBM)


def vmem(count):
    return [pl.BlockSpec(memory_space=pltpu.VMEM)] * count


def match_call(shared, matching, remote, previous):
    pairing, offsets, image, rims, table, forward, inverse, power, places = shared
    height, breadth = image.shape[2] // 2, image.shape[3]
    finish = matching == MATCH - 1
    coherence = pltpu.VMEM((2, height, breadth), F32)
    filtered = pltpu.VMEM((2, 2, height, breadth), BF)
    inputs = [pairing, offsets, image, rims, table, forward, inverse, power, *remote]
    specs = [pl.BlockSpec(memory_space=pltpu.SMEM)] * 2 + vmem(6 + len(remote))
    out_shape, out_specs, scratch = (coherence, filtered), vmem(2), []
    if finish:
        inputs += previous
        specs += vmem(len(previous))
        out_shape = (
            jax.ShapeDtypeStruct((MATCH, 2, height, breadth), F32),
            jax.ShapeDtypeStruct((2, MATCH, 2, height, breadth), BF),
        )
        out_specs = [pl.BlockSpec(memory_space=pl.ANY)] * 2
        scratch = [coherence, filtered, pltpu.SemaphoreType.DMA((3 * matching + 6,))]
    return pl.pallas_call(
        functools.partial(match_kernel, matching, places, finish),
        out_shape=out_shape,
        in_specs=specs,
        out_specs=tuple(out_specs),
        scratch_shapes=scratch,
        cost_estimate=pl.CostEstimate(flops=2 * 10**9, bytes_accessed=3 * 10**6, transcendentals=0),
        compiler_params=GRANT,
    )(*inputs)


def xor_swap(value, mask):
    return lax.ppermute(value, "acq", [(i, i ^ mask) for i in range(lax.axis_size("acq"))])


def neighbour_swap(value, parity):
    places, groups = lax.axis_size("rng"), lax.axis_size("acq")
    pairs = []
    for group in range(groups):
        for place in range(places):
            other = place + 1 if place % 2 == parity else place - 1
            if 0 <= other < places:
                target = group * places + other
            else:
                target = (group ^ 1) * places + place
            pairs.append((group * places + place, target))
    return lax.ppermute(value, ("acq", "rng"), pairs)


def per_device(images, pairing, tile_offsets):
    lines, breadth = images.shape[2:]
    height = lines // 2
    table, places = all_tables(breadth, height)
    row_table, row_places = line_tables(height)
    table, row_table = jnp.asarray(table), jnp.asarray(row_table)
    side = pltpu.VMEM((lines, 128), BF)
    payload = pltpu.VMEM((5, height, breadth), BF)
    offsets = tile_offsets.T
    mains = pltpu.VMEM((4, height, breadth), BF)
    scalars = [pl.BlockSpec(memory_space=pltpu.SMEM)] * 2
    image, first, second, far, pairing, offsets = pl.pallas_call(
        pack_kernel,
        out_shape=(
            pltpu.VMEM(images.shape, BF),
            side,
            side,
            mains,
            pltpu.SMEM(pairing.shape, jnp.int32),
            pltpu.SMEM(offsets.shape, jnp.int32),
        ),
        in_specs=[pl.BlockSpec(memory_space=pl.ANY)] * 3,
        out_specs=(*vmem(4), *scalars),
        scratch_shapes=[pltpu.SemaphoreType.DMA((3,))],
        cost_estimate=pl.CostEstimate(flops=COST, bytes_accessed=10**6, transcendentals=0),
        compiler_params=GRANT,
        name="pack",
    )(in_hbm(images), in_hbm(pairing), in_hbm(offsets))
    first = neighbour_swap(first, 0)
    second = neighbour_swap(second, 1)
    far = xor_swap(far, 2)
    freqs = height + PATCH
    near, forward, inverse = pl.pallas_call(
        functools.partial(main_kernel, row_places),
        out_shape=(
            payload,
            pltpu.VMEM((MATCH, 2 * freqs, 4 * height), BF),
            pltpu.VMEM((MATCH, 2 * height, 6 * freqs), BF),
        ),
        in_specs=[*vmem(1), scalars[0], *vmem(1)],
        out_specs=tuple(vmem(3)),
        cost_estimate=pl.CostEstimate(flops=COST, bytes_accessed=10**6, transcendentals=0),
        compiler_params=GRANT,
        name="mains",
    )(image, offsets, row_table)
    near, far_rims, rims = pl.pallas_call(
        functools.partial(rim_kernel, lax.axis_size("rng") - 1),
        out_shape=(
            payload,
            pltpu.VMEM((height, breadth), BF),
            pltpu.VMEM((2, lines, 128), BF),
        ),
        in_specs=vmem(3),
        out_specs=tuple(vmem(3)),
        input_output_aliases={2: 0},
        compiler_params=GRANT,
        name="rims",
    )(first, second, near)
    near = xor_swap(near, 1)
    far_rims = xor_swap(far_rims, 2)
    power = pl.pallas_call(
        functools.partial(power_kernel, places),
        out_shape=pltpu.VMEM((2, 2, height, breadth), F32),
        in_specs=vmem(3),
        out_specs=vmem(1)[0],
        cost_estimate=pl.CostEstimate(flops=10**9, bytes_accessed=10**6, transcendentals=0),
        compiler_params=GRANT,
        name="power",
    )(image, rims, table)
    call = functools.partial(
        match_call, (pairing, offsets, image, rims, table, forward, inverse, power, places)
    )
    outputs = call(0, (near,), ())
    far, far_rims, *outputs = lax.optimization_barrier((far, far_rims, *outputs))
    both = xor_swap(far, 1)
    both_rims = xor_swap(far_rims, 1)
    outputs = [*outputs, *call(1, (far, far_rims), ())]
    return tuple(call(2, (both, both_rims), outputs))


def solution(mesh):
    in_specs = (P(None, ("stack", "acq"), None, "rng"), P(), P())
    out_specs = (
        P(None, ("stack", "acq"), None, "rng"),
        P(None, None, ("stack", "acq"), None, "rng"),
    )

    return jax.shard_map(
        per_device, mesh=mesh, in_specs=in_specs, out_specs=out_specs, check_vma=False
    )
```

```python
import functools

import jax
import jax.numpy as jnp
import numpy as np
from jax import lax
from jax.experimental import pallas as pl
from jax.experimental.pallas import tpu as pltpu
from jax.sharding import PartitionSpec as P

MATCH = 3
REACH = 32
PATCH = 32
EPSILON = 1e-06
BF = jnp.bfloat16
F32 = jnp.float32
GRANT = pltpu.CompilerParams(vmem_limit_bytes=24 << 20)


def split_table(table):
    high = table.astype(np.float32).astype(BF)
    low = (table - high.astype(np.float64)).astype(np.float32).astype(BF)
    return high, low


def gauss(spread):
    width = REACH / 8.0
    weights = np.exp(-(spread.astype(np.float64) ** 2) / (2.0 * width * width))
    return np.where(np.abs(spread) <= REACH, weights, 0.0)


def stacked(table, copies=1):
    high, low = split_table(table)
    return np.concatenate([high] * copies + [low], axis=0)


def range_table(breadth):
    lanes = breadth + 128
    row = np.arange(lanes)
    cell = np.where(row < breadth + REACH, row, row - lanes)
    band = gauss(cell[:, None] - np.arange(breadth)[None, :])
    valid = (row < breadth + REACH) | (row >= lanes - REACH)
    return stacked(band * valid[:, None])


def azimuth_table(height):
    line = np.arange(height)
    return stacked(gauss(line[:, None] - line[None, :]), 2).T


def waves(rows, cols):
    angle = 2.0 * np.pi / PATCH * ((rows[:, None] * cols[None, :]) % PATCH)
    return np.cos(angle), np.sin(angle)


def column_tables():
    lane = np.arange(128)
    same = (lane[:, None] // PATCH) == (lane[None, :] // PATCH)
    cosine, sine = waves(lane % PATCH, lane % PATCH)
    cosine, sine = cosine * same, sine * same
    forward = np.block([[cosine, -sine], [sine, cosine]])
    return stacked(forward), same.astype(np.float32).astype(BF)


def row_tables(height):
    patches = height // PATCH + 1
    freq = np.arange(patches * PATCH) % PATCH
    cosine, sine = waves(freq, np.arange(height))
    forward = np.block([[cosine, sine], [-sine, cosine]])
    return stacked(forward.T).T, stacked(forward / (PATCH * PATCH), 2).T


def laid_out(parts):
    places, rows, start = {}, [], 0
    for name, part in parts.items():
        tall = -(-part.shape[0] // 16) * 16
        places[name] = []
        for first in range(0, part.shape[1], 256):
            piece = part[:, first : first + 256]
            block = np.zeros((tall, 256), BF)
            block[: piece.shape[0], : piece.shape[1]] = piece
            places[name].append((start, *piece.shape))
            rows.append(block)
            start += tall
    return np.concatenate(rows, axis=0), places


def all_tables(breadth, height):
    parts = {"band": range_table(breadth), "azimuth": azimuth_table(height)}
    parts["forward"], parts["same"] = column_tables()
    return laid_out(parts)


def line_tables(height):
    forward, inverse = row_tables(height)
    return laid_out({"row_forward": forward, "row_inverse": inverse})


def halves(value):
    high = value.astype(BF)
    return high, (value - high.astype(F32)).astype(BF)


def thirds(value, axis):
    high, low = halves(value)
    return jnp.concatenate([high, low, high], axis=axis)


def fold(table, axis):
    high, low = jnp.split(table, 2, axis=axis)
    return jnp.concatenate([high, high, low], axis=axis)


def mm(left, right):
    return jnp.dot(left, right, preferred_element_type=F32)


def lane_group(shape):
    return lax.broadcasted_iota(jnp.int32, shape, 1) >> 5


def even_place():
    return lax.axis_index("rng") % 2 == 0


def outgoing(mask, height):
    grouped = lax.axis_index("acq")
    upper = (grouped > jnp.bitwise_xor(grouped, mask)).astype(jnp.int32)
    return pl.multiple_of((1 - upper) * height, height)


def pack_kernel(
    source_ref,
    pairing_source,
    offset_source,
    image_ref,
    first_ref,
    second_ref,
    far_ref,
    pairing_ref,
    offset_ref,
    sem,
):
    copies = [
        pltpu.make_async_copy(source_ref, image_ref, sem.at[0]),
        pltpu.make_async_copy(pairing_source, pairing_ref, sem.at[1]),
        pltpu.make_async_copy(offset_source, offset_ref, sem.at[2]),
    ]
    for copy in copies:
        copy.start()
    copies[0].wait()
    breadth = image_ref.shape[3]
    group = lane_group((image_ref.shape[2], 128))
    sides = []
    for first, order in (
        (breadth - 128, ((1, 1, 32), (0, 1, 64), (1, 0, 96), (0, 0, 0))),
        (0, ((0, 0, 0), (1, 1, 32), (0, 1, 64), (1, 0, 96))),
    ):
        value = None
        for position, (part, member, shift) in enumerate(order):
            cells = image_ref[part, member, :, first : first + 128].astype(F32)
            cells = pltpu.roll(cells, shift, 1) if shift else cells
            value = cells if value is None else jnp.where(group == position, cells, value)
        sides.append(value)
    tail, head = sides
    even = even_place()
    first_ref[...] = jnp.where(even, tail, head).astype(BF)
    second_ref[...] = jnp.where(even, head, tail).astype(BF)
    height = image_ref.shape[2] // 2
    fill(far_ref, image_ref, outgoing(2, height), height)
    for copy in copies[1:]:
        copy.wait()


def fill(target, image_ref, start, height):
    for part in range(2):
        for member in range(2):
            target[2 * part + member] = image_ref[part, member, pl.ds(start, height), :]


def row_mask(height, row_offset, freq_dim, thrice):
    freqs = height + PATCH
    rows, cols = 2 * height, 2 * freqs
    if freq_dim == 0:
        line = lax.broadcasted_iota(jnp.int32, (PATCH, rows), 1) & (height - 1)
        patch = (line + PATCH - row_offset) >> 5
        keep = jnp.concatenate(
            [jnp.where(patch == place, 1.0, 0.0).astype(BF) for place in range(freqs // PATCH)] * 2,
            axis=0,
        )
        return jnp.concatenate([keep] * thrice, axis=1)
    line = lax.broadcasted_iota(jnp.int32, (rows, thrice * cols), 0) & (height - 1)
    lane = lax.broadcasted_iota(jnp.int32, (8, thrice * cols), 1)
    for step in (4, 2, 1):
        lane = jnp.where(lane >= step * freqs, lane - step * freqs, lane)
    keep = ((line + PATCH - row_offset) >> 5) == (lane >> 5)[:1]
    return jnp.where(keep, 1.0, 0.0).astype(BF)


def table_part(table_ref, pieces):
    pieces = [table_ref[first : first + rows, :cols] for first, rows, cols in pieces]
    return jnp.concatenate(pieces, axis=1) if len(pieces) > 1 else pieces[0]


def main_kernel(places, image_ref, offset_ref, row_ref, near_ref, forward_ref, inverse_ref):
    height = image_ref.shape[2] // 2
    fill(near_ref, image_ref, outgoing(1, height), height)
    row_forward = table_part(row_ref, places["row_forward"])
    row_inverse = table_part(row_ref, places["row_inverse"])
    for matching in range(MATCH):
        row_offset = offset_ref[0, matching]
        forward_ref[matching] = row_forward * row_mask(height, row_offset, 0, 2)
        inverse_ref[matching] = row_inverse * row_mask(height, row_offset, 1, 3)


def rim_kernel(ends, first_ref, second_ref, near_in, near_ref, far_ref, rim_ref):
    height = far_ref.shape[0]
    even = even_place()
    place = lax.axis_index("rng")
    first = first_ref[...].astype(F32)
    second = second_ref[...].astype(F32)
    head = jnp.where(place < ends, jnp.where(even, first, second), 0.0)
    tail = jnp.where(place > 0, jnp.where(even, second, first), 0.0)
    odd = (lane_group(tail.shape) & 1) == 1
    rim_ref[0] = jnp.where(odd, tail, head).astype(BF)
    rim_ref[1] = pltpu.roll(jnp.where(odd, head, tail), 32, 1).astype(BF)
    for target, mask in ((near_ref.at[4], 1), (far_ref, 2)):
        start = outgoing(mask, height)
        for part in range(2):
            target[:, 128 * part : 128 * part + 128] = rim_ref[part, pl.ds(start, height), :]


def half_of(matching, height):
    grouped = lax.axis_index("acq")
    upper = (grouped > jnp.bitwise_xor(grouped, matching + 1)).astype(jnp.int32)
    return pl.multiple_of(upper * height, height)


def own_cells(image_ref, rim_ref, part, member, start, height):
    rim = rim_ref[part, pl.ds(start, height), :].astype(F32)
    if member:
        rim = pltpu.roll(rim, 64, 1)
    main = image_ref[part, member, pl.ds(start, height), :].astype(F32)
    return jnp.concatenate([main, rim], axis=1)


def along_lines(azimuth, ranged, index, height):
    return mm(azimuth, thirds(ranged[index * height : index * height + height], 0))


def power_kernel(places, image_ref, rim_ref, table_ref, power_ref):
    height = image_ref.shape[2] // 2
    fields = []
    for matching in range(2):
        for member in range(2):
            real, imag = [
                own_cells(image_ref, rim_ref, part, member, half_of(matching, height), height)
                for part in range(2)
            ]
            fields.append(real * real + imag * imag)
    azimuth = table_part(table_ref, places["azimuth"])
    ranged = [
        mm(
            thirds(jnp.concatenate(fields[first : first + 2], axis=0), 1),
            fold(table_part(table_ref, places["band"]), 0),
        )
        for first in (0, 2)
    ]
    for index in range(2):
        for matching in range(2):
            power_ref[matching, index] = along_lines(azimuth, ranged[matching], index, height)


COST = 4 * 10**9
JC, JR, JI = True, True, False
ORDER = (
    "F0", "F1", "R1", "C0", "C1", "R0", "Z0", "A1", "S0", "Z1",
    "S1", "B0", "B1", "M1", "M0", "A0", "I0", "I1", "O1", "O0",
)


def match_kernel(
    matching,
    places,
    finish,
    pairing_ref,
    offset_ref,
    image_ref,
    rim_ref,
    table_ref,
    forward_ref,
    inverse_ref,
    power_ref,
    remote_ref,
    *rest,
):
    if matching:
        remote_rim_ref, *rest = rest
    else:
        remote_rim_ref = remote_ref.at[4]
    copies = []

    def send(source, target):
        copy = pltpu.make_async_copy(source, target, sems.at[len(copies)])
        copy.start()
        copies.append(copy)

    if finish:
        earlier, (coherence_out, filtered_out) = rest[: 2 * matching], rest[2 * matching :][:2]
        coherence_ref, filtered_ref, sems = rest[2 * matching + 2 :]
        for index in range(matching):
            send(earlier[2 * index], coherence_out.at[index])
            send(earlier[2 * index + 1], filtered_out.at[:, index])
    else:
        coherence_ref, filtered_ref = rest
    height = image_ref.shape[2] // 2
    breadth = image_ref.shape[3]
    patches = height // PATCH + 1
    freqs = patches * PATCH
    blocks = breadth // 128
    grouped = lax.axis_index("acq")
    start = half_of(matching, height)
    shift = REACH - offset_ref[1, matching]
    lane = lax.broadcasted_iota(jnp.int32, (height, 128), 1)
    state = {}

    def block(value, index):
        return value[:, 128 * index : 128 * index + 128]

    def fields(member):
        partner = pairing_ref[matching, 2 * grouped + member] % 2
        ours, theirs = [], []
        for part in range(2):
            ours.append(own_cells(image_ref, rim_ref, part, member, start, height))
            if ("rims", part) not in state:
                rim = block(remote_rim_ref[...], part).astype(F32)
                state["rims", part] = rim, pltpu.roll(rim, 64, 1)
            rim = jnp.where(partner == 1, *state["rims", part][::-1])
            main = remote_ref[2 * part + partner].astype(F32)
            theirs.append(jnp.concatenate([main, rim], axis=1))
        inter_real = ours[0] * theirs[0] + ours[1] * theirs[1]
        inter_imag = ours[1] * theirs[0] - ours[0] * theirs[1]
        power = theirs[0] * theirs[0] + theirs[1] * theirs[1]
        state["fields", member] = [inter_real, inter_imag, power]
        windows = []
        for value in (inter_real, inter_imag):
            turned = [pltpu.roll(block(value, index), shift, 1) for index in range(blocks + 1)]
            windows.append(
                [jnp.where(lane < shift, turned[index - 1], turned[index]) for index in range(blocks + 1)]
            )
        state["window", member] = windows

    def joint(stage, together, member):
        if not together:
            return [(member,)]
        return [(0, 1)] if ("ready " + stage, 1 - member) in state else []

    def columns(member):
        windows = state["window", member]
        groups = [
            jnp.concatenate([part[index] for part in windows], axis=1) for index in range(blocks)
        ]
        if member == 0:
            other = state["window", 1]
            groups.append(
                jnp.concatenate(
                    [
                        jnp.where(
                            lane < PATCH, windows[part][blocks], pltpu.roll(other[part][blocks], PATCH, 1)
                        )
                        for part in range(2)
                    ],
                    axis=1,
                )
            )
        state["ready column", member] = groups
        for members in joint("column", JC, member):
            values = sum((state["ready column", one] for one in members), [])
            found = mm(
                thirds(jnp.concatenate(values, axis=0), 1),
                fold(table_part(table_ref, places["forward"]), 0),
            )
            for one in members:
                count = len(state["ready column", one])
                state["column", one] = jnp.concatenate(
                    [
                        jnp.concatenate(
                            [
                                block(found[height * group : height * group + height], part)
                                for part in range(2)
                            ],
                            axis=0,
                        )
                        for group in range(count)
                    ],
                    axis=1,
                )
                found = found[count * height :]

    def ranges(member):
        state["ready range", member] = state["fields", member]
        for members in joint("range", JR, member):
            values = sum((state["fields", one] for one in members), [])
            found = mm(
                thirds(jnp.concatenate(values, axis=0), 1),
                fold(table_part(table_ref, places["band"]), 0),
            )
            for one in members:
                state["range", one], found = found[: 3 * height], found[3 * height :]

    def coherence(member):
        azimuth = table_part(table_ref, places["azimuth"])
        real, imag, power = [
            along_lines(azimuth, state["range", member], index, height) for index in range(3)
        ]
        own = power_ref[min(matching, 1), member]
        coherence_ref[member] = (real * real + imag * imag) / (own * power + EPSILON)
        if finish:
            send(coherence_ref.at[member], coherence_out.at[matching, member])

    def rows(member):
        state["freq", member] = mm(fold(forward_ref[matching], 1), thirds(state["column", member], 0))

    def scaled(member):
        freq = state["freq", member]
        freq_real, freq_imag = freq[:freqs], freq[freqs:]
        power = freq_real * freq_real + freq_imag * freq_imag + EPSILON
        magnitude = lax.rsqrt(lax.rsqrt(power))

        state["magnitude", member] = magnitude
        state["weighted", member] = jnp.concatenate(
            [freq_real * magnitude, freq_imag * magnitude], axis=0
        )

    def means(member):
        magnitude = state["magnitude", member]
        count = magnitude.shape[1] // 128
        sums = [
            jnp.sum(block(magnitude[PATCH * place : PATCH * place + PATCH], group), axis=0, keepdims=True)
            for group in range(count)
            for place in range(patches)
        ]
        high, low = halves(jnp.concatenate(sums, axis=0))
        same = table_part(table_ref, places["same"])
        totals = mm(high, same) + mm(low, same)
        inverse = 1.0 / (totals * (1.0 / (PATCH * PATCH)) + EPSILON)
        line = lax.broadcasted_iota(jnp.int32, (height, 128), 0)
        patch = (line + PATCH - offset_ref[0, matching]) >> 5
        scales = []
        for group in range(count):
            scale = inverse[group * patches][None]
            for place in range(1, patches):
                scale = jnp.where(patch == place, inverse[group * patches + place][None], scale)
            scales.append(scale)
        state["scale", member] = scales

    def backs(member):
        back = mm(inverse_ref[matching], thirds(state["weighted", member], 0))
        state["back", member] = [
            jnp.concatenate(
                [block(back[height * part : height * part + height], group) for part in (1, 0)], axis=1
            )
            for group in range(back.shape[1] // 128)
        ]

    def inverses(member):
        state["ready final", member] = state["back", member]
        for members in joint("final", JI, member):
            values = sum((state["back", one] for one in members), [])
            found = mm(
                thirds(jnp.concatenate(values, axis=0), 1),
                fold(table_part(table_ref, places["forward"]), 0),
            )
            for one in members:
                count = len(state["back", one])
                state["final", one] = [
                    found[height * group : height * group + height] for group in range(count)
                ]
                found = found[count * height :]

    def outputs(member):
        edge = state["final", 0][blocks]
        edge_scale = state["scale", 0][blocks]
        for part in range(2):
            whole = [
                block(group, 1 - part) * scale
                for group, scale in zip(state["final", member][:blocks], state["scale", member])
            ]
            side = block(edge, 1 - part) * edge_scale
            turned = [pltpu.roll(value, 128 - shift, 1) for value in whole]
            turned.append(pltpu.roll(side, (128 - PATCH if member else 128) - shift, 1))
            cells = [
                jnp.where(lane < 128 - shift, turned[index], turned[index + 1])
                for index in range(blocks)
            ]
            filtered_ref[part, member] = jnp.concatenate(cells, axis=1).astype(BF)
        if finish:
            send(filtered_ref.at[:, member], filtered_out.at[:, matching, member])

    stages = dict(
        F=fields, C=columns, R=ranges, A=coherence, Z=rows, S=scaled, M=means, B=backs, I=inverses, O=outputs
    )
    for step in ORDER:
        stages[step[0]](int(step[1]))
    for copy in copies:
        copy.wait()


def in_hbm(value):
    return pltpu.with_memory_space_constraint(value, pltpu.HBM)


def vmem(count):
    return [pl.BlockSpec(memory_space=pltpu.VMEM)] * count


def match_call(shared, matching, remote, previous):
    pairing, offsets, image, rims, table, forward, inverse, power, places = shared
    height, breadth = image.shape[2] // 2, image.shape[3]
    finish = matching == MATCH - 1
    coherence = pltpu.VMEM((2, height, breadth), F32)
    filtered = pltpu.VMEM((2, 2, height, breadth), BF)
    inputs = [pairing, offsets, image, rims, table, forward, inverse, power, *remote]
    specs = [pl.BlockSpec(memory_space=pltpu.SMEM)] * 2 + vmem(6 + len(remote))
    out_shape, out_specs, scratch = (coherence, filtered), vmem(2), []
    if finish:
        inputs += previous
        specs += vmem(len(previous))
        out_shape = (
            jax.ShapeDtypeStruct((MATCH, 2, height, breadth), F32),
            jax.ShapeDtypeStruct((2, MATCH, 2, height, breadth), BF),
        )
        out_specs = [pl.BlockSpec(memory_space=pl.ANY)] * 2
        scratch = [coherence, filtered, pltpu.SemaphoreType.DMA((2 * matching + 4,))]
    return pl.pallas_call(
        functools.partial(match_kernel, matching, places, finish),
        out_shape=out_shape,
        in_specs=specs,
        out_specs=tuple(out_specs),
        scratch_shapes=scratch,
        cost_estimate=pl.CostEstimate(flops=2 * 10**9, bytes_accessed=3 * 10**6, transcendentals=0),
        compiler_params=GRANT,
    )(*inputs)


def xor_swap(value, mask):
    return lax.ppermute(value, "acq", [(i, i ^ mask) for i in range(lax.axis_size("acq"))])


def neighbour_swap(value, parity):
    places, groups = lax.axis_size("rng"), lax.axis_size("acq")
    pairs = []
    for group in range(groups):
        for place in range(places):
            other = place + 1 if place % 2 == parity else place - 1
            if 0 <= other < places:
                target = group * places + other
            else:
                target = (group ^ 1) * places + place
            pairs.append((group * places + place, target))
    return lax.ppermute(value, ("acq", "rng"), pairs)


def per_device(images, pairing, tile_offsets):
    lines, breadth = images.shape[2:]
    height = lines // 2
    table, places = all_tables(breadth, height)
    row_table, row_places = line_tables(height)
    table, row_table = jnp.asarray(table), jnp.asarray(row_table)
    side = pltpu.VMEM((lines, 128), BF)
    payload = pltpu.VMEM((5, height, breadth), BF)
    offsets = tile_offsets.T
    mains = pltpu.VMEM((4, height, breadth), BF)
    scalars = [pl.BlockSpec(memory_space=pltpu.SMEM)] * 2
    image, first, second, far, pairing, offsets = pl.pallas_call(
        pack_kernel,
        out_shape=(
            pltpu.VMEM(images.shape, BF),
            side,
            side,
            mains,
            pltpu.SMEM(pairing.shape, jnp.int32),
            pltpu.SMEM(offsets.shape, jnp.int32),
        ),
        in_specs=[pl.BlockSpec(memory_space=pl.ANY)] * 3,
        out_specs=(*vmem(4), *scalars),
        scratch_shapes=[pltpu.SemaphoreType.DMA((3,))],
        cost_estimate=pl.CostEstimate(flops=COST, bytes_accessed=10**6, transcendentals=0),
        compiler_params=GRANT,
        name="pack",
    )(in_hbm(images), in_hbm(pairing), in_hbm(offsets))
    first = neighbour_swap(first, 0)
    second = neighbour_swap(second, 1)
    far = xor_swap(far, 2)
    freqs = height + PATCH
    near, forward, inverse = pl.pallas_call(
        functools.partial(main_kernel, row_places),
        out_shape=(
            payload,
            pltpu.VMEM((MATCH, 2 * freqs, 4 * height), BF),
            pltpu.VMEM((MATCH, 2 * height, 6 * freqs), BF),
        ),
        in_specs=[*vmem(1), scalars[0], *vmem(1)],
        out_specs=tuple(vmem(3)),
        cost_estimate=pl.CostEstimate(flops=COST, bytes_accessed=10**6, transcendentals=0),
        compiler_params=GRANT,
        name="mains",
    )(image, offsets, row_table)
    near, far_rims, rims = pl.pallas_call(
        functools.partial(rim_kernel, lax.axis_size("rng") - 1),
        out_shape=(
            payload,
            pltpu.VMEM((height, breadth), BF),
            pltpu.VMEM((2, lines, 128), BF),
        ),
        in_specs=vmem(3),
        out_specs=tuple(vmem(3)),
        input_output_aliases={2: 0},
        compiler_params=GRANT,
        name="rims",
    )(first, second, near)
    near = xor_swap(near, 1)
    far_rims = xor_swap(far_rims, 2)
    power = pl.pallas_call(
        functools.partial(power_kernel, places),
        out_shape=pltpu.VMEM((2, 2, height, breadth), F32),
        in_specs=vmem(3),
        out_specs=vmem(1)[0],
        cost_estimate=pl.CostEstimate(flops=10**9, bytes_accessed=10**6, transcendentals=0),
        compiler_params=GRANT,
        name="power",
    )(image, rims, table)
    call = functools.partial(
        match_call, (pairing, offsets, image, rims, table, forward, inverse, power, places)
    )
    outputs = call(0, (near,), ())
    far, far_rims, *outputs = lax.optimization_barrier((far, far_rims, *outputs))
    both = xor_swap(far, 1)
    both_rims = xor_swap(far_rims, 1)
    outputs = [*outputs, *call(1, (far, far_rims), ())]
    return tuple(call(2, (both, both_rims), outputs))


def solution(mesh):
    in_specs = (P(None, ("stack", "acq"), None, "rng"), P(), P())
    out_specs = (
        P(None, ("stack", "acq"), None, "rng"),
        P(None, None, ("stack", "acq"), None, "rng"),
    )

    return jax.shard_map(
        per_device, mesh=mesh, in_specs=in_specs, out_specs=out_specs, check_vma=False
    )
```

```python
import functools

import jax
import jax.numpy as jnp
import numpy as np
from jax import lax
from jax.experimental import pallas as pl
from jax.experimental.pallas import tpu as pltpu
from jax.sharding import PartitionSpec as P

MATCH = 3
REACH = 32
PATCH = 32
EPSILON = 1e-06
BF = jnp.bfloat16
F32 = jnp.float32
GRANT = pltpu.CompilerParams(vmem_limit_bytes=24 << 20)


def split_table(table):
    high = table.astype(np.float32).astype(BF)
    low = (table - high.astype(np.float64)).astype(np.float32).astype(BF)
    return high, low


def gauss(spread):
    width = REACH / 8.0
    weights = np.exp(-(spread.astype(np.float64) ** 2) / (2.0 * width * width))
    return np.where(np.abs(spread) <= REACH, weights, 0.0)


def stacked(table, copies=1):
    high, low = split_table(table)
    return np.concatenate([high] * copies + [low], axis=0)


def range_table(breadth):
    lanes = breadth + 128
    row = np.arange(lanes)
    cell = np.where(row < breadth + REACH, row, row - lanes)
    band = gauss(cell[:, None] - np.arange(breadth)[None, :])
    valid = (row < breadth + REACH) | (row >= lanes - REACH)
    return stacked(band * valid[:, None])


def azimuth_table(height):
    line = np.arange(height)
    return stacked(gauss(line[:, None] - line[None, :]), 2).T


def waves(rows, cols):
    angle = 2.0 * np.pi / PATCH * ((rows[:, None] * cols[None, :]) % PATCH)
    return np.cos(angle), np.sin(angle)


def column_tables():
    lane = np.arange(128)
    same = (lane[:, None] // PATCH) == (lane[None, :] // PATCH)
    cosine, sine = waves(lane % PATCH, lane % PATCH)
    cosine, sine = cosine * same, sine * same
    forward = np.block([[cosine, -sine], [sine, cosine]])
    return stacked(forward), same.astype(np.float32).astype(BF)


def row_tables(height):
    patches = height // PATCH + 1
    freq = np.arange(patches * PATCH) % PATCH
    cosine, sine = waves(freq, np.arange(height))
    forward = np.block([[cosine, sine], [-sine, cosine]])
    return stacked(forward.T).T, stacked(forward / (PATCH * PATCH), 2).T


def laid_out(parts):
    places, rows, start = {}, [], 0
    for name, part in parts.items():
        tall = -(-part.shape[0] // 16) * 16
        places[name] = []
        for first in range(0, part.shape[1], 256):
            piece = part[:, first : first + 256]
            block = np.zeros((tall, 256), BF)
            block[: piece.shape[0], : piece.shape[1]] = piece
            places[name].append((start, *piece.shape))
            rows.append(block)
            start += tall
    return np.concatenate(rows, axis=0), places


def all_tables(breadth, height):
    parts = {"band": range_table(breadth), "azimuth": azimuth_table(height)}
    parts["forward"], parts["same"] = column_tables()
    return laid_out(parts)


def line_tables(height):
    forward, inverse = row_tables(height)
    return laid_out({"row_forward": forward, "row_inverse": inverse})


def halves(value):
    high = value.astype(BF)
    return high, (value - high.astype(F32)).astype(BF)


def thirds(value, axis):
    high, low = halves(value)
    return jnp.concatenate([high, low, high], axis=axis)


def fold(table, axis):
    high, low = jnp.split(table, 2, axis=axis)
    return jnp.concatenate([high, high, low], axis=axis)


def mm(left, right):
    return jnp.dot(left, right, preferred_element_type=F32)


def lane_group(shape):
    return lax.broadcasted_iota(jnp.int32, shape, 1) >> 5


def kind_of(place):
    return (place + 3) % 3


def outgoing(mask, height):
    grouped = lax.axis_index("acq")
    upper = (grouped > jnp.bitwise_xor(grouped, mask)).astype(jnp.int32)
    return pl.multiple_of((1 - upper) * height, height)


def pack_kernel(
    source_ref,
    pairing_source,
    offset_source,
    image_ref,
    first_ref,
    second_ref,
    third_ref,
    far_ref,
    pairing_ref,
    offset_ref,
    sem,
):
    copies = [
        pltpu.make_async_copy(source_ref, image_ref, sem.at[0]),
        pltpu.make_async_copy(pairing_source, pairing_ref, sem.at[1]),
        pltpu.make_async_copy(offset_source, offset_ref, sem.at[2]),
    ]
    for copy in copies:
        copy.start()
    copies[0].wait()
    breadth = image_ref.shape[3]
    group = lane_group((image_ref.shape[2], 128))
    sides = []
    for first, order in (
        (breadth - 128, ((1, 1, 32), (0, 1, 64), (1, 0, 96), (0, 0, 0))),
        (0, ((0, 0, 0), (1, 1, 32), (0, 1, 64), (1, 0, 96))),
    ):
        value = None
        for position, (part, member, shift) in enumerate(order):
            cells = image_ref[part, member, :, first : first + 128].astype(F32)
            cells = pltpu.roll(cells, shift, 1) if shift else cells
            value = cells if value is None else jnp.where(group == position, cells, value)
        sides.append(value)
    tail, head = sides
    kind = kind_of(lax.axis_index("rng"))
    for turn, target in enumerate((first_ref, second_ref, third_ref)):
        target[...] = jnp.where(kind == turn, tail, head).astype(BF)
    height = image_ref.shape[2] // 2
    fill(far_ref, image_ref, outgoing(2, height), height)
    for copy in copies[1:]:
        copy.wait()


def fill(target, image_ref, start, height):
    for part in range(2):
        for member in range(2):
            target[2 * part + member] = image_ref[part, member, pl.ds(start, height), :]


def row_mask(height, row_offset, freq_dim, thrice):
    freqs = height + PATCH
    rows, cols = 2 * height, 2 * freqs
    if freq_dim == 0:
        line = lax.broadcasted_iota(jnp.int32, (PATCH, rows), 1) & (height - 1)
        patch = (line + PATCH - row_offset) >> 5
        keep = jnp.concatenate(
            [jnp.where(patch == place, 1.0, 0.0).astype(BF) for place in range(freqs // PATCH)] * 2,
            axis=0,
        )
        return jnp.concatenate([keep] * thrice, axis=1)
    line = lax.broadcasted_iota(jnp.int32, (rows, thrice * cols), 0) & (height - 1)
    lane = lax.broadcasted_iota(jnp.int32, (8, thrice * cols), 1)
    for step in (4, 2, 1):
        lane = jnp.where(lane >= step * freqs, lane - step * freqs, lane)
    keep = ((line + PATCH - row_offset) >> 5) == (lane >> 5)[:1]
    return jnp.where(keep, 1.0, 0.0).astype(BF)


def table_part(table_ref, pieces):
    pieces = [table_ref[first : first + rows, :cols] for first, rows, cols in pieces]
    return jnp.concatenate(pieces, axis=1) if len(pieces) > 1 else pieces[0]


def main_kernel(places, image_ref, offset_ref, row_ref, near_ref, forward_ref, inverse_ref):
    height = image_ref.shape[2] // 2
    fill(near_ref, image_ref, outgoing(1, height), height)
    row_forward = table_part(row_ref, places["row_forward"])
    row_inverse = table_part(row_ref, places["row_inverse"])
    for matching in range(MATCH):
        row_offset = offset_ref[0, matching]
        forward_ref[matching] = row_forward * row_mask(height, row_offset, 0, 2)
        inverse_ref[matching] = row_inverse * row_mask(height, row_offset, 1, 3)


def rim_kernel(ends, first_ref, second_ref, third_ref, near_in, near_ref, far_ref, rim_ref):
    height = far_ref.shape[0]
    place = lax.axis_index("rng")
    turns = [ref[...].astype(F32) for ref in (first_ref, second_ref, third_ref)]

    def taken(kind):
        return jnp.where(kind == 0, turns[0], jnp.where(kind == 1, turns[1], turns[2]))

    head = jnp.where(place < ends, taken(kind_of(place)), 0.0)
    tail = jnp.where(place > 0, taken(kind_of(place - 1)), 0.0)
    odd = (lane_group(tail.shape) & 1) == 1
    rim_ref[0] = jnp.where(odd, tail, head).astype(BF)
    rim_ref[1] = pltpu.roll(jnp.where(odd, head, tail), 32, 1).astype(BF)
    for target, mask in ((near_ref.at[4], 1), (far_ref, 2)):
        start = outgoing(mask, height)
        for part in range(2):
            target[:, 128 * part : 128 * part + 128] = rim_ref[part, pl.ds(start, height), :]


def half_of(matching, height):
    grouped = lax.axis_index("acq")
    upper = (grouped > jnp.bitwise_xor(grouped, matching + 1)).astype(jnp.int32)
    return pl.multiple_of(upper * height, height)


def own_cells(image_ref, rim_ref, part, member, start, height):
    rim = rim_ref[part, pl.ds(start, height), :].astype(F32)
    if member:
        rim = pltpu.roll(rim, 64, 1)
    main = image_ref[part, member, pl.ds(start, height), :].astype(F32)
    return jnp.concatenate([main, rim], axis=1)


def along_lines(azimuth, ranged, index, height):
    return mm(azimuth, thirds(ranged[index * height : index * height + height], 0))


def power_kernel(places, image_ref, rim_ref, table_ref, power_ref):
    height = image_ref.shape[2] // 2
    fields = []
    for matching in range(2):
        for member in range(2):
            real, imag = [
                own_cells(image_ref, rim_ref, part, member, half_of(matching, height), height)
                for part in range(2)
            ]
            fields.append(real * real + imag * imag)
    azimuth = table_part(table_ref, places["azimuth"])
    ranged = [
        mm(
            thirds(jnp.concatenate(fields[first : first + 2], axis=0), 1),
            fold(table_part(table_ref, places["band"]), 0),
        )
        for first in (0, 2)
    ]
    for index in range(2):
        for matching in range(2):
            power_ref[matching, index] = along_lines(azimuth, ranged[matching], index, height)


COST = 4 * 10**9
JC, JR, JI = True, True, False
ORDER = (
    "F0", "F1", "R1", "C0", "C1", "R0", "Z0", "A1", "S0", "Z1",
    "S1", "B0", "B1", "M1", "M0", "A0", "I0", "I1", "O1", "O0",
)


def match_kernel(
    matching,
    places,
    finish,
    pairing_ref,
    offset_ref,
    image_ref,
    rim_ref,
    table_ref,
    forward_ref,
    inverse_ref,
    power_ref,
    remote_ref,
    *rest,
):
    if matching:
        remote_rim_ref, *rest = rest
    else:
        remote_rim_ref = remote_ref.at[4]
    copies = []

    def send(source, target):
        copy = pltpu.make_async_copy(source, target, sems.at[len(copies)])
        copy.start()
        copies.append(copy)

    if finish:
        earlier, (coherence_out, filtered_out) = rest[: 2 * matching], rest[2 * matching :][:2]
        coherence_ref, filtered_ref, sems = rest[2 * matching + 2 :]
        for index in range(matching):
            send(earlier[2 * index], coherence_out.at[index])
            send(earlier[2 * index + 1], filtered_out.at[:, index])
    else:
        coherence_ref, filtered_ref = rest
    height = image_ref.shape[2] // 2
    breadth = image_ref.shape[3]
    patches = height // PATCH + 1
    freqs = patches * PATCH
    blocks = breadth // 128
    grouped = lax.axis_index("acq")
    start = half_of(matching, height)
    shift = REACH - offset_ref[1, matching]
    lane = lax.broadcasted_iota(jnp.int32, (height, 128), 1)
    state = {}

    def block(value, index):
        return value[:, 128 * index : 128 * index + 128]

    def fields(member):
        partner = pairing_ref[matching, 2 * grouped + member] % 2
        ours, theirs = [], []
        for part in range(2):
            ours.append(own_cells(image_ref, rim_ref, part, member, start, height))
            if ("rims", part) not in state:
                rim = block(remote_rim_ref[...], part).astype(F32)
                state["rims", part] = rim, pltpu.roll(rim, 64, 1)
            rim = jnp.where(partner == 1, *state["rims", part][::-1])
            main = remote_ref[2 * part + partner].astype(F32)
            theirs.append(jnp.concatenate([main, rim], axis=1))
        inter_real = ours[0] * theirs[0] + ours[1] * theirs[1]
        inter_imag = ours[1] * theirs[0] - ours[0] * theirs[1]
        power = theirs[0] * theirs[0] + theirs[1] * theirs[1]
        state["fields", member] = [inter_real, inter_imag, power]
        windows = []
        for value in (inter_real, inter_imag):
            turned = [pltpu.roll(block(value, index), shift, 1) for index in range(blocks + 1)]
            windows.append(
                [jnp.where(lane < shift, turned[index - 1], turned[index]) for index in range(blocks + 1)]
            )
        state["window", member] = windows

    def joint(stage, together, member):
        if not together:
            return [(member,)]
        return [(0, 1)] if ("ready " + stage, 1 - member) in state else []

    def columns(member):
        windows = state["window", member]
        groups = [
            jnp.concatenate([part[index] for part in windows], axis=1) for index in range(blocks)
        ]
        if member == 0:
            other = state["window", 1]
            groups.append(
                jnp.concatenate(
                    [
                        jnp.where(
                            lane < PATCH, windows[part][blocks], pltpu.roll(other[part][blocks], PATCH, 1)
                        )
                        for part in range(2)
                    ],
                    axis=1,
                )
            )
        state["ready column", member] = groups
        for members in joint("column", JC, member):
            values = sum((state["ready column", one] for one in members), [])
            found = mm(
                thirds(jnp.concatenate(values, axis=0), 1),
                fold(table_part(table_ref, places["forward"]), 0),
            )
            for one in members:
                count = len(state["ready column", one])
                state["column", one] = jnp.concatenate(
                    [
                        jnp.concatenate(
                            [
                                block(found[height * group : height * group + height], part)
                                for part in range(2)
                            ],
                            axis=0,
                        )
                        for group in range(count)
                    ],
                    axis=1,
                )
                found = found[count * height :]

    def ranges(member):
        state["ready range", member] = state["fields", member]
        for members in joint("range", JR, member):
            values = sum((state["fields", one] for one in members), [])
            found = mm(
                thirds(jnp.concatenate(values, axis=0), 1),
                fold(table_part(table_ref, places["band"]), 0),
            )
            for one in members:
                state["range", one], found = found[: 3 * height], found[3 * height :]

    def coherence(member):
        azimuth = table_part(table_ref, places["azimuth"])
        real, imag, power = [
            along_lines(azimuth, state["range", member], index, height) for index in range(3)
        ]
        own = power_ref[min(matching, 1), member]
        coherence_ref[member] = (real * real + imag * imag) / (own * power + EPSILON)
        if finish:
            send(coherence_ref.at[member], coherence_out.at[matching, member])

    def rows(member):
        state["freq", member] = mm(fold(forward_ref[matching], 1), thirds(state["column", member], 0))

    def scaled(member):
        freq = state["freq", member]
        freq_real, freq_imag = freq[:freqs], freq[freqs:]
        power = freq_real * freq_real + freq_imag * freq_imag + EPSILON
        magnitude = lax.rsqrt(lax.rsqrt(power))

        state["magnitude", member] = magnitude
        state["weighted", member] = jnp.concatenate(
            [freq_real * magnitude, freq_imag * magnitude], axis=0
        )

    def means(member):
        magnitude = state["magnitude", member]
        count = magnitude.shape[1] // 128
        sums = [
            jnp.sum(block(magnitude[PATCH * place : PATCH * place + PATCH], group), axis=0, keepdims=True)
            for group in range(count)
            for place in range(patches)
        ]
        high, low = halves(jnp.concatenate(sums, axis=0))
        same = table_part(table_ref, places["same"])
        totals = mm(high, same) + mm(low, same)
        inverse = 1.0 / (totals * (1.0 / (PATCH * PATCH)) + EPSILON)
        line = lax.broadcasted_iota(jnp.int32, (height, 128), 0)
        patch = (line + PATCH - offset_ref[0, matching]) >> 5
        scales = []
        for group in range(count):
            scale = inverse[group * patches][None]
            for place in range(1, patches):
                scale = jnp.where(patch == place, inverse[group * patches + place][None], scale)
            scales.append(scale)
        state["scale", member] = scales

    def backs(member):
        back = mm(inverse_ref[matching], thirds(state["weighted", member], 0))
        state["back", member] = [
            jnp.concatenate(
                [block(back[height * part : height * part + height], group) for part in (1, 0)], axis=1
            )
            for group in range(back.shape[1] // 128)
        ]

    def inverses(member):
        state["ready final", member] = state["back", member]
        for members in joint("final", JI, member):
            values = sum((state["back", one] for one in members), [])
            found = mm(
                thirds(jnp.concatenate(values, axis=0), 1),
                fold(table_part(table_ref, places["forward"]), 0),
            )
            for one in members:
                count = len(state["back", one])
                state["final", one] = [
                    found[height * group : height * group + height] for group in range(count)
                ]
                found = found[count * height :]

    def outputs(member):
        edge = state["final", 0][blocks]
        edge_scale = state["scale", 0][blocks]
        for part in range(2):
            whole = [
                block(group, 1 - part) * scale
                for group, scale in zip(state["final", member][:blocks], state["scale", member])
            ]
            side = block(edge, 1 - part) * edge_scale
            turned = [pltpu.roll(value, 128 - shift, 1) for value in whole]
            turned.append(pltpu.roll(side, (128 - PATCH if member else 128) - shift, 1))
            cells = [
                jnp.where(lane < 128 - shift, turned[index], turned[index + 1])
                for index in range(blocks)
            ]
            filtered_ref[part, member] = jnp.concatenate(cells, axis=1).astype(BF)
        if finish:
            send(filtered_ref.at[:, member], filtered_out.at[:, matching, member])

    stages = dict(
        F=fields, C=columns, R=ranges, A=coherence, Z=rows, S=scaled, M=means, B=backs, I=inverses, O=outputs
    )
    for step in ORDER:
        stages[step[0]](int(step[1]))
    for copy in copies:
        copy.wait()


def in_hbm(value):
    return pltpu.with_memory_space_constraint(value, pltpu.HBM)


def vmem(count):
    return [pl.BlockSpec(memory_space=pltpu.VMEM)] * count


def match_call(shared, matching, remote, previous):
    pairing, offsets, image, rims, table, forward, inverse, power, places = shared
    height, breadth = image.shape[2] // 2, image.shape[3]
    finish = matching == MATCH - 1
    coherence = pltpu.VMEM((2, height, breadth), F32)
    filtered = pltpu.VMEM((2, 2, height, breadth), BF)
    inputs = [pairing, offsets, image, rims, table, forward, inverse, power, *remote]
    specs = [pl.BlockSpec(memory_space=pltpu.SMEM)] * 2 + vmem(6 + len(remote))
    out_shape, out_specs, scratch = (coherence, filtered), vmem(2), []
    if finish:
        inputs += previous
        specs += vmem(len(previous))
        out_shape = (
            jax.ShapeDtypeStruct((MATCH, 2, height, breadth), F32),
            jax.ShapeDtypeStruct((2, MATCH, 2, height, breadth), BF),
        )
        out_specs = [pl.BlockSpec(memory_space=pl.ANY)] * 2
        scratch = [coherence, filtered, pltpu.SemaphoreType.DMA((2 * matching + 4,))]
    return pl.pallas_call(
        functools.partial(match_kernel, matching, places, finish),
        out_shape=out_shape,
        in_specs=specs,
        out_specs=tuple(out_specs),
        scratch_shapes=scratch,
        cost_estimate=pl.CostEstimate(flops=2 * 10**9, bytes_accessed=3 * 10**6, transcendentals=0),
        compiler_params=GRANT,
    )(*inputs)


def xor_swap(value, mask):
    return lax.ppermute(value, "acq", [(i, i ^ mask) for i in range(lax.axis_size("acq"))])


def neighbour_swap(value, turn):
    places, groups = lax.axis_size("rng"), lax.axis_size("acq")
    pairs = []
    for group in range(groups):
        for place in range(places):
            target = (group ^ 1) * places + place
            if place % 3 == turn and place + 1 < places:
                target = group * places + place + 1
            elif place and (place - 1) % 3 == turn:
                target = group * places + place - 1
            pairs.append((group * places + place, target))
    return lax.ppermute(value, ("acq", "rng"), pairs)


def per_device(images, pairing, tile_offsets):
    lines, breadth = images.shape[2:]
    height = lines // 2
    table, places = all_tables(breadth, height)
    row_table, row_places = line_tables(height)
    table, row_table = jnp.asarray(table), jnp.asarray(row_table)
    side = pltpu.VMEM((lines, 128), BF)
    payload = pltpu.VMEM((5, height, breadth), BF)
    offsets = tile_offsets.T
    mains = pltpu.VMEM((4, height, breadth), BF)
    scalars = [pl.BlockSpec(memory_space=pltpu.SMEM)] * 2
    image, first, second, third, far, pairing, offsets = pl.pallas_call(
        pack_kernel,
        out_shape=(
            pltpu.VMEM(images.shape, BF),
            side,
            side,
            side,
            mains,
            pltpu.SMEM(pairing.shape, jnp.int32),
            pltpu.SMEM(offsets.shape, jnp.int32),
        ),
        in_specs=[pl.BlockSpec(memory_space=pl.ANY)] * 3,
        out_specs=(*vmem(5), *scalars),
        scratch_shapes=[pltpu.SemaphoreType.DMA((3,))],
        cost_estimate=pl.CostEstimate(flops=COST, bytes_accessed=10**6, transcendentals=0),
        compiler_params=GRANT,
        name="pack",
    )(in_hbm(images), in_hbm(pairing), in_hbm(offsets))
    first = neighbour_swap(first, 0)
    second = neighbour_swap(second, 1)
    third = neighbour_swap(third, 2)
    far = xor_swap(far, 2)
    freqs = height + PATCH
    near, forward, inverse = pl.pallas_call(
        functools.partial(main_kernel, row_places),
        out_shape=(
            payload,
            pltpu.VMEM((MATCH, 2 * freqs, 4 * height), BF),
            pltpu.VMEM((MATCH, 2 * height, 6 * freqs), BF),
        ),
        in_specs=[*vmem(1), scalars[0], *vmem(1)],
        out_specs=tuple(vmem(3)),
        cost_estimate=pl.CostEstimate(flops=COST, bytes_accessed=10**6, transcendentals=0),
        compiler_params=GRANT,
        name="mains",
    )(image, offsets, row_table)
    near, far_rims, rims = pl.pallas_call(
        functools.partial(rim_kernel, lax.axis_size("rng") - 1),
        out_shape=(
            payload,
            pltpu.VMEM((height, breadth), BF),
            pltpu.VMEM((2, lines, 128), BF),
        ),
        in_specs=vmem(4),
        out_specs=tuple(vmem(3)),
        input_output_aliases={3: 0},
        compiler_params=GRANT,
        name="rims",
    )(first, second, third, near)
    near = xor_swap(near, 1)
    far_rims = xor_swap(far_rims, 2)
    power = pl.pallas_call(
        functools.partial(power_kernel, places),
        out_shape=pltpu.VMEM((2, 2, height, breadth), F32),
        in_specs=vmem(3),
        out_specs=vmem(1)[0],
        cost_estimate=pl.CostEstimate(flops=10**9, bytes_accessed=10**6, transcendentals=0),
        compiler_params=GRANT,
        name="power",
    )(image, rims, table)
    call = functools.partial(
        match_call, (pairing, offsets, image, rims, table, forward, inverse, power, places)
    )
    outputs = call(0, (near,), ())
    far, far_rims, *outputs = lax.optimization_barrier((far, far_rims, *outputs))
    both = xor_swap(far, 1)
    both_rims = xor_swap(far_rims, 1)
    outputs = [*outputs, *call(1, (far, far_rims), ())]
    return tuple(call(2, (both, both_rims), outputs))


def solution(mesh):
    in_specs = (P(None, ("stack", "acq"), None, "rng"), P(), P())
    out_specs = (
        P(None, ("stack", "acq"), None, "rng"),
        P(None, None, ("stack", "acq"), None, "rng"),
    )

    return jax.shard_map(
        per_device, mesh=mesh, in_specs=in_specs, out_specs=out_specs, check_vma=False
    )
```

```python
import functools

import jax
import jax.numpy as jnp
import numpy as np
from jax import lax
from jax.experimental import pallas as pl
from jax.experimental.pallas import tpu as pltpu
from jax.sharding import PartitionSpec as P

MATCH = 3
REACH = 32
PATCH = 32
EPSILON = 1e-06
BF = jnp.bfloat16
F32 = jnp.float32
GRANT = pltpu.CompilerParams(vmem_limit_bytes=24 << 20)


def split_table(table):
    high = table.astype(np.float32).astype(BF)
    low = (table - high.astype(np.float64)).astype(np.float32).astype(BF)
    return high, low


def gauss(spread):
    width = REACH / 8.0
    weights = np.exp(-(spread.astype(np.float64) ** 2) / (2.0 * width * width))
    return np.where(np.abs(spread) <= REACH, weights, 0.0)


def stacked(table, copies=1):
    high, low = split_table(table)
    return np.concatenate([high] * copies + [low], axis=0)


def range_table(breadth):
    lanes = breadth + 128
    row = np.arange(lanes)
    cell = np.where(row < breadth + REACH, row, row - lanes)
    band = gauss(cell[:, None] - np.arange(breadth)[None, :])
    valid = (row < breadth + REACH) | (row >= lanes - REACH)
    return stacked(band * valid[:, None])


def azimuth_table(height):
    line = np.arange(height)
    return stacked(gauss(line[:, None] - line[None, :]), 2).T


def waves(rows, cols):
    angle = 2.0 * np.pi / PATCH * ((rows[:, None] * cols[None, :]) % PATCH)
    return np.cos(angle), np.sin(angle)


def column_tables():
    lane = np.arange(128)
    same = (lane[:, None] // PATCH) == (lane[None, :] // PATCH)
    cosine, sine = waves(lane % PATCH, lane % PATCH)
    cosine, sine = cosine * same, sine * same
    forward = np.block([[cosine, -sine], [sine, cosine]])
    return stacked(forward), same.astype(np.float32).astype(BF)


def row_tables(height):
    patches = height // PATCH + 1
    freq = np.arange(patches * PATCH) % PATCH
    cosine, sine = waves(freq, np.arange(height))
    forward = np.block([[cosine, sine], [-sine, cosine]])
    return stacked(forward.T).T, stacked(forward / (PATCH * PATCH), 2).T


def laid_out(parts):
    places, rows, start = {}, [], 0
    for name, part in parts.items():
        tall = -(-part.shape[0] // 16) * 16
        places[name] = []
        for first in range(0, part.shape[1], 256):
            piece = part[:, first : first + 256]
            block = np.zeros((tall, 256), BF)
            block[: piece.shape[0], : piece.shape[1]] = piece
            places[name].append((start, *piece.shape))
            rows.append(block)
            start += tall
    return np.concatenate(rows, axis=0), places


def all_tables(breadth, height):
    parts = {"band": range_table(breadth), "azimuth": azimuth_table(height)}
    parts["forward"], parts["same"] = column_tables()
    return laid_out(parts)


def line_tables(height):
    forward, inverse = row_tables(height)
    return laid_out({"row_forward": forward, "row_inverse": inverse})


def halves(value):
    high = value.astype(BF)
    return high, (value - high.astype(F32)).astype(BF)


def thirds(value, axis):
    high, low = halves(value)
    return jnp.concatenate([high, low, high], axis=axis)


def fold(table, axis):
    high, low = jnp.split(table, 2, axis=axis)
    return jnp.concatenate([high, high, low], axis=axis)


def mm(left, right):
    return jnp.dot(left, right, preferred_element_type=F32)


def lane_group(shape):
    return lax.broadcasted_iota(jnp.int32, shape, 1) >> 5


def kind_of(place):
    return (place + 3) % 3


def outgoing(mask, height):
    grouped = lax.axis_index("acq")
    upper = (grouped > jnp.bitwise_xor(grouped, mask)).astype(jnp.int32)
    return pl.multiple_of((1 - upper) * height, height)


def pack_kernel(
    source_ref,
    pairing_source,
    offset_source,
    image_ref,
    first_ref,
    second_ref,
    third_ref,
    far_ref,
    pairing_ref,
    offset_ref,
    sem,
):
    copies = [
        pltpu.make_async_copy(source_ref, image_ref, sem.at[0]),
        pltpu.make_async_copy(pairing_source, pairing_ref, sem.at[1]),
        pltpu.make_async_copy(offset_source, offset_ref, sem.at[2]),
    ]
    for copy in copies:
        copy.start()
    copies[0].wait()
    breadth = image_ref.shape[3]
    group = lane_group((image_ref.shape[2], 128))
    sides = []
    for first, order in (
        (breadth - 128, ((1, 1, 32), (0, 1, 64), (1, 0, 96), (0, 0, 0))),
        (0, ((0, 0, 0), (1, 1, 32), (0, 1, 64), (1, 0, 96))),
    ):
        value = None
        for position, (part, member, shift) in enumerate(order):
            cells = image_ref[part, member, :, first : first + 128].astype(F32)
            cells = pltpu.roll(cells, shift, 1) if shift else cells
            value = cells if value is None else jnp.where(group == position, cells, value)
        sides.append(value)
    tail, head = sides
    kind = kind_of(lax.axis_index("rng"))
    for turn, target in enumerate((first_ref, second_ref, third_ref)):
        target[...] = jnp.where(kind == turn, tail, head).astype(BF)
    height = image_ref.shape[2] // 2
    fill(far_ref, image_ref, outgoing(2, height), height)
    for copy in copies[1:]:
        copy.wait()


def fill(target, image_ref, start, height):
    for part in range(2):
        for member in range(2):
            target[2 * part + member] = image_ref[part, member, pl.ds(start, height), :]


def row_mask(height, row_offset, freq_dim, thrice):
    freqs = height + PATCH
    rows, cols = 2 * height, 2 * freqs
    if freq_dim == 0:
        line = lax.broadcasted_iota(jnp.int32, (PATCH, rows), 1) & (height - 1)
        patch = (line + PATCH - row_offset) >> 5
        keep = jnp.concatenate(
            [jnp.where(patch == place, 1.0, 0.0).astype(BF) for place in range(freqs // PATCH)] * 2,
            axis=0,
        )
        return jnp.concatenate([keep] * thrice, axis=1)
    line = lax.broadcasted_iota(jnp.int32, (rows, thrice * cols), 0) & (height - 1)
    lane = lax.broadcasted_iota(jnp.int32, (8, thrice * cols), 1)
    for step in (4, 2, 1):
        lane = jnp.where(lane >= step * freqs, lane - step * freqs, lane)
    keep = ((line + PATCH - row_offset) >> 5) == (lane >> 5)[:1]
    return jnp.where(keep, 1.0, 0.0).astype(BF)


def table_part(table_ref, pieces):
    pieces = [table_ref[first : first + rows, :cols] for first, rows, cols in pieces]
    return jnp.concatenate(pieces, axis=1) if len(pieces) > 1 else pieces[0]


def main_kernel(places, image_ref, offset_ref, row_ref, near_ref, forward_ref, inverse_ref):
    height = image_ref.shape[2] // 2
    fill(near_ref, image_ref, outgoing(1, height), height)
    row_forward = table_part(row_ref, places["row_forward"])
    row_inverse = table_part(row_ref, places["row_inverse"])
    for matching in range(MATCH):
        row_offset = offset_ref[0, matching]
        forward_ref[matching] = row_forward * row_mask(height, row_offset, 0, 2)
        inverse_ref[matching] = row_inverse * row_mask(height, row_offset, 1, 3)


def rim_kernel(ends, first_ref, second_ref, third_ref, near_in, near_ref, far_ref, rim_ref):
    height = far_ref.shape[0]
    place = lax.axis_index("rng")
    turns = [ref[...].astype(F32) for ref in (first_ref, second_ref, third_ref)]

    def taken(kind):
        return jnp.where(kind == 0, turns[0], jnp.where(kind == 1, turns[1], turns[2]))

    head = jnp.where(place < ends, taken(kind_of(place)), 0.0)
    tail = jnp.where(place > 0, taken(kind_of(place - 1)), 0.0)
    odd = (lane_group(tail.shape) & 1) == 1
    rim_ref[0] = jnp.where(odd, tail, head).astype(BF)
    rim_ref[1] = pltpu.roll(jnp.where(odd, head, tail), 32, 1).astype(BF)
    for target, mask in ((near_ref.at[4], 1), (far_ref, 2)):
        start = outgoing(mask, height)
        for part in range(2):
            target[:, 128 * part : 128 * part + 128] = rim_ref[part, pl.ds(start, height), :]


def merge_kernel(main_ref, rim_ref, both_ref):
    both_ref[:4] = main_ref[...]
    both_ref[4] = rim_ref[...]


def half_of(matching, height):
    grouped = lax.axis_index("acq")
    upper = (grouped > jnp.bitwise_xor(grouped, matching + 1)).astype(jnp.int32)
    return pl.multiple_of(upper * height, height)


def own_cells(image_ref, rim_ref, part, member, start, height):
    rim = rim_ref[part, pl.ds(start, height), :].astype(F32)
    if member:
        rim = pltpu.roll(rim, 64, 1)
    main = image_ref[part, member, pl.ds(start, height), :].astype(F32)
    return jnp.concatenate([main, rim], axis=1)


def along_lines(azimuth, ranged, index, height):
    return mm(azimuth, thirds(ranged[index * height : index * height + height], 0))


def power_kernel(places, image_ref, rim_ref, table_ref, power_ref):
    height = image_ref.shape[2] // 2
    fields = []
    for matching in range(2):
        for member in range(2):
            real, imag = [
                own_cells(image_ref, rim_ref, part, member, half_of(matching, height), height)
                for part in range(2)
            ]
            fields.append(real * real + imag * imag)
    azimuth = table_part(table_ref, places["azimuth"])
    ranged = [
        mm(
            thirds(jnp.concatenate(fields[first : first + 2], axis=0), 1),
            fold(table_part(table_ref, places["band"]), 0),
        )
        for first in (0, 2)
    ]
    for index in range(2):
        for matching in range(2):
            power_ref[matching, index] = along_lines(azimuth, ranged[matching], index, height)


COST = 4 * 10**9
JC, JR, JI = True, True, False
ORDER = (
    "F0", "F1", "R1", "C0", "C1", "R0", "Z0", "A1", "S0", "Z1",
    "S1", "B0", "B1", "M1", "M0", "A0", "I0", "I1", "O1", "O0",
)


def match_kernel(
    matching,
    places,
    finish,
    pairing_ref,
    offset_ref,
    image_ref,
    rim_ref,
    table_ref,
    forward_ref,
    inverse_ref,
    power_ref,
    remote_ref,
    *rest,
):
    if matching == 1:
        remote_rim_ref, *rest = rest
    else:
        remote_rim_ref = remote_ref.at[4]
    copies = []

    def send(source, target):
        copy = pltpu.make_async_copy(source, target, sems.at[len(copies)])
        copy.start()
        copies.append(copy)

    if finish:
        earlier, (coherence_out, filtered_out) = rest[: 2 * matching], rest[2 * matching :][:2]
        coherence_ref, filtered_ref, sems = rest[2 * matching + 2 :]
        for index in range(matching):
            send(earlier[2 * index], coherence_out.at[index])
            send(earlier[2 * index + 1], filtered_out.at[:, index])
    else:
        coherence_ref, filtered_ref = rest
    height = image_ref.shape[2] // 2
    breadth = image_ref.shape[3]
    patches = height // PATCH + 1
    freqs = patches * PATCH
    blocks = breadth // 128
    grouped = lax.axis_index("acq")
    start = half_of(matching, height)
    shift = REACH - offset_ref[1, matching]
    lane = lax.broadcasted_iota(jnp.int32, (height, 128), 1)
    state = {}

    def block(value, index):
        return value[:, 128 * index : 128 * index + 128]

    def fields(member):
        partner = pairing_ref[matching, 2 * grouped + member] % 2
        ours, theirs = [], []
        for part in range(2):
            ours.append(own_cells(image_ref, rim_ref, part, member, start, height))
            if ("rims", part) not in state:
                rim = block(remote_rim_ref[...], part).astype(F32)
                state["rims", part] = rim, pltpu.roll(rim, 64, 1)
            rim = jnp.where(partner == 1, *state["rims", part][::-1])
            main = remote_ref[2 * part + partner].astype(F32)
            theirs.append(jnp.concatenate([main, rim], axis=1))
        inter_real = ours[0] * theirs[0] + ours[1] * theirs[1]
        inter_imag = ours[1] * theirs[0] - ours[0] * theirs[1]
        power = theirs[0] * theirs[0] + theirs[1] * theirs[1]
        state["fields", member] = [inter_real, inter_imag, power]
        windows = []
        for value in (inter_real, inter_imag):
            turned = [pltpu.roll(block(value, index), shift, 1) for index in range(blocks + 1)]
            windows.append(
                [jnp.where(lane < shift, turned[index - 1], turned[index]) for index in range(blocks + 1)]
            )
        state["window", member] = windows

    def joint(stage, together, member):
        if not together:
            return [(member,)]
        return [(0, 1)] if ("ready " + stage, 1 - member) in state else []

    def columns(member):
        windows = state["window", member]
        groups = [
            jnp.concatenate([part[index] for part in windows], axis=1) for index in range(blocks)
        ]
        if member == 0:
            other = state["window", 1]
            groups.append(
                jnp.concatenate(
                    [
                        jnp.where(
                            lane < PATCH, windows[part][blocks], pltpu.roll(other[part][blocks], PATCH, 1)
                        )
                        for part in range(2)
                    ],
                    axis=1,
                )
            )
        state["ready column", member] = groups
        for members in joint("column", JC, member):
            values = sum((state["ready column", one] for one in members), [])
            found = mm(
                thirds(jnp.concatenate(values, axis=0), 1),
                fold(table_part(table_ref, places["forward"]), 0),
            )
            for one in members:
                count = len(state["ready column", one])
                state["column", one] = jnp.concatenate(
                    [
                        jnp.concatenate(
                            [
                                block(found[height * group : height * group + height], part)
                                for part in range(2)
                            ],
                            axis=0,
                        )
                        for group in range(count)
                    ],
                    axis=1,
                )
                found = found[count * height :]

    def ranges(member):
        state["ready range", member] = state["fields", member]
        for members in joint("range", JR, member):
            values = sum((state["fields", one] for one in members), [])
            found = mm(
                thirds(jnp.concatenate(values, axis=0), 1),
                fold(table_part(table_ref, places["band"]), 0),
            )
            for one in members:
                state["range", one], found = found[: 3 * height], found[3 * height :]

    def coherence(member):
        azimuth = table_part(table_ref, places["azimuth"])
        real, imag, power = [
            along_lines(azimuth, state["range", member], index, height) for index in range(3)
        ]
        own = power_ref[min(matching, 1), member]
        coherence_ref[member] = (real * real + imag * imag) / (own * power + EPSILON)
        if finish:
            send(coherence_ref.at[member], coherence_out.at[matching, member])

    def rows(member):
        state["freq", member] = mm(fold(forward_ref[matching], 1), thirds(state["column", member], 0))

    def scaled(member):
        freq = state["freq", member]
        freq_real, freq_imag = freq[:freqs], freq[freqs:]
        power = freq_real * freq_real + freq_imag * freq_imag + EPSILON
        magnitude = lax.rsqrt(lax.rsqrt(power))

        state["magnitude", member] = magnitude
        state["weighted", member] = jnp.concatenate(
            [freq_real * magnitude, freq_imag * magnitude], axis=0
        )

    def means(member):
        magnitude = state["magnitude", member]
        count = magnitude.shape[1] // 128
        sums = [
            jnp.sum(block(magnitude[PATCH * place : PATCH * place + PATCH], group), axis=0, keepdims=True)
            for group in range(count)
            for place in range(patches)
        ]
        high, low = halves(jnp.concatenate(sums, axis=0))
        same = table_part(table_ref, places["same"])
        totals = mm(high, same) + mm(low, same)
        inverse = 1.0 / (totals * (1.0 / (PATCH * PATCH)) + EPSILON)
        line = lax.broadcasted_iota(jnp.int32, (height, 128), 0)
        patch = (line + PATCH - offset_ref[0, matching]) >> 5
        scales = []
        for group in range(count):
            scale = inverse[group * patches][None]
            for place in range(1, patches):
                scale = jnp.where(patch == place, inverse[group * patches + place][None], scale)
            scales.append(scale)
        state["scale", member] = scales

    def backs(member):
        back = mm(inverse_ref[matching], thirds(state["weighted", member], 0))
        state["back", member] = [
            jnp.concatenate(
                [block(back[height * part : height * part + height], group) for part in (1, 0)], axis=1
            )
            for group in range(back.shape[1] // 128)
        ]

    def inverses(member):
        state["ready final", member] = state["back", member]
        for members in joint("final", JI, member):
            values = sum((state["back", one] for one in members), [])
            found = mm(
                thirds(jnp.concatenate(values, axis=0), 1),
                fold(table_part(table_ref, places["forward"]), 0),
            )
            for one in members:
                count = len(state["back", one])
                state["final", one] = [
                    found[height * group : height * group + height] for group in range(count)
                ]
                found = found[count * height :]

    def outputs(member):
        edge = state["final", 0][blocks]
        edge_scale = state["scale", 0][blocks]
        for part in range(2):
            whole = [
                block(group, 1 - part) * scale
                for group, scale in zip(state["final", member][:blocks], state["scale", member])
            ]
            side = block(edge, 1 - part) * edge_scale
            turned = [pltpu.roll(value, 128 - shift, 1) for value in whole]
            turned.append(pltpu.roll(side, (128 - PATCH if member else 128) - shift, 1))
            cells = [
                jnp.where(lane < 128 - shift, turned[index], turned[index + 1])
                for index in range(blocks)
            ]
            filtered_ref[part, member] = jnp.concatenate(cells, axis=1).astype(BF)
        if finish:
            send(filtered_ref.at[:, member], filtered_out.at[:, matching, member])

    stages = dict(
        F=fields, C=columns, R=ranges, A=coherence, Z=rows, S=scaled, M=means, B=backs, I=inverses, O=outputs
    )
    for step in ORDER:
        stages[step[0]](int(step[1]))
    for copy in copies:
        copy.wait()


def in_hbm(value):
    return pltpu.with_memory_space_constraint(value, pltpu.HBM)


def vmem(count):
    return [pl.BlockSpec(memory_space=pltpu.VMEM)] * count


def match_call(shared, matching, remote, previous):
    pairing, offsets, image, rims, table, forward, inverse, power, places = shared
    height, breadth = image.shape[2] // 2, image.shape[3]
    finish = matching == MATCH - 1
    coherence = pltpu.VMEM((2, height, breadth), F32)
    filtered = pltpu.VMEM((2, 2, height, breadth), BF)
    inputs = [pairing, offsets, image, rims, table, forward, inverse, power, *remote]
    specs = [pl.BlockSpec(memory_space=pltpu.SMEM)] * 2 + vmem(6 + len(remote))
    out_shape, out_specs, scratch = (coherence, filtered), vmem(2), []
    if finish:
        inputs += previous
        specs += vmem(len(previous))
        out_shape = (
            jax.ShapeDtypeStruct((MATCH, 2, height, breadth), F32),
            jax.ShapeDtypeStruct((2, MATCH, 2, height, breadth), BF),
        )
        out_specs = [pl.BlockSpec(memory_space=pl.ANY)] * 2
        scratch = [coherence, filtered, pltpu.SemaphoreType.DMA((2 * matching + 4,))]
    return pl.pallas_call(
        functools.partial(match_kernel, matching, places, finish),
        out_shape=out_shape,
        in_specs=specs,
        out_specs=tuple(out_specs),
        scratch_shapes=scratch,
        cost_estimate=pl.CostEstimate(flops=2 * 10**9, bytes_accessed=3 * 10**6, transcendentals=0),
        compiler_params=GRANT,
    )(*inputs)


def xor_swap(value, mask):
    return lax.ppermute(value, "acq", [(i, i ^ mask) for i in range(lax.axis_size("acq"))])


def neighbour_swap(value, turn):
    places, groups = lax.axis_size("rng"), lax.axis_size("acq")
    pairs = []
    for group in range(groups):
        for place in range(places):
            target = (group ^ 1) * places + place
            if place % 3 == turn and place + 1 < places:
                target = group * places + place + 1
            elif place and (place - 1) % 3 == turn:
                target = group * places + place - 1
            pairs.append((group * places + place, target))
    return lax.ppermute(value, ("acq", "rng"), pairs)


def per_device(images, pairing, tile_offsets):
    lines, breadth = images.shape[2:]
    height = lines // 2
    table, places = all_tables(breadth, height)
    row_table, row_places = line_tables(height)
    table, row_table = jnp.asarray(table), jnp.asarray(row_table)
    side = pltpu.VMEM((lines, 128), BF)
    payload = pltpu.VMEM((5, height, breadth), BF)
    offsets = tile_offsets.T
    mains = pltpu.VMEM((4, height, breadth), BF)
    scalars = [pl.BlockSpec(memory_space=pltpu.SMEM)] * 2
    image, first, second, third, far, pairing, offsets = pl.pallas_call(
        pack_kernel,
        out_shape=(
            pltpu.VMEM(images.shape, BF),
            side,
            side,
            side,
            mains,
            pltpu.SMEM(pairing.shape, jnp.int32),
            pltpu.SMEM(offsets.shape, jnp.int32),
        ),
        in_specs=[pl.BlockSpec(memory_space=pl.ANY)] * 3,
        out_specs=(*vmem(5), *scalars),
        scratch_shapes=[pltpu.SemaphoreType.DMA((3,))],
        cost_estimate=pl.CostEstimate(flops=COST, bytes_accessed=10**6, transcendentals=0),
        compiler_params=GRANT,
        name="pack",
    )(in_hbm(images), in_hbm(pairing), in_hbm(offsets))
    first = neighbour_swap(first, 0)
    second = neighbour_swap(second, 1)
    third = neighbour_swap(third, 2)
    far = xor_swap(far, 2)
    freqs = height + PATCH
    near, forward, inverse = pl.pallas_call(
        functools.partial(main_kernel, row_places),
        out_shape=(
            payload,
            pltpu.VMEM((MATCH, 2 * freqs, 4 * height), BF),
            pltpu.VMEM((MATCH, 2 * height, 6 * freqs), BF),
        ),
        in_specs=[*vmem(1), scalars[0], *vmem(1)],
        out_specs=tuple(vmem(3)),
        cost_estimate=pl.CostEstimate(flops=COST, bytes_accessed=10**6, transcendentals=0),
        compiler_params=GRANT,
        name="mains",
    )(image, offsets, row_table)
    near, far_rims, rims = pl.pallas_call(
        functools.partial(rim_kernel, lax.axis_size("rng") - 1),
        out_shape=(
            payload,
            pltpu.VMEM((height, breadth), BF),
            pltpu.VMEM((2, lines, 128), BF),
        ),
        in_specs=vmem(4),
        out_specs=tuple(vmem(3)),
        input_output_aliases={3: 0},
        compiler_params=GRANT,
        name="rims",
    )(first, second, third, near)
    near = xor_swap(near, 1)
    far_rims = xor_swap(far_rims, 2)
    power = pl.pallas_call(
        functools.partial(power_kernel, places),
        out_shape=pltpu.VMEM((2, 2, height, breadth), F32),
        in_specs=vmem(3),
        out_specs=vmem(1)[0],
        cost_estimate=pl.CostEstimate(flops=10**9, bytes_accessed=10**6, transcendentals=0),
        compiler_params=GRANT,
        name="power",
    )(image, rims, table)
    call = functools.partial(
        match_call, (pairing, offsets, image, rims, table, forward, inverse, power, places)
    )
    outputs = call(0, (near,), ())
    far, far_rims, *outputs = lax.optimization_barrier((far, far_rims, *outputs))
    both = pl.pallas_call(
        merge_kernel,
        out_shape=payload,
        in_specs=vmem(2),
        out_specs=vmem(1)[0],
        compiler_params=GRANT,
        name="merge",
    )(far, far_rims)
    both = xor_swap(both, 1)
    outputs = [*outputs, *call(1, (far, far_rims), ())]
    return tuple(call(2, (both,), outputs))


def solution(mesh):
    in_specs = (P(None, ("stack", "acq"), None, "rng"), P(), P())
    out_specs = (
        P(None, ("stack", "acq"), None, "rng"),
        P(None, None, ("stack", "acq"), None, "rng"),
    )

    return jax.shard_map(
        per_device, mesh=mesh, in_specs=in_specs, out_specs=out_specs, check_vma=False
    )
```

```python
import functools

import jax
import jax.numpy as jnp
import numpy as np
from jax import lax
from jax.experimental import pallas as pl
from jax.experimental.pallas import tpu as pltpu
from jax.sharding import PartitionSpec as P

MATCH = 3
REACH = 32
PATCH = 32
EPSILON = 1e-06
BF = jnp.bfloat16
F32 = jnp.float32
GRANT = pltpu.CompilerParams(vmem_limit_bytes=24 << 20)


def split_table(table):
    high = table.astype(np.float32).astype(BF)
    low = (table - high.astype(np.float64)).astype(np.float32).astype(BF)
    return high, low


def gauss(spread):
    width = REACH / 8.0
    weights = np.exp(-(spread.astype(np.float64) ** 2) / (2.0 * width * width))
    return np.where(np.abs(spread) <= REACH, weights, 0.0)


def stacked(table, copies=1):
    high, low = split_table(table)
    return np.concatenate([high] * copies + [low], axis=0)


def range_table(breadth):
    lanes = breadth + 128
    row = np.arange(lanes)
    cell = np.where(row < breadth + REACH, row, row - lanes)
    band = gauss(cell[:, None] - np.arange(breadth)[None, :])
    valid = (row < breadth + REACH) | (row >= lanes - REACH)
    return stacked(band * valid[:, None])


def azimuth_table(height):
    line = np.arange(height)
    return stacked(gauss(line[:, None] - line[None, :]), 2).T


def waves(rows, cols):
    angle = 2.0 * np.pi / PATCH * ((rows[:, None] * cols[None, :]) % PATCH)
    return np.cos(angle), np.sin(angle)


def column_tables():
    lane = np.arange(128)
    same = (lane[:, None] // PATCH) == (lane[None, :] // PATCH)
    cosine, sine = waves(lane % PATCH, lane % PATCH)
    cosine, sine = cosine * same, sine * same
    forward = np.block([[cosine, -sine], [sine, cosine]])
    return stacked(forward), same.astype(np.float32).astype(BF)


def row_tables(height):
    patches = height // PATCH + 1
    freq = np.arange(patches * PATCH) % PATCH
    cosine, sine = waves(freq, np.arange(height))
    forward = np.block([[cosine, sine], [-sine, cosine]])
    return stacked(forward.T).T, stacked(forward / (PATCH * PATCH), 2).T


def laid_out(parts):
    places, rows, start = {}, [], 0
    for name, part in parts.items():
        tall = -(-part.shape[0] // 16) * 16
        places[name] = []
        for first in range(0, part.shape[1], 256):
            piece = part[:, first : first + 256]
            block = np.zeros((tall, 256), BF)
            block[: piece.shape[0], : piece.shape[1]] = piece
            places[name].append((start, *piece.shape))
            rows.append(block)
            start += tall
    return np.concatenate(rows, axis=0), places


def all_tables(breadth, height):
    parts = {"band": range_table(breadth), "azimuth": azimuth_table(height)}
    parts["forward"], parts["same"] = column_tables()
    return laid_out(parts)


def line_tables(height):
    forward, inverse = row_tables(height)
    return laid_out({"row_forward": forward, "row_inverse": inverse})


def halves(value):
    high = value.astype(BF)
    return high, (value - high.astype(F32)).astype(BF)


def thirds(value, axis):
    high, low = halves(value)
    return jnp.concatenate([low, high, high], axis=axis)


def fold(table, axis):
    high, low = jnp.split(table, 2, axis=axis)
    return jnp.concatenate([high, high, low], axis=axis)


def mm(left, right):
    return jnp.dot(left, right, preferred_element_type=F32)


def lane_group(shape):
    return lax.broadcasted_iota(jnp.int32, shape, 1) >> 5


def kind_of(place):
    return (place + 3) % 3


def outgoing(mask, height):
    grouped = lax.axis_index("acq")
    upper = (grouped > jnp.bitwise_xor(grouped, mask)).astype(jnp.int32)
    return pl.multiple_of((1 - upper) * height, height)


def pack_kernel(
    source_ref,
    pairing_source,
    offset_source,
    image_ref,
    first_ref,
    second_ref,
    third_ref,
    far_ref,
    pairing_ref,
    offset_ref,
    sem,
):
    copies = [
        pltpu.make_async_copy(pairing_source, pairing_ref, sem.at[1]),
        pltpu.make_async_copy(offset_source, offset_ref, sem.at[2]),
        pltpu.make_async_copy(source_ref, image_ref, sem.at[0]),
    ]
    for copy in copies:
        copy.start()
    copies[2].wait()
    breadth = image_ref.shape[3]
    group = lane_group((image_ref.shape[2], 128))
    sides = []
    for first, order in (
        (breadth - 128, ((1, 1, 32), (0, 1, 64), (1, 0, 96), (0, 0, 0))),
        (0, ((0, 0, 0), (1, 1, 32), (0, 1, 64), (1, 0, 96))),
    ):
        value = None
        for position, (part, member, shift) in enumerate(order):
            cells = image_ref[part, member, :, first : first + 128].astype(F32)
            cells = pltpu.roll(cells, shift, 1) if shift else cells
            value = cells if value is None else jnp.where(group == position, cells, value)
        sides.append(value)
    tail, head = sides
    kind = kind_of(lax.axis_index("rng"))
    for turn, target in enumerate((first_ref, second_ref, third_ref)):
        target[...] = jnp.where(kind == turn, tail, head).astype(BF)
    height = image_ref.shape[2] // 2
    fill(far_ref, image_ref, outgoing(2, height), height)
    for copy in copies[:2]:
        copy.wait()


def fill(target, image_ref, start, height):
    for part in range(2):
        for member in range(2):
            target[2 * part + member] = image_ref[part, member, pl.ds(start, height), :]


def row_mask(height, row_offset, freq_dim, thrice):
    freqs = height + PATCH
    rows, cols = 2 * height, 2 * freqs
    if freq_dim == 0:
        line = lax.broadcasted_iota(jnp.int32, (PATCH, rows), 1) & (height - 1)
        patch = (line + PATCH - row_offset) >> 5
        keep = jnp.concatenate(
            [jnp.where(patch == place, 1.0, 0.0).astype(BF) for place in range(freqs // PATCH)] * 2,
            axis=0,
        )
        return jnp.concatenate([keep] * thrice, axis=1)
    line = lax.broadcasted_iota(jnp.int32, (rows, thrice * cols), 0) & (height - 1)
    lane = lax.broadcasted_iota(jnp.int32, (8, thrice * cols), 1)
    for step in (4, 2, 1):
        lane = jnp.where(lane >= step * freqs, lane - step * freqs, lane)
    keep = ((line + PATCH - row_offset) >> 5) == (lane >> 5)[:1]
    return jnp.where(keep, 1.0, 0.0).astype(BF)


def table_part(table_ref, pieces):
    pieces = [table_ref[first : first + rows, :cols] for first, rows, cols in pieces]
    return jnp.concatenate(pieces, axis=1) if len(pieces) > 1 else pieces[0]


def main_kernel(places, image_ref, offset_ref, row_ref, near_ref, forward_ref, inverse_ref):
    height = image_ref.shape[2] // 2
    fill(near_ref, image_ref, outgoing(1, height), height)
    row_forward = table_part(row_ref, places["row_forward"])
    row_inverse = table_part(row_ref, places["row_inverse"])
    for matching in range(MATCH):
        row_offset = offset_ref[0, matching]
        forward_ref[matching] = row_forward * row_mask(height, row_offset, 0, 2)
        inverse_ref[matching] = row_inverse * row_mask(height, row_offset, 1, 3)


def rim_kernel(ends, first_ref, second_ref, third_ref, near_in, near_ref, far_ref, rim_ref):
    height = far_ref.shape[0]
    place = lax.axis_index("rng")
    turns = [ref[...].astype(F32) for ref in (first_ref, second_ref, third_ref)]

    def taken(kind):
        return jnp.where(kind == 0, turns[0], jnp.where(kind == 1, turns[1], turns[2]))

    head = jnp.where(place < ends, taken(kind_of(place)), 0.0)
    tail = jnp.where(place > 0, taken(kind_of(place - 1)), 0.0)
    odd = (lane_group(tail.shape) & 1) == 1
    rim_ref[0] = jnp.where(odd, tail, head).astype(BF)
    rim_ref[1] = pltpu.roll(jnp.where(odd, head, tail), 32, 1).astype(BF)
    for target, mask in ((near_ref.at[4], 1), (far_ref, 2)):
        start = outgoing(mask, height)
        for part in range(2):
            target[:, 128 * part : 128 * part + 128] = rim_ref[part, pl.ds(start, height), :]


def merge_main_kernel(main_ref, both_ref):
    both_ref[:4] = main_ref[...]


def merge_rim_kernel(both_in, rim_ref, both_ref):
    both_ref[4] = rim_ref[...]


def half_of(matching, height):
    grouped = lax.axis_index("acq")
    upper = (grouped > jnp.bitwise_xor(grouped, matching + 1)).astype(jnp.int32)
    return pl.multiple_of(upper * height, height)


def own_cells(image_ref, rim_ref, part, member, start, height):
    rim = rim_ref[part, pl.ds(start, height), :].astype(F32)
    if member:
        rim = pltpu.roll(rim, 64, 1)
    main = image_ref[part, member, pl.ds(start, height), :].astype(F32)
    return jnp.concatenate([main, rim], axis=1)


def along_lines(azimuth, ranged, index, height):
    return mm(azimuth, thirds(ranged[index * height : index * height + height], 0))


def power_kernel(places, image_ref, rim_ref, table_ref, power_ref):
    height = image_ref.shape[2] // 2
    fields = []
    for matching in range(2):
        for member in range(2):
            real, imag = [
                own_cells(image_ref, rim_ref, part, member, half_of(matching, height), height)
                for part in range(2)
            ]
            fields.append(real * real + imag * imag)
    azimuth = table_part(table_ref, places["azimuth"])
    ranged = [
        mm(
            thirds(jnp.concatenate(fields[first : first + 2], axis=0), 1),
            fold(table_part(table_ref, places["band"]), 0),
        )
        for first in (0, 2)
    ]
    for index in range(2):
        for matching in range(2):
            power_ref[matching, index] = along_lines(azimuth, ranged[matching], index, height)


COST = 4 * 10**9
JC, JR, JI = True, True, False
ORDER = (
    "F0", "F1", "R1", "C1", "R0", "C0", "Z0", "A1", "S0", "Z1",
    "S1", "B0", "B1", "M1", "M0", "A0", "I0", "I1", "O1", "O0",
)


def match_kernel(
    matching,
    places,
    finish,
    pairing_ref,
    offset_ref,
    image_ref,
    rim_ref,
    table_ref,
    forward_ref,
    inverse_ref,
    power_ref,
    remote_ref,
    *rest,
):
    if matching == 1:
        remote_rim_ref, *rest = rest
    else:
        remote_rim_ref = remote_ref.at[4]
    copies = []

    def send(source, target):
        copy = pltpu.make_async_copy(source, target, sems.at[len(copies)])
        copy.start()
        copies.append(copy)

    if finish:
        earlier, (coherence_out, filtered_out) = rest[: 2 * matching], rest[2 * matching :][:2]
        coherence_ref, filtered_ref, sems = rest[2 * matching + 2 :]
        for index in range(matching):
            send(earlier[2 * index], coherence_out.at[index])
            send(earlier[2 * index + 1], filtered_out.at[:, index])
    else:
        coherence_ref, filtered_ref = rest
    height = image_ref.shape[2] // 2
    breadth = image_ref.shape[3]
    patches = height // PATCH + 1
    freqs = patches * PATCH
    blocks = breadth // 128
    grouped = lax.axis_index("acq")
    start = half_of(matching, height)
    shift = REACH - offset_ref[1, matching]
    lane = lax.broadcasted_iota(jnp.int32, (height, 128), 1)
    state = {}

    def block(value, index):
        return value[:, 128 * index : 128 * index + 128]

    def fields(member):
        partner = pairing_ref[matching, 2 * grouped + member] % 2
        ours, theirs = [], []
        for part in range(2):
            ours.append(own_cells(image_ref, rim_ref, part, member, start, height))
            if ("rims", part) not in state:
                rim = block(remote_rim_ref[...], part).astype(F32)
                state["rims", part] = rim, pltpu.roll(rim, 64, 1)
            rim = jnp.where(partner == 1, *state["rims", part][::-1])
            main = remote_ref[2 * part + partner].astype(F32)
            theirs.append(jnp.concatenate([main, rim], axis=1))
        inter_real = ours[0] * theirs[0] + ours[1] * theirs[1]
        inter_imag = ours[1] * theirs[0] - ours[0] * theirs[1]
        power = theirs[0] * theirs[0] + theirs[1] * theirs[1]
        state["fields", member] = [inter_real, inter_imag, power]
        windows = []
        for value in (inter_real, inter_imag):
            turned = [pltpu.roll(block(value, index), shift, 1) for index in range(blocks + 1)]
            windows.append(
                [jnp.where(lane < shift, turned[index - 1], turned[index]) for index in range(blocks + 1)]
            )
        state["window", member] = windows

    def joint(stage, together, member):
        if not together:
            return [(member,)]
        return [(0, 1)] if ("ready " + stage, 1 - member) in state else []

    def columns(member):
        windows = state["window", member]
        groups = [
            jnp.concatenate([part[index] for part in windows], axis=1) for index in range(blocks)
        ]
        if member == 0:
            other = state["window", 1]
            groups.append(
                jnp.concatenate(
                    [
                        jnp.where(
                            lane < PATCH, windows[part][blocks], pltpu.roll(other[part][blocks], PATCH, 1)
                        )
                        for part in range(2)
                    ],
                    axis=1,
                )
            )
        state["ready column", member] = groups
        for members in joint("column", JC, member):
            values = sum((state["ready column", one] for one in members), [])
            found = mm(
                thirds(jnp.concatenate(values, axis=0), 1),
                fold(table_part(table_ref, places["forward"]), 0),
            )
            for one in members:
                count = len(state["ready column", one])
                state["column", one] = jnp.concatenate(
                    [
                        jnp.concatenate(
                            [
                                block(found[height * group : height * group + height], part)
                                for part in range(2)
                            ],
                            axis=0,
                        )
                        for group in range(count)
                    ],
                    axis=1,
                )
                found = found[count * height :]

    def ranges(member):
        state["ready range", member] = state["fields", member]
        for members in joint("range", JR, member):
            values = sum((state["fields", one] for one in members), [])
            found = mm(
                thirds(jnp.concatenate(values, axis=0), 1),
                fold(table_part(table_ref, places["band"]), 0),
            )
            for one in members:
                state["range", one], found = found[: 3 * height], found[3 * height :]

    def coherence(member):
        azimuth = table_part(table_ref, places["azimuth"])
        real, imag, power = [
            along_lines(azimuth, state["range", member], index, height) for index in range(3)
        ]
        own = power_ref[min(matching, 1), member]
        coherence_ref[member] = (real * real + imag * imag) / (own * power + EPSILON)
        if finish:
            send(coherence_ref.at[member], coherence_out.at[matching, member])

    def rows(member):
        state["freq", member] = mm(fold(forward_ref[matching], 1), thirds(state["column", member], 0))

    def scaled(member):
        freq = state["freq", member]
        freq_real, freq_imag = freq[:freqs], freq[freqs:]
        power = freq_real * freq_real + freq_imag * freq_imag + EPSILON
        magnitude = lax.rsqrt(lax.rsqrt(power))

        state["magnitude", member] = magnitude
        state["weighted", member] = jnp.concatenate(
            [freq_real * magnitude, freq_imag * magnitude], axis=0
        )

    def means(member):
        magnitude = state["magnitude", member]
        count = magnitude.shape[1] // 128
        sums = [
            jnp.sum(block(magnitude[PATCH * place : PATCH * place + PATCH], group), axis=0, keepdims=True)
            for group in range(count)
            for place in range(patches)
        ]
        high, low = halves(jnp.concatenate(sums, axis=0))
        same = table_part(table_ref, places["same"])
        totals = mm(high, same) + mm(low, same)
        inverse = 1.0 / (totals * (1.0 / (PATCH * PATCH)) + EPSILON)
        line = lax.broadcasted_iota(jnp.int32, (height, 128), 0)
        patch = (line + PATCH - offset_ref[0, matching]) >> 5
        scales = []
        for group in range(count):
            scale = inverse[group * patches][None]
            for place in range(1, patches):
                scale = jnp.where(patch == place, inverse[group * patches + place][None], scale)
            scales.append(scale)
        state["scale", member] = scales

    def backs(member):
        back = mm(inverse_ref[matching], thirds(state["weighted", member], 0))
        state["back", member] = [
            jnp.concatenate(
                [block(back[height * part : height * part + height], group) for part in (1, 0)], axis=1
            )
            for group in range(back.shape[1] // 128)
        ]

    def inverses(member):
        state["ready final", member] = state["back", member]
        for members in joint("final", JI, member):
            values = sum((state["back", one] for one in members), [])
            found = mm(
                thirds(jnp.concatenate(values, axis=0), 1),
                fold(table_part(table_ref, places["forward"]), 0),
            )
            for one in members:
                count = len(state["back", one])
                state["final", one] = [
                    found[height * group : height * group + height] for group in range(count)
                ]
                found = found[count * height :]

    def outputs(member):
        edge = state["final", 0][blocks]
        edge_scale = state["scale", 0][blocks]
        for part in range(2):
            whole = [
                block(group, 1 - part) * scale
                for group, scale in zip(state["final", member][:blocks], state["scale", member])
            ]
            side = block(edge, 1 - part) * edge_scale
            turned = [pltpu.roll(value, 128 - shift, 1) for value in whole]
            turned.append(pltpu.roll(side, (128 - PATCH if member else 128) - shift, 1))
            cells = [
                jnp.where(lane < 128 - shift, turned[index], turned[index + 1])
                for index in range(blocks)
            ]
            filtered_ref[part, member] = jnp.concatenate(cells, axis=1).astype(BF)
        if finish:
            send(filtered_ref.at[:, member], filtered_out.at[:, matching, member])

    stages = dict(
        F=fields, C=columns, R=ranges, A=coherence, Z=rows, S=scaled, M=means, B=backs, I=inverses, O=outputs
    )
    for step in ORDER:
        stages[step[0]](int(step[1]))
    for copy in copies:
        copy.wait()


def in_hbm(value):
    return pltpu.with_memory_space_constraint(value, pltpu.HBM)


def vmem(count):
    return [pl.BlockSpec(memory_space=pltpu.VMEM)] * count


def match_call(shared, matching, remote, previous):
    pairing, offsets, image, rims, table, forward, inverse, power, places = shared
    height, breadth = image.shape[2] // 2, image.shape[3]
    finish = matching == MATCH - 1
    coherence = pltpu.VMEM((2, height, breadth), F32)
    filtered = pltpu.VMEM((2, 2, height, breadth), BF)
    inputs = [pairing, offsets, image, rims, table, forward, inverse, power, *remote]
    specs = [pl.BlockSpec(memory_space=pltpu.SMEM)] * 2 + vmem(6 + len(remote))
    out_shape, out_specs, scratch = (coherence, filtered), vmem(2), []
    if finish:
        inputs += previous
        specs += vmem(len(previous))
        out_shape = (
            jax.ShapeDtypeStruct((MATCH, 2, height, breadth), F32),
            jax.ShapeDtypeStruct((2, MATCH, 2, height, breadth), BF),
        )
        out_specs = [pl.BlockSpec(memory_space=pl.ANY)] * 2
        scratch = [coherence, filtered, pltpu.SemaphoreType.DMA((2 * matching + 4,))]
    return pl.pallas_call(
        functools.partial(match_kernel, matching, places, finish),
        out_shape=out_shape,
        in_specs=specs,
        out_specs=tuple(out_specs),
        scratch_shapes=scratch,
        cost_estimate=pl.CostEstimate(flops=2 * 10**9, bytes_accessed=3 * 10**6, transcendentals=0),
        compiler_params=GRANT,
    )(*inputs)


def xor_swap(value, mask):
    return lax.ppermute(value, "acq", [(i, i ^ mask) for i in range(lax.axis_size("acq"))])


def neighbour_swap(value, turn):
    places, groups = lax.axis_size("rng"), lax.axis_size("acq")
    pairs = []
    for group in range(groups):
        for place in range(places):
            target = (group ^ 1) * places + place
            if place % 3 == turn and place + 1 < places:
                target = group * places + place + 1
            elif place and (place - 1) % 3 == turn:
                target = group * places + place - 1
            pairs.append((group * places + place, target))
    return lax.ppermute(value, ("acq", "rng"), pairs)


def per_device(images, pairing, tile_offsets):
    lines, breadth = images.shape[2:]
    height = lines // 2
    table, places = all_tables(breadth, height)
    row_table, row_places = line_tables(height)
    table, row_table = jnp.asarray(table), jnp.asarray(row_table)
    side = pltpu.VMEM((lines, 128), BF)
    payload = pltpu.VMEM((5, height, breadth), BF)
    offsets = tile_offsets.T
    mains = pltpu.VMEM((4, height, breadth), BF)
    scalars = [pl.BlockSpec(memory_space=pltpu.SMEM)] * 2
    image, first, second, third, far, pairing, offsets = pl.pallas_call(
        pack_kernel,
        out_shape=(
            pltpu.VMEM(images.shape, BF),
            side,
            side,
            side,
            mains,
            pltpu.SMEM(pairing.shape, jnp.int32),
            pltpu.SMEM(offsets.shape, jnp.int32),
        ),
        in_specs=[pl.BlockSpec(memory_space=pl.ANY)] * 3,
        out_specs=(*vmem(5), *scalars),
        scratch_shapes=[pltpu.SemaphoreType.DMA((3,))],
        cost_estimate=pl.CostEstimate(flops=COST, bytes_accessed=10**6, transcendentals=0),
        compiler_params=GRANT,
        name="pack",
    )(in_hbm(images), in_hbm(pairing), in_hbm(offsets))
    first = neighbour_swap(first, 0)
    second = neighbour_swap(second, 1)
    third = neighbour_swap(third, 2)
    far = xor_swap(far, 2)
    freqs = height + PATCH
    near, forward, inverse = pl.pallas_call(
        functools.partial(main_kernel, row_places),
        out_shape=(
            payload,
            pltpu.VMEM((MATCH, 2 * freqs, 4 * height), BF),
            pltpu.VMEM((MATCH, 2 * height, 6 * freqs), BF),
        ),
        in_specs=[*vmem(1), scalars[0], *vmem(1)],
        out_specs=tuple(vmem(3)),
        cost_estimate=pl.CostEstimate(flops=COST, bytes_accessed=10**6, transcendentals=0),
        compiler_params=GRANT,
        name="mains",
    )(image, offsets, row_table)
    near, far_rims, rims = pl.pallas_call(
        functools.partial(rim_kernel, lax.axis_size("rng") - 1),
        out_shape=(
            payload,
            pltpu.VMEM((height, breadth), BF),
            pltpu.VMEM((2, lines, 128), BF),
        ),
        in_specs=vmem(4),
        out_specs=tuple(vmem(3)),
        input_output_aliases={3: 0},
        compiler_params=GRANT,
        name="rims",
    )(first, second, third, near)
    near = xor_swap(near, 1)
    far_rims = xor_swap(far_rims, 2)
    power = pl.pallas_call(
        functools.partial(power_kernel, places),
        out_shape=pltpu.VMEM((2, 2, height, breadth), F32),
        in_specs=vmem(3),
        out_specs=vmem(1)[0],
        cost_estimate=pl.CostEstimate(flops=10**9, bytes_accessed=10**6, transcendentals=0),
        compiler_params=GRANT,
        name="power",
    )(image, rims, table)
    call = functools.partial(
        match_call, (pairing, offsets, image, rims, table, forward, inverse, power, places)
    )
    outputs = call(0, (near,), ())
    far, *outputs = lax.optimization_barrier((far, *outputs))
    both = pl.pallas_call(
        merge_main_kernel,
        out_shape=payload,
        in_specs=vmem(1),
        out_specs=vmem(1)[0],
        compiler_params=GRANT,
        name="merge_mains",
    )(far)
    both = pl.pallas_call(
        merge_rim_kernel,
        out_shape=payload,
        in_specs=vmem(2),
        out_specs=vmem(1)[0],
        input_output_aliases={0: 0},
        compiler_params=GRANT,
        name="merge_rims",
    )(both, far_rims)
    both = xor_swap(both, 1)
    outputs = [*outputs, *call(1, (far, far_rims), ())]
    return tuple(call(2, (both,), outputs))


def solution(mesh):
    in_specs = (P(None, ("stack", "acq"), None, "rng"), P(), P())
    out_specs = (
        P(None, ("stack", "acq"), None, "rng"),
        P(None, None, ("stack", "acq"), None, "rng"),
    )

    return jax.shard_map(
        per_device, mesh=mesh, in_specs=in_specs, out_specs=out_specs, check_vma=False
    )
```
